32 devices in a mesh: sec: 4 (over y, x), ctx: 8 (over z, core).
Axes of the slice: x: 2, y: 2, z: 4, core: 2. Of those that a mesh axis runs over, the one named last changes fastest.
Arguments:
- hidden_state: bfloat16 [4, 1024, 4096], P('sec', 'ctx'), may hold values from -8 to 8
- queries: bfloat16 [4, 1024, 4096], P('sec', 'ctx'), may hold values from -6 to 6
- key_vectors: bfloat16 [4, 1024, 4096], P('sec', 'ctx'), may hold values from -4.5 to 4.5
- value_vectors: bfloat16 [4, 1024, 4096], P('sec', 'ctx'), may hold values from -6 to 6
- modulation: float32 [32, 3, 4096], replicated, may hold values from -3 to 3
- down_weight: bfloat16 [4096, 256], replicated, may hold values from -0.09375 to 0.09375
- conv_weight: bfloat16 [3, 3, 3, 256, 256], replicated, may hold values from -0.078125 to 0.078125
- clip_frames: int32 [4], replicated, may hold values from 4 to 16, as said below
- destination: int32 [4], replicated, may hold values from 0 to 3, as said below
- timestep: int32 [4], replicated, may hold values from 0 to 31
Outputs:
- upsampled: bfloat16 [4, 1024, 256], P('sec', 'ctx')
The draws below stay inside these ranges and needn't reach their ends.
Inputs may be any that keep to these rules, and one draw needn't show every extreme that they name: `clip_frames`: one section's clip fills all 16 frames. `destination`: every upsampler group receives exactly one clip; some group d receives the clip of section (d + 2) mod 4.
All inputs are finite; a program needn't handle non-finite values.
Results may differ from the reference program's by a relative error of at most 0.0063.
Values may be sent and summed in bfloat16 or wider, within the bound.
No kernel may reach another device: no remote copies, remote signals or barrier semaphores. Data moves between devices by JAX's collectives and lax.ppermute only.
A program may use at most 64 MiB of HBM per device.

```python
import math
import jax
import jax.numpy as jnp
from jax import lax

HEADS = 32
HD = 128
D = 4096
C_UP = 256
HH = 8
WW = 8
STEPS = 32
FRAMES = 16
SEQ = 1024
SECS = 4


def attention_pair(key):
    query_key, other_key = jax.random.split(jax.random.fold_in(key, 7), 2)
    query_rows = jnp.clip(jax.random.normal(query_key, (SECS, SEQ, D), jnp.float32), -4.5, 4.5)
    key_rows = jnp.clip(jax.random.normal(other_key, (SECS, SEQ, D), jnp.float32), -4.5, 4.5)
    return (query_rows, key_rows)


def draw_queries(key, part):
    return attention_pair(key)[0].astype(jnp.bfloat16)


def draw_key_vectors(key, part):
    return attention_pair(key)[1].astype(jnp.bfloat16)


def draw_hidden_state(key, part):
    scale_key, row_key, entry_key = jax.random.split(jax.random.fold_in(key, 11), 3)
    column_scale = jnp.exp(jax.random.uniform(scale_key, (D,), jnp.float32, 0.0, math.log(10.0)))
    row_scale = jnp.exp(jax.random.uniform(row_key, (SECS, SEQ, 1), jnp.float32, 0.0, math.log(10.0)))
    entries = jnp.clip(jax.random.normal(entry_key, (SECS, SEQ, D), jnp.float32), -4.0, 4.0)
    result = 0.02 * row_scale * entries * column_scale
    return jnp.clip(result, -8.0, 8.0).astype(jnp.bfloat16)


def draw_clip_frames(key, part):
    first_key, second_key = jax.random.split(jax.random.fold_in(key, 13))
    lengths = jax.random.randint(first_key, (SECS,), max(1, FRAMES // 4), FRAMES + 1)
    longest = jax.random.randint(second_key, (), 0, SECS)
    return jnp.where(jnp.arange(SECS) == longest, FRAMES, lengths).astype(jnp.int32)


def draw_destination(key, part):
    order_key, pick_key = jax.random.split(jax.random.fold_in(key, 17))
    section_ids = jnp.arange(SECS, dtype=jnp.int32)
    order = jax.random.permutation(order_key, section_ids).astype(jnp.int32)
    target = jax.random.randint(pick_key, (), 0, SECS).astype(jnp.int32)
    sender = ((target + SECS // 2) % SECS).astype(jnp.int32)
    holder = jnp.sum(jnp.where(order == target, section_ids, 0)).astype(jnp.int32)
    displaced = jnp.sum(jnp.where(section_ids == sender, order, 0)).astype(jnp.int32)
    order = jnp.where(section_ids == holder, displaced, order)
    order = jnp.where(section_ids == sender, target, order)
    return order.astype(jnp.int32)


def set_ends(values, stream_key, least, largest):
    extent = values.shape
    place = [jax.random.randint(jax.random.fold_in(stream_key, axis), (), 0, extent[axis]) for axis in range(len(extent))]
    values = values.at[tuple(place)].set(least)
    longest = extent.index(max(extent))
    place[longest] = (place[longest] + 1) % extent[longest]
    return values.at[tuple(place)].set(largest)


def block_levels(own_key, dims, cuts, smallest, top_value):
    def one(axis_at, parts):
        draws = jax.random.uniform(jax.random.fold_in(jax.random.fold_in(own_key, 6), axis_at), (parts,), jnp.float32, smallest / len(cuts), top_value / len(cuts))
        return jnp.repeat(jnp.exp(draws), dims[axis_at] // parts).reshape((-1,) + (1,) * (len(dims) - axis_at - 1))

    gain = one(*cuts[0])
    for cut in cuts[1:]:
        gain = gain * one(*cut)
    return gain


def scatter_about(own_key, dims, width, bound, shards=(), kind=jnp.bfloat16):
    array = jax.random.normal(own_key, dims, jnp.float32) * width
    if len(shards) > 0:
        array = block_levels(own_key, dims, shards, -0.22, 0.18) * array
    return jnp.clip(array, min=-bound, max=bound).astype(kind)


def setup_inputs(seed: int = 0) -> dict:
    splits = jax.random.split(jax.random.key(seed), 11)
    hidden_state = draw_hidden_state(jax.random.fold_in(splits[10], 71), 0)
    queries = draw_queries(jax.random.fold_in(splits[10], 71), 0)
    key_vectors = draw_key_vectors(jax.random.fold_in(splits[10], 71), 0)
    value_vectors = scatter_about(splits[3], (SECS, SEQ, D), 1.0, 6.0, ((0, 4), (1, 8)))
    modulation = scatter_about(splits[4], (STEPS, 3, D), 0.5, 3.0, (), jnp.float32)
    down_weight = scatter_about(splits[5], (D, C_UP), D ** -0.5, 0.09375)
    conv_weight = scatter_about(splits[6], (3, 3, 3, C_UP, C_UP), (27 * C_UP) ** -0.5, 0.078125)
    clip_frames = draw_clip_frames(jax.random.fold_in(splits[10], 71), 0)
    destination = draw_destination(jax.random.fold_in(splits[10], 71), 0)
    timestep = set_ends(jax.random.randint(splits[9], (SECS,), 0, STEPS), jax.random.fold_in(splits[9], 1), 0, STEPS - 1).astype(jnp.int32)
    return {"hidden_state": hidden_state, "queries": queries, "key_vectors": key_vectors, "value_vectors": value_vectors, "modulation": modulation, "down_weight": down_weight, "conv_weight": conv_weight, "clip_frames": clip_frames, "destination": destination, "timestep": timestep}


def head_attention(query_head, key_head, value_head, key_valid):
    block_rows = min(512, SEQ)
    score_scale = 1.0 / math.sqrt(HD)
    query_blocks = query_head.reshape(SEQ // block_rows, block_rows, HD)

    def one_block(query_block):
        scores = jnp.dot(query_block, key_head.T, preferred_element_type=jnp.float32) * score_scale
        scores = jnp.where(key_valid[None, :], scores, -jnp.inf)
        weights = jnp.exp(scores - lax.optimization_barrier(jnp.max(scores, axis=1, keepdims=True)))
        row_total = lax.optimization_barrier(jnp.sum(weights, axis=1, keepdims=True))
        rounded = weights.astype(jnp.bfloat16)
        product = jnp.dot(rounded, value_head, preferred_element_type=jnp.float32)
        return (product / row_total).astype(jnp.bfloat16)
    return lax.map(one_block, query_blocks).reshape(SEQ, HD)

def section_block(hidden_rows, query_rows, key_rows, value_rows, mod_rows, frames, down_weight):
    positions = jnp.arange(SEQ, dtype=jnp.int32) // (HH * WW)
    key_valid = positions < frames

    def by_heads(tensor):
        return tensor.reshape(SEQ, HEADS, HD).transpose(1, 0, 2)

    def one_head(head_inputs):
        return head_attention(head_inputs[0], head_inputs[1], head_inputs[2], key_valid)
    attended = lax.map(one_head, (by_heads(query_rows), by_heads(key_rows), by_heads(value_rows)))
    attended = attended.transpose(1, 0, 2).reshape(SEQ, D)
    block_out = (hidden_rows.astype(jnp.float32) + mod_rows[2] * attended.astype(jnp.float32)).astype(jnp.bfloat16)
    wide_values = block_out.astype(jnp.float32)
    centre = lax.optimization_barrier(jnp.mean(wide_values, axis=-1, keepdims=True))
    spread = lax.optimization_barrier(jnp.mean(jnp.square(wide_values - centre), axis=-1, keepdims=True))
    normed = ((wide_values - centre) * lax.rsqrt(spread + 1e-06) * (1.0 + mod_rows[1]) + mod_rows[0]).astype(jnp.bfloat16)
    return jnp.dot(normed, down_weight, preferred_element_type=jnp.float32).astype(jnp.bfloat16)

def reference(hidden_state, queries, key_vectors, value_vectors, modulation, down_weight, conv_weight, clip_frames, destination, timestep):
    projected_list = []
    for section in range(SECS):
        projected_list.append(section_block(hidden_state[section], queries[section], key_vectors[section], value_vectors[section], modulation[timestep[section]], clip_frames[section], down_weight))
    projected = jnp.stack(projected_list)
    source_of = jnp.argsort(destination)
    positions = jnp.arange(SEQ, dtype=jnp.int32) // (HH * WW)
    outputs = []
    for target in range(SECS):
        source = source_of[target]
        keep_token = (positions < clip_frames[source])[:, None]
        clip_cells = jnp.where(keep_token, projected[source], 0).astype(jnp.bfloat16)
        convolved = lax.conv_general_dilated(clip_cells.reshape(1, FRAMES, HH, WW, C_UP), conv_weight, (1, 1, 1), ((1, 1), (1, 1), (1, 1)), dimension_numbers=('NDHWC', 'DHWIO', 'NDHWC'), preferred_element_type=jnp.float32)
        convolved = convolved.reshape(SEQ, C_UP)
        outputs.append(jnp.where(keep_token, clip_cells.astype(jnp.float32) + convolved, 0.0).astype(jnp.bfloat16))
    return jnp.stack(outputs)
```

```python
import functools
import math

import jax
import jax.numpy as jnp
from jax import lax
from jax.experimental import pallas as pl
from jax.experimental.pallas import tpu as pltpu
from jax.sharding import PartitionSpec as P

HEADS = 32
HH = 8
WW = 8


def partner(me, step, count):
    if count & (count - 1) == 0:
        return me ^ step, me ^ step
    return lax.rem(me + step, count), lax.rem(me - step + count, count)


def ring(step, count):
    if count & (count - 1) == 0:
        return [(i, i ^ step) for i in range(count)]
    return [(i, (i + step) % count) for i in range(count)]


def exchange(pieces, axis, count):
    out = [pieces[0]] + [None] * (count - 1)
    for step in range(count - 1, 0, -1):
        out[step] = lax.ppermute(pieces[step], axis, ring(step, count))
    return out


def pack_kernel(count, head_cols, first_col, width, q_ref, k_ref, v_ref, *rest):
    outs, (buf, in_sem, out_sem) = rest[:count], rest[count:]
    me = lax.axis_index("ctx")
    order = list(range(count - 1, -1, -1))

    def load(step, kind):
        col = pl.multiple_of(partner(me, step, count)[0] * head_cols + first_col, 128)
        source = (q_ref, k_ref, v_ref)[kind]
        return pltpu.make_async_copy(
            source.at[0, :, pl.ds(col, width)], buf.at[step, kind], in_sem.at[step, kind]
        )

    def save(step):
        return pltpu.make_async_copy(buf.at[step], outs[step], out_sem.at[step])

    for step in order:
        for kind in range(3):
            load(step, kind).start()
    for step in order:
        for kind in range(3):
            load(step, kind).wait()
        save(step).start()
    for step in order:
        save(step).wait()


def pack(queries, key_vectors, value_vectors, count, head_cols, first_col, width):
    rows = queries.shape[1]
    piece = jax.ShapeDtypeStruct((3, rows, width), queries.dtype)
    moved = 6 * count * rows * width * 2
    return pl.pallas_call(
        functools.partial(pack_kernel, count, head_cols, first_col, width),
        out_shape=[piece] * count,
        in_specs=[pl.BlockSpec(memory_space=pl.ANY)] * 3,
        out_specs=[pl.BlockSpec(memory_space=pl.ANY)] * count,
        scratch_shapes=[
            pltpu.VMEM((count, 3, rows, width), queries.dtype),
            pltpu.SemaphoreType.DMA((count, 3)),
            pltpu.SemaphoreType.DMA((count,)),
        ],
        cost_estimate=pl.CostEstimate(flops=0, bytes_accessed=moved, transcendentals=0),
        name="pack",
    )(queries, key_vectors, value_vectors)


def attend_kernel(count, heads, block_rows, frames_ref, *rest):
    pieces, outs = rest[:count], rest[count : 2 * count]
    data, result, in_sem, out_sem = rest[2 * count :]
    me = lax.axis_index("ctx")
    rows = pieces[0].shape[1]
    seq = count * rows
    size = pieces[0].shape[2] // heads
    scale = 1.0 / math.sqrt(size)

    def load(step):
        place = pl.multiple_of(partner(me, step, count)[1] * rows, rows)
        return pltpu.make_async_copy(
            pieces[step], data.at[:, pl.ds(place, rows), :], in_sem.at[step]
        )

    def save(step):
        place = pl.multiple_of(partner(me, step, count)[1] * rows, rows)
        return pltpu.make_async_copy(
            result.at[pl.ds(place, rows), :], outs[step], out_sem.at[step]
        )

    for step in range(count):
        load(step).start()
    for step in range(count):
        load(step).wait()
    valid = frames_ref[0] * (HH * WW)
    places = lax.broadcasted_iota(jnp.int32, (1, seq), 1)
    bias = jnp.where(places < valid, 0.0, -jnp.inf)
    blocks = seq // block_rows

    def block(index, carry):
        start = pl.multiple_of(index * block_rows, block_rows)
        here = pl.ds(start, block_rows)
        for head in range(heads):
            lanes = pl.ds(head * size, size)
            scores = lax.dot_general(
                data[0, here, lanes],
                data[1, :, lanes],
                (((1,), (1,)), ((), ())),
                preferred_element_type=jnp.float32,
            )
            scores = scores * scale + bias
            weights = jnp.exp(scores - jnp.max(scores, axis=1, keepdims=True))
            total = jnp.sum(weights, axis=1, keepdims=True)
            product = jnp.dot(
                weights.astype(jnp.bfloat16),
                data[2, :, lanes],
                preferred_element_type=jnp.float32,
            )
            result[here, lanes] = (product / total).astype(result.dtype)
        return carry

    lax.fori_loop(0, blocks, block, 0)
    for step in range(count):
        save(step).start()
    for step in range(count):
        save(step).wait()


def attend(frames, pieces, count, heads):
    _, rows, width = pieces[0].shape
    seq = count * rows
    block_rows = min(256, seq)
    size = width // heads
    return pl.pallas_call(
        functools.partial(attend_kernel, count, heads, block_rows),
        out_shape=[jax.ShapeDtypeStruct((rows, width), jnp.bfloat16)] * count,
        in_specs=[pl.BlockSpec(memory_space=pltpu.SMEM)]
        + [pl.BlockSpec(memory_space=pl.ANY)] * count,
        out_specs=[pl.BlockSpec(memory_space=pl.ANY)] * count,
        scratch_shapes=[
            pltpu.VMEM((3, seq, width), jnp.bfloat16),
            pltpu.VMEM((seq, width), jnp.bfloat16),
            pltpu.SemaphoreType.DMA((count,)),
            pltpu.SemaphoreType.DMA((count,)),
        ],
        cost_estimate=pl.CostEstimate(
            flops=4 * seq * seq * width,
            bytes_accessed=8 * seq * width,
            transcendentals=seq * seq * heads,
        ),
        name="attend",
    )(frames, *pieces)


def project_kernel(count, chunks, step_ref, h_ref, mod_ref, weight_ref, *rest):
    pieces, (out_ref, attended, mod_rows, in_sem, mod_sem) = rest[: chunks * count], rest[chunks * count :]
    me = lax.axis_index("ctx")
    width = pieces[0].shape[1]

    def load(chunk, step):
        owner = partner(me, step, count)[1]
        col = pl.multiple_of(owner * (chunks * width) + chunk * width, 128)
        return pltpu.make_async_copy(
            pieces[chunk * count + step],
            attended.at[:, pl.ds(col, width)],
            in_sem.at[chunk, step],
        )

    mod_copy = pltpu.make_async_copy(mod_ref.at[step_ref[0]], mod_rows, mod_sem)
    mod_copy.start()
    for chunk in range(chunks):
        for step in range(count):
            load(chunk, step).start()
    mod_copy.wait()
    for chunk in range(chunks):
        for step in range(count):
            load(chunk, step).wait()
    mod = mod_rows[...]
    block = (
        h_ref[0].astype(jnp.float32) + mod[2:3] * attended[...].astype(jnp.float32)
    ).astype(jnp.bfloat16)
    wide = block.astype(jnp.float32)
    centre = jnp.mean(wide, axis=-1, keepdims=True)
    spread = jnp.mean(jnp.square(wide - centre), axis=-1, keepdims=True)
    normed = (
        (wide - centre) * lax.rsqrt(spread + 1e-06) * (1.0 + mod[1:2]) + mod[0:1]
    ).astype(jnp.bfloat16)
    out_ref[...] = jnp.dot(normed, weight_ref[...], preferred_element_type=jnp.float32).astype(
        out_ref.dtype
    )


def project(step, hidden_state, modulation, down_weight, pieces, count, chunks):
    _, rows, model = hidden_state.shape
    channels = down_weight.shape[1]
    return pl.pallas_call(
        functools.partial(project_kernel, count, chunks),
        out_shape=jax.ShapeDtypeStruct((rows, channels), jnp.bfloat16),
        in_specs=[
            pl.BlockSpec(memory_space=pltpu.SMEM),
            pl.BlockSpec(memory_space=pltpu.VMEM),
            pl.BlockSpec(memory_space=pl.ANY),
            pl.BlockSpec(memory_space=pltpu.VMEM),
        ]
        + [pl.BlockSpec(memory_space=pl.ANY)] * (count * chunks),
        out_specs=pl.BlockSpec(memory_space=pltpu.VMEM),
        scratch_shapes=[
            pltpu.VMEM((rows, model), jnp.bfloat16),
            pltpu.VMEM((3, model), jnp.float32),
            pltpu.SemaphoreType.DMA((chunks, count)),
            pltpu.SemaphoreType.DMA,
        ],
        cost_estimate=pl.CostEstimate(
            flops=2 * rows * model * channels,
            bytes_accessed=4 * rows * model + 2 * model * channels,
            transcendentals=0,
        ),
        name="project",
    )(step, hidden_state, modulation, down_weight, *pieces)


def body(
    hidden_state,
    queries,
    key_vectors,
    value_vectors,
    modulation,
    down_weight,
    conv_weight,
    clip_frames,
    destination,
    timestep,
):
    my_section = lax.axis_index("sec")
    my_place = lax.axis_index("ctx")
    sec_count = lax.axis_size("sec")
    count = lax.axis_size("ctx")
    sections, tok_rows, model_width = hidden_state.shape
    head_size = model_width // HEADS
    local_heads = HEADS // count
    chunks = 2 if local_heads % 2 == 0 else 1
    heads = local_heads // chunks
    width = heads * head_size
    own_frames = lax.dynamic_slice(clip_frames, (my_section,), (1,))
    my_step = lax.dynamic_slice(timestep, (my_section,), (1,))

    returned = []
    received = []
    for chunk in range(chunks):
        sent = pack(
            queries, key_vectors, value_vectors, count, local_heads * head_size, chunk * width, width
        )
        received.append(exchange(sent, "ctx", count))
    for chunk in range(chunks):
        outs = attend(own_frames, received[chunk], count, heads)
        returned += exchange(outs, "ctx", count)
    own_projected = project(
        my_step, hidden_state, modulation, down_weight, returned, count, chunks
    )

    section_ids = jnp.arange(destination.shape[0], dtype=jnp.int32)
    source = jnp.sum(jnp.where(destination == my_section, section_ids, 0))
    everyone = exchange([own_projected] * sec_count, "sec", sec_count)
    projected = everyone[0]
    for step in range(1, sec_count):
        projected = jnp.where(
            source == partner(my_section, step, sec_count)[1], everyone[step], projected
        )
    frames_here = tok_rows // (HH * WW)
    frame_number = my_place * frames_here + jnp.arange(frames_here, dtype=jnp.int32)
    keep_frame = (frame_number < clip_frames[source])[None, :, None, None, None]
    clip_cells = jnp.where(keep_frame, projected.reshape(1, frames_here, HH, WW, -1), 0)
    forward = [(i, i + 1) for i in range(count - 1)]
    backward = [(i + 1, i) for i in range(count - 1)]
    low = lax.ppermute(clip_cells[:, -1:], "ctx", forward)
    high = lax.ppermute(clip_cells[:, :1], "ctx", backward)
    padded = jnp.concatenate([low, clip_cells, high], axis=1)
    convolved = lax.conv_general_dilated(
        padded,
        conv_weight,
        (1, 1, 1),
        ((0, 0), (1, 1), (1, 1)),
        dimension_numbers=("NDHWC", "DHWIO", "NDHWC"),
        preferred_element_type=jnp.float32,
    )
    upsampled = jnp.where(keep_frame, clip_cells.astype(jnp.float32) + convolved, 0.0).astype(
        jnp.bfloat16
    )
    return upsampled.reshape(sections, tok_rows, -1)


def solution(mesh):
    split = P("sec", "ctx", None)
    return jax.shard_map(
        body,
        mesh=mesh,
        in_specs=(split,) * 4 + (P(),) * 6,
        out_specs=split,
        check_vma=False,
    )
```

```python
import functools
import itertools
import math

import jax
import jax.numpy as jnp
from jax import lax
from jax.experimental import pallas as pl
from jax.experimental.pallas import tpu as pltpu
from jax.sharding import PartitionSpec as P

HEADS = 32
HH = 8
WW = 8


def partner(me, step, count):
    if count & (count - 1) == 0:
        return me ^ step, me ^ step
    return lax.rem(me + step, count), lax.rem(me - step + count, count)


def ring(step, count):
    if count & (count - 1) == 0:
        return [(i, i ^ step) for i in range(count)]
    return [(i, (i + step) % count) for i in range(count)]


def exchange(pieces, axis, count):
    out = [pieces[0]] + [None] * (count - 1)
    for step in range(count - 1, 0, -1):
        out[step] = lax.ppermute(pieces[step], axis, ring(step, count))
    return out


def pack_kernel(count, kinds, width, *rest):
    sources, outs, (buf, in_sem, out_sem) = rest[:kinds], rest[kinds : kinds + count], rest[kinds + count :]
    me = lax.axis_index("ctx")
    order = list(range(count - 1, -1, -1))

    def load(step, kind):
        col = pl.multiple_of(partner(me, step, count)[0] * width, 128)
        return pltpu.make_async_copy(
            sources[kind].at[0, :, pl.ds(col, width)], buf.at[step, kind], in_sem.at[step, kind]
        )

    def save(step):
        return pltpu.make_async_copy(buf.at[step], outs[step], out_sem.at[step])

    for step in order:
        for kind in range(kinds):
            load(step, kind).start()
    for step in order:
        for kind in range(kinds):
            load(step, kind).wait()
        save(step).start()
    for step in order:
        save(step).wait()


def pack(sources, count, width):
    rows = sources[0].shape[1]
    kinds = len(sources)
    piece = jax.ShapeDtypeStruct((kinds, rows, width), sources[0].dtype)
    return pl.pallas_call(
        functools.partial(pack_kernel, count, kinds, width),
        out_shape=[piece] * count,
        in_specs=[pl.BlockSpec(memory_space=pl.ANY)] * kinds,
        out_specs=[pl.BlockSpec(memory_space=pl.ANY)] * count,
        scratch_shapes=[
            pltpu.VMEM((count, kinds, rows, width), sources[0].dtype),
            pltpu.SemaphoreType.DMA((count, kinds)),
            pltpu.SemaphoreType.DMA((count,)),
        ],
        cost_estimate=pl.CostEstimate(
            flops=0, bytes_accessed=4 * kinds * count * rows * width, transcendentals=0
        ),
        name="pack",
    )(*sources)


def score_kernel(count, heads, frames_ref, *rest):
    pieces, (out_ref, data, bias, in_sem) = rest[:count], rest[count:]
    me = lax.axis_index("ctx")
    rows = pieces[0].shape[1]
    seq = count * rows
    size = data.shape[2] // heads
    block_rows = out_ref.shape[1]
    head, index = pl.program_id(0), pl.program_id(1)
    scale = 1.0 / math.sqrt(size)

    def load(step):
        place = pl.multiple_of(partner(me, step, count)[1] * rows, rows)
        return pltpu.make_async_copy(
            pieces[step], data.at[:, pl.ds(place, rows), :], in_sem.at[step]
        )

    @pl.when((head == 0) & (index == 0))
    def _():
        for step in range(count):
            load(step).start()
        valid = frames_ref[0] * (HH * WW)
        places = lax.broadcasted_iota(jnp.int32, (1, seq), 1)
        bias[...] = jnp.where(places < valid, 0.0, -jnp.inf)
        for step in range(count):
            load(step).wait()

    start = pl.multiple_of(index * block_rows, block_rows)
    lanes = pl.ds(pl.multiple_of(head * size, size), size)
    scores = lax.dot_general(
        data[0, pl.ds(start, block_rows), lanes],
        data[1, :, lanes],
        (((1,), (1,)), ((), ())),
        preferred_element_type=jnp.float32,
    )
    scores = scores * scale + bias[...]
    out_ref[0] = jnp.exp(scores - jnp.max(scores, axis=1, keepdims=True)).astype(out_ref.dtype)


def score(frames, pieces, count, heads):
    _, rows, width = pieces[0].shape
    seq = count * rows
    block_rows = min(256, seq)
    return pl.pallas_call(
        functools.partial(score_kernel, count, heads),
        grid=(heads, seq // block_rows),
        out_shape=jax.ShapeDtypeStruct((heads, seq, seq), jnp.bfloat16),
        in_specs=[pl.BlockSpec(memory_space=pltpu.SMEM)]
        + [pl.BlockSpec(memory_space=pl.ANY)] * count,
        out_specs=pl.BlockSpec((1, block_rows, seq), lambda head, index: (head, index, 0)),
        scratch_shapes=[
            pltpu.VMEM((2, seq, width), jnp.bfloat16),
            pltpu.VMEM((1, seq), jnp.float32),
            pltpu.SemaphoreType.DMA((count,)),
        ],
        cost_estimate=pl.CostEstimate(
            flops=2 * seq * seq * width,
            bytes_accessed=4 * seq * width + 2 * heads * seq * seq,
            transcendentals=seq * seq * heads,
        ),
        name="score",
    )(frames, *pieces)


def mix_kernel(count, heads, weights_ref, *rest):
    pieces, outs = rest[:count], rest[count : 2 * count]
    slots, values, result, w_sem, in_sem, out_sem = rest[2 * count :]
    me = lax.axis_index("ctx")
    rows, width = pieces[0].shape[1:]
    seq = count * rows
    size = width // heads

    block_rows = slots.shape[1]
    tasks = [(head, index) for head in range(heads) for index in range(seq // block_rows)]

    def fetch(task):
        head, index = tasks[task]
        return pltpu.make_async_copy(
            weights_ref.at[head, pl.ds(index * block_rows, block_rows), :],
            slots.at[task % 2],
            w_sem.at[task % 2],
        )

    def load(step, head):
        place = pl.multiple_of(partner(me, step, count)[1] * rows, rows)
        return pltpu.make_async_copy(
            pieces[step].at[0, :, pl.ds(head * size, size)],
            values.at[pl.ds(place, rows), pl.ds(head * 2 * size, size)],
            in_sem.at[head, step],
        )

    def save(step):
        place = pl.multiple_of(partner(me, step, count)[1] * rows, rows)
        return pltpu.make_async_copy(
            result.at[pl.ds(place, rows), :], outs[step], out_sem.at[step]
        )

    for head in range(heads):
        for step in range(count):
            load(step, head).start()
    fetch(0).start()
    for head in range(heads):
        values[:, pl.ds((head * 2 + 1) * size, size)] = jnp.ones((seq, size), jnp.bfloat16)
    for task, (head, index) in enumerate(tasks):
        if task + 1 < len(tasks):
            fetch(task + 1).start()
        if index == 0:
            for step in range(count):
                load(step, head).wait()
        fetch(task).wait()
        both = jnp.dot(
            slots[task % 2],
            values[:, pl.ds(head * 2 * size, 2 * size)],
            preferred_element_type=jnp.float32,
        )
        result[pl.ds(index * block_rows, block_rows), pl.ds(head * size, size)] = (
            both[:, :size] / both[:, size:]
        ).astype(result.dtype)
    for step in range(count):
        save(step).start()
    for step in range(count):
        save(step).wait()


def mix(weights, pieces, count, heads):
    _, rows, width = pieces[0].shape
    seq = count * rows
    return pl.pallas_call(
        functools.partial(mix_kernel, count, heads),
        out_shape=[jax.ShapeDtypeStruct((rows, width), jnp.bfloat16)] * count,
        in_specs=[pl.BlockSpec(memory_space=pl.ANY)] * (count + 1),
        out_specs=[pl.BlockSpec(memory_space=pl.ANY)] * count,
        scratch_shapes=[
            pltpu.VMEM((2, min(1024, seq), seq), jnp.bfloat16),
            pltpu.VMEM((seq, 2 * width), jnp.bfloat16),
            pltpu.VMEM((seq, width), jnp.bfloat16),
            pltpu.SemaphoreType.DMA((2,)),
            pltpu.SemaphoreType.DMA((heads, count)),
            pltpu.SemaphoreType.DMA((count,)),
        ],
        cost_estimate=pl.CostEstimate(
            flops=4 * seq * seq * width,
            bytes_accessed=4 * seq * width + 2 * heads * seq * seq,
            transcendentals=0,
        ),
        name="mix",
    )(weights, *pieces)


def project_kernel(count, step_ref, frames_ref, h_ref, mod_ref, weight_ref, *rest):
    pieces, rest = rest[:count], rest[count:]
    out_ref, attended, hidden, weight, mod_rows, in_sem, mod_sem, h_sem, weight_sem = rest
    me = lax.axis_index("ctx")
    rows, width = pieces[0].shape
    block_rows = 16

    def load(step):
        owner = partner(me, step, count)[1]
        col = pl.multiple_of(owner * width, 128)
        return pltpu.make_async_copy(
            pieces[step], attended.at[:, pl.ds(col, width)], in_sem.at[step]
        )

    mod_copy = pltpu.make_async_copy(mod_ref.at[step_ref[0]], mod_rows, mod_sem)
    h_copy = pltpu.make_async_copy(h_ref.at[0], hidden, h_sem)
    weight_copy = pltpu.make_async_copy(weight_ref, weight, weight_sem)
    mod_copy.start()
    h_copy.start()
    for step in range(count):
        load(step).start()
    weight_copy.start()
    mod_copy.wait()
    h_copy.wait()
    for step in range(count):
        load(step).wait()

    def rows_of(index, carry):
        here = pl.ds(pl.multiple_of(index * block_rows, block_rows), block_rows)
        block = (
            hidden[here, :].astype(jnp.float32)
            + mod_rows[2:3, :] * attended[here, :].astype(jnp.float32)
        ).astype(jnp.bfloat16)
        wide = block.astype(jnp.float32)
        centre = jnp.mean(wide, axis=-1, keepdims=True)
        spread = jnp.mean(jnp.square(wide - centre), axis=-1, keepdims=True)
        normed = (wide - centre) * lax.rsqrt(spread + 1e-06) * (
            1.0 + mod_rows[1:2, :]
        ) + mod_rows[0:1, :]
        attended[here, :] = normed.astype(jnp.bfloat16)
        return carry

    lax.fori_loop(0, rows // block_rows, rows_of, 0)
    weight_copy.wait()
    projected = jnp.dot(attended[...], weight[...], preferred_element_type=jnp.float32)
    token = me * rows + lax.broadcasted_iota(jnp.int32, (rows, 1), 0)
    out_ref[...] = jnp.where(token < frames_ref[0] * (HH * WW), projected, 0.0).astype(
        out_ref.dtype
    )


def project(step, frames, hidden_state, modulation, down_weight, pieces, count):
    _, rows, model = hidden_state.shape
    channels = down_weight.shape[1]
    return pl.pallas_call(
        functools.partial(project_kernel, count),
        out_shape=jax.ShapeDtypeStruct((rows, channels), jnp.bfloat16),
        in_specs=[pl.BlockSpec(memory_space=pltpu.SMEM)] * 2
        + [pl.BlockSpec(memory_space=pl.ANY)] * (count + 3),
        out_specs=pl.BlockSpec(memory_space=pltpu.VMEM),
        scratch_shapes=[
            pltpu.VMEM((rows, model), jnp.bfloat16),
            pltpu.VMEM((rows, model), jnp.bfloat16),
            pltpu.VMEM((model, channels), jnp.bfloat16),
            pltpu.VMEM((3, model), jnp.float32),
            pltpu.SemaphoreType.DMA((count,)),
            pltpu.SemaphoreType.DMA,
            pltpu.SemaphoreType.DMA,
            pltpu.SemaphoreType.DMA,
        ],
        cost_estimate=pl.CostEstimate(
            flops=2 * rows * model * channels,
            bytes_accessed=4 * rows * model + 2 * model * channels,
            transcendentals=0,
        ),
        name="project",
    )(step, frames, hidden_state, modulation, down_weight, *pieces)


def refine_kernel(frames_ref, low_ref, mid_ref, high_ref, weight_ref, out_ref, weight, sem):
    cells = HH * WW
    rows, channels = mid_ref.shape
    frames_here = rows // cells
    copy = pltpu.make_async_copy(weight_ref, weight, sem)
    copy.start()
    held = [low_ref[...]] + [
        mid_ref[pl.ds(frame * cells, cells), :] for frame in range(frames_here)
    ] + [high_ref[...]]
    column = lax.broadcasted_iota(jnp.int32, (cells, 1), 0) % WW
    blank = jnp.zeros((WW, channels), jnp.float32)
    shifted = []
    for offset in (-1, 0, 1):
        frames = []
        for frame in held:
            cell = frame.astype(jnp.float32)
            if offset:
                cell = pltpu.roll(cell, (-offset) % cells, 0)
                inside = (column + offset >= 0) & (column + offset < WW)
                cell = jnp.where(inside, cell, 0.0)
            frames.append(jnp.concatenate([blank, cell, blank], axis=0))
        shifted.append(frames)
    total = mid_ref[...].astype(jnp.float32)
    copy.wait()
    for down in range(3):
        for across in range(3):
            picked = jnp.concatenate(
                [f[down * WW : down * WW + cells] for f in shifted[across]], axis=0
            ).astype(jnp.bfloat16)
            for ahead in range(3):
                total += jnp.dot(
                    picked[ahead * cells : ahead * cells + rows],
                    weight[(ahead * 3 + down) * 3 + across],
                    preferred_element_type=jnp.float32,
                )
    token = lax.axis_index("ctx") * rows + lax.broadcasted_iota(jnp.int32, (rows, 1), 0)
    out_ref[0] = jnp.where(token < frames_ref[0] * cells, total, 0.0).astype(out_ref.dtype)


def refine(frames, low, mid, high, conv_weight):
    rows, channels = mid.shape
    taps = conv_weight.reshape(-1, channels, channels)
    return pl.pallas_call(
        refine_kernel,
        out_shape=jax.ShapeDtypeStruct((1, rows, channels), jnp.bfloat16),
        in_specs=[pl.BlockSpec(memory_space=pltpu.SMEM)]
        + [pl.BlockSpec(memory_space=pltpu.VMEM)] * 3
        + [pl.BlockSpec(memory_space=pl.ANY)],
        out_specs=pl.BlockSpec(memory_space=pltpu.VMEM),
        scratch_shapes=[
            pltpu.VMEM(taps.shape, taps.dtype),
            pltpu.SemaphoreType.DMA,
        ],
        cost_estimate=pl.CostEstimate(
            flops=54 * rows * channels * channels,
            bytes_accessed=2 * taps.size + 6 * rows * channels,
            transcendentals=0,
        ),
        name="refine",
    )(frames, low, mid, high, taps)


def handoff(projected, destination, source, sec_count, count):
    cells = HH * WW
    axes = ("sec", "ctx")
    if sec_count <= 4:
        orders = [
            order
            for order in itertools.permutations(range(sec_count))
            if any(order[(d + sec_count // 2) % sec_count] == d for d in range(sec_count))
        ]

        def take(order):
            def moved(value, shift):
                pairs = [
                    (sec * count + place, order[sec] * count + place + shift)
                    for sec in range(sec_count)
                    for place in range(count)
                    if 0 <= place + shift < count
                ]
                return lax.ppermute(value, axes, pairs)

            def branch(value):
                return moved(value[-cells:], 1), moved(value, 0), moved(value[:cells], -1)

            return branch

        codes = jnp.asarray(
            [sum(d * sec_count**i for i, d in enumerate(order)) for order in orders], jnp.int32
        )
        code = jnp.sum(destination * jnp.asarray([sec_count**i for i in range(sec_count)], jnp.int32))
        which = jnp.sum(jnp.where(codes == code, jnp.arange(len(orders), dtype=jnp.int32), 0))
        return lax.switch(which, [take(order) for order in orders], projected)
    my_section = lax.axis_index("sec")
    low = lax.ppermute(projected[-cells:], "ctx", [(i, i + 1) for i in range(count - 1)])
    high = lax.ppermute(projected[:cells], "ctx", [(i + 1, i) for i in range(count - 1)])
    whole = jnp.concatenate([low, projected, high], axis=0)
    everyone = exchange([whole] * sec_count, "sec", sec_count)
    chosen = everyone[0]
    for step in range(1, sec_count):
        chosen = jnp.where(
            source == partner(my_section, step, sec_count)[1], everyone[step], chosen
        )
    return chosen[:cells], chosen[cells:-cells], chosen[-cells:]


def body(
    hidden_state,
    queries,
    key_vectors,
    value_vectors,
    modulation,
    down_weight,
    conv_weight,
    clip_frames,
    destination,
    timestep,
):
    my_section = lax.axis_index("sec")
    sec_count = lax.axis_size("sec")
    count = lax.axis_size("ctx")
    model_width = hidden_state.shape[2]
    heads = HEADS // count
    width = model_width // count
    section_ids = jnp.arange(destination.shape[0], dtype=jnp.int32)
    source = jnp.sum(jnp.where(destination == my_section, section_ids, 0))
    own_frames = lax.dynamic_slice(clip_frames, (my_section,), (1,))
    clip_length = lax.dynamic_slice(clip_frames, (source,), (1,))
    my_step = lax.dynamic_slice(timestep, (my_section,), (1,))

    asked = exchange(pack((queries, key_vectors), count, width), "ctx", count)
    values = exchange(pack((value_vectors,), count, width), "ctx", count)
    weights = score(own_frames, asked, count, heads)
    returned = exchange(mix(weights, values, count, heads), "ctx", count)
    projected = project(
        my_step, own_frames, hidden_state, modulation, down_weight, returned, count
    )
    low, mid, high = handoff(projected, destination, source, sec_count, count)
    return refine(clip_length, low, mid, high, conv_weight)


def solution(mesh):
    split = P("sec", "ctx", None)
    return jax.shard_map(
        body,
        mesh=mesh,
        in_specs=(split,) * 4 + (P(),) * 6,
        out_specs=split,
        check_vma=False,
    )
```

```python
import functools
import itertools
import math

import jax
import jax.numpy as jnp
from jax import lax
from jax.experimental import pallas as pl
from jax.experimental.pallas import tpu as pltpu
from jax.sharding import PartitionSpec as P


HEADS = 32
HH = 8
WW = 8


def head_chunks(count):
    local_heads = HEADS // count
    return (local_heads - 1, 1) if local_heads > 1 else (1,)


def partner(me, step, count):
    if count & (count - 1) == 0:
        return me ^ step, me ^ step
    return lax.rem(me + step, count), lax.rem(me - step + count, count)


def ring(step, count):
    if count & (count - 1) == 0:
        return [(i, i ^ step) for i in range(count)]
    return [(i, (i + step) % count) for i in range(count)]


def exchange(pieces, axis, count):
    out = [pieces[0]] + [None] * (count - 1)
    for step in range(1, count):
        out[step] = lax.ppermute(pieces[step], axis, ring(step, count))
    return out


def pack_kernel(count, kinds, head_cols, first_col, width, *rest):
    sources, outs, (buf, in_sem, out_sem) = rest[:kinds], rest[kinds : kinds + count], rest[kinds + count :]
    me = lax.axis_index("ctx")
    order = list(range(count - 1, -1, -1))

    def load(step, kind):
        col = pl.multiple_of(partner(me, step, count)[0] * head_cols + first_col, 128)
        return pltpu.make_async_copy(
            sources[kind].at[0, :, pl.ds(col, width)], buf.at[step, kind], in_sem.at[step, kind]
        )

    def save(step):
        return pltpu.make_async_copy(buf.at[step], outs[step], out_sem.at[step])

    for step in order:
        for kind in range(kinds):
            load(step, kind).start()
    for step in order:
        for kind in range(kinds):
            load(step, kind).wait()
        save(step).start()
    for step in order:
        save(step).wait()


def pack(sources, count, head_cols, first_col, width):
    rows = sources[0].shape[1]
    kinds = len(sources)
    piece = jax.ShapeDtypeStruct((kinds, rows, width), sources[0].dtype)
    return pl.pallas_call(
        functools.partial(pack_kernel, count, kinds, head_cols, first_col, width),
        out_shape=[piece] * count,
        in_specs=[pl.BlockSpec(memory_space=pltpu.HBM)] * kinds,
        out_specs=[pl.BlockSpec(memory_space=pltpu.HBM)] * count,
        scratch_shapes=[
            pltpu.VMEM((count, kinds, rows, width), sources[0].dtype),
            pltpu.SemaphoreType.DMA((count, kinds)),
            pltpu.SemaphoreType.DMA((count,)),
        ],
        cost_estimate=pl.CostEstimate(
            flops=0, bytes_accessed=4 * kinds * count * rows * width, transcendentals=0
        ),
        name="pack",
    )(*sources)


def attend_kernel(count, heads, block_rows, frames_ref, *rest):
    pieces, outs = rest[:count], rest[count : 2 * count]
    data, values, result, in_sem, value_sem, out_sem = rest[2 * count :]
    me = lax.axis_index("ctx")
    rows = pieces[0].shape[1]
    seq = count * rows
    size = pieces[0].shape[2] // heads
    scale = math.log2(math.e) / math.sqrt(size)

    def place(step):
        return pl.ds(pl.multiple_of(partner(me, step, count)[1] * rows, rows), rows)

    def load(step):
        return pltpu.make_async_copy(
            pieces[step].at[pl.ds(0, 2)], data.at[:, place(step), :], in_sem.at[step]
        )

    def load_values(step, head):
        return pltpu.make_async_copy(
            pieces[step].at[2, :, pl.ds(head * size, size)],
            values.at[place(step), pl.ds(head * 2 * size, size)],
            value_sem.at[head, step],
        )

    def save(step):
        return pltpu.make_async_copy(result.at[place(step), :], outs[step], out_sem.at[step])

    for step in range(count):
        load(step).start()
    for head in range(heads):
        for step in range(count):
            load_values(step, head).start()
    for head in range(heads):
        values[:, pl.ds((head * 2 + 1) * size, size)] = jnp.ones((seq, size), jnp.bfloat16)
    for step in range(count):
        load(step).wait()
    for head in range(heads):
        for step in range(count):
            load_values(step, head).wait()
    valid = frames_ref[0] * (HH * WW)
    places = lax.broadcasted_iota(jnp.int32, (1, seq), 1)
    bias = jnp.where(places < valid, 0.0, -jnp.inf)

    def block(index, carry):
        start = pl.multiple_of(index * block_rows, block_rows)
        here = pl.ds(start, block_rows)
        for head in range(heads):
            lanes = pl.ds(head * size, size)
            scores = lax.dot_general(
                data[0, here, lanes],
                data[1, :, lanes],
                (((1,), (1,)), ((), ())),
                preferred_element_type=jnp.float32,
            )
            scores = scores * scale + bias
            weights = jnp.exp2(scores - jnp.max(scores, axis=1, keepdims=True))
            both = jnp.dot(
                weights.astype(jnp.bfloat16),
                values[:, pl.ds(head * 2 * size, 2 * size)],
                preferred_element_type=jnp.float32,
            )
            result[here, lanes] = (both[:, :size] / both[:, size:]).astype(result.dtype)
        return carry

    lax.fori_loop(0, seq // block_rows, block, 0)
    for step in range(count):
        save(step).start()
    for step in range(count):
        save(step).wait()


def attend(frames, pieces, count, heads):
    _, rows, width = pieces[0].shape
    seq = count * rows
    block_rows = min(256, seq)
    return pl.pallas_call(
        functools.partial(attend_kernel, count, heads, block_rows),
        out_shape=[jax.ShapeDtypeStruct((rows, width), jnp.bfloat16)] * count,
        in_specs=[pl.BlockSpec(memory_space=pltpu.SMEM)]
        + [pl.BlockSpec(memory_space=pltpu.HBM)] * count,
        out_specs=[pl.BlockSpec(memory_space=pltpu.HBM)] * count,
        scratch_shapes=[
            pltpu.VMEM((2, seq, width), jnp.bfloat16),
            pltpu.VMEM((seq, 2 * width), jnp.bfloat16),
            pltpu.VMEM((seq, width), jnp.bfloat16),
            pltpu.SemaphoreType.DMA((count,)),
            pltpu.SemaphoreType.DMA((heads, count)),
            pltpu.SemaphoreType.DMA((count,)),
        ],
        cost_estimate=pl.CostEstimate(
            flops=6 * seq * seq * width,
            bytes_accessed=8 * seq * width,
            transcendentals=seq * seq * heads,
        ),
        name="attend",
    )(frames, *pieces)


def project_kernel(count, frames_ref, h_ref, mod_ref, weight_ref, *rest):
    pieces, rest = rest[:count], rest[count:]
    out_ref, attended, hidden, weight, mod_rows, in_sem, mod_sem, h_sem, weight_sem = rest
    me = lax.axis_index("ctx")
    rows, width = pieces[0].shape
    block_rows = 16

    def load(step):
        owner = partner(me, step, count)[1]
        col = pl.multiple_of(owner * width, 128)
        return pltpu.make_async_copy(
            pieces[step], attended.at[:, pl.ds(col, width)], in_sem.at[step]
        )

    mod_copy = pltpu.make_async_copy(mod_ref, mod_rows, mod_sem)
    h_copy = pltpu.make_async_copy(h_ref.at[0], hidden, h_sem)
    weight_copy = pltpu.make_async_copy(weight_ref, weight, weight_sem)
    mod_copy.start()
    h_copy.start()
    for step in range(count):
        load(step).start()
    weight_copy.start()
    mod_copy.wait()
    h_copy.wait()
    for step in range(count):
        load(step).wait()

    def rows_of(index, carry):
        here = pl.ds(pl.multiple_of(index * block_rows, block_rows), block_rows)
        block = (
            hidden[here, :].astype(jnp.float32)
            + mod_rows[2:3, :] * attended[here, :].astype(jnp.float32)
        ).astype(jnp.bfloat16)
        wide = block.astype(jnp.float32)
        centre = jnp.mean(wide, axis=-1, keepdims=True)
        spread = jnp.mean(jnp.square(wide - centre), axis=-1, keepdims=True)
        normed = (wide - centre) * lax.rsqrt(spread + 1e-06) * (
            1.0 + mod_rows[1:2, :]
        ) + mod_rows[0:1, :]
        attended[here, :] = normed.astype(jnp.bfloat16)
        return carry

    lax.fori_loop(0, rows // block_rows, rows_of, 0)
    weight_copy.wait()
    projected = jnp.dot(attended[...], weight[...], preferred_element_type=jnp.float32)
    token = me * rows + lax.broadcasted_iota(jnp.int32, (rows, 1), 0)
    out_ref[...] = jnp.where(token < frames_ref[0] * (HH * WW), projected, 0.0).astype(
        out_ref.dtype
    )


def project(frames, hidden_state, modulation, down_weight, pieces, count):
    _, rows, model = hidden_state.shape
    channels = down_weight.shape[1]
    return pl.pallas_call(
        functools.partial(project_kernel, count),
        out_shape=jax.ShapeDtypeStruct((rows, channels), jnp.bfloat16),
        in_specs=[pl.BlockSpec(memory_space=pltpu.SMEM)]
        + [pl.BlockSpec(memory_space=pltpu.HBM)] * (count + 3),
        out_specs=pl.BlockSpec(memory_space=pltpu.VMEM),
        scratch_shapes=[
            pltpu.VMEM((rows, model), jnp.bfloat16),
            pltpu.VMEM((rows, model), jnp.bfloat16),
            pltpu.VMEM((model, channels), jnp.bfloat16),
            pltpu.VMEM((3, model), jnp.float32),
            pltpu.SemaphoreType.DMA((count,)),
            pltpu.SemaphoreType.DMA,
            pltpu.SemaphoreType.DMA,
            pltpu.SemaphoreType.DMA,
        ],
        cost_estimate=pl.CostEstimate(
            flops=2 * rows * model * channels,
            bytes_accessed=4 * rows * model + 2 * model * channels,
            transcendentals=0,
        ),
        name="project",
    )(frames, hidden_state, modulation, down_weight, *pieces)


def constants_kernel(mod_ref, weight_ref, out_ref):
    def product(row):
        high = row.astype(jnp.bfloat16)
        low = (row - high.astype(jnp.float32)).astype(jnp.bfloat16)
        split = jnp.concatenate(
            [jnp.broadcast_to(high, (8,) + high.shape[1:]), jnp.broadcast_to(low, (8,) + low.shape[1:])],
            axis=0,
        )
        both = jnp.dot(split, weight_ref[...], preferred_element_type=jnp.float32)
        return both[:8] + both[8:]

    out_ref[0] = product(1.0 + mod_ref[1:2, :])
    out_ref[1] = product(mod_ref[0:1, :])


def constants(mod_rows, down_weight):
    model, channels = down_weight.shape
    return pl.pallas_call(
        constants_kernel,
        out_shape=jax.ShapeDtypeStruct((2, 8, channels), jnp.float32),
        in_specs=[pl.BlockSpec(memory_space=pltpu.VMEM)] * 2,
        out_specs=pl.BlockSpec(memory_space=pltpu.VMEM),
        cost_estimate=pl.CostEstimate(
            flops=64 * model * channels, bytes_accessed=2 * model * channels, transcendentals=0
        ),
        name="constants",
    )(mod_rows, down_weight)


def early_kernel(count, head_cols, h_ref, mod_ref, weight_ref, *rest):
    pieces, rest = rest[:count], rest[count:]
    acc_ref, centre_ref, square_ref, late_h, late_mod, late_weight = rest[:6]
    attended, hidden, weight, mod, in_sem, h_sem, mod_sem, weight_sem, late_sem = rest[6:]
    me = lax.axis_index("ctx")
    rows, width = pieces[0].shape
    late = head_cols - width
    block_rows = 16

    def copies(step):
        col = pl.multiple_of(partner(me, step, count)[1] * head_cols, 128)
        here = pl.ds(step * width, width)
        return (
            pltpu.make_async_copy(pieces[step], attended.at[:, here], in_sem.at[step]),
            pltpu.make_async_copy(
                h_ref.at[0, :, pl.ds(col, width)], hidden.at[:, here], h_sem.at[step]
            ),
            pltpu.make_async_copy(
                mod_ref.at[:, pl.ds(col, width)], mod.at[:, here], mod_sem.at[step]
            ),
            pltpu.make_async_copy(
                weight_ref.at[pl.ds(col, width), :], weight.at[here, :], weight_sem.at[step]
            ),
        )

    def late_copies(step):
        col = pl.multiple_of(partner(me, step, count)[1] * head_cols + width, 128)
        here = pl.ds(step * late, late)
        return (
            pltpu.make_async_copy(
                h_ref.at[0, :, pl.ds(col, late)], late_h.at[:, here], late_sem.at[0, step]
            ),
            pltpu.make_async_copy(
                mod_ref.at[:, pl.ds(col, late)], late_mod.at[:, here], late_sem.at[1, step]
            ),
            pltpu.make_async_copy(
                weight_ref.at[pl.ds(col, late), :], late_weight.at[here, :], late_sem.at[2, step]
            ),
        )

    for step in range(count):
        for copy in copies(step):
            copy.start()
    for step in range(count):
        for copy in late_copies(step):
            copy.start()
    for step in range(count):
        for copy in copies(step)[:3]:
            copy.wait()

    def rows_of(index, carry):
        here = pl.ds(pl.multiple_of(index * block_rows, block_rows), block_rows)
        wide = (
            (
                hidden[here, :].astype(jnp.float32)
                + mod[2:3, :] * attended[here, :].astype(jnp.float32)
            )
            .astype(jnp.bfloat16)
            .astype(jnp.float32)
        )
        centre = jnp.mean(wide, axis=-1, keepdims=True)
        away = wide - centre
        square = jnp.sum(jnp.square(away), axis=-1, keepdims=True)
        attended[here, :] = (away * (1.0 + mod[1:2, :])).astype(jnp.bfloat16)
        centre_ref[here, :] = jnp.broadcast_to(centre, (block_rows, 128))
        square_ref[here, :] = jnp.broadcast_to(square, (block_rows, 128))
        return carry

    lax.fori_loop(0, rows // block_rows, rows_of, 0)
    for step in range(count):
        copies(step)[3].wait()
    acc_ref[...] = jnp.dot(attended[...], weight[...], preferred_element_type=jnp.float32)
    for step in range(count):
        for copy in late_copies(step):
            copy.wait()


def project_early(hidden_state, mod_rows, down_weight, pieces, count):
    _, rows, model = hidden_state.shape
    channels = down_weight.shape[1]
    head_cols = model // count
    width = pieces[0].shape[1]
    late = head_cols - width
    hbm = pl.BlockSpec(memory_space=pltpu.HBM)
    vmem = pl.BlockSpec(memory_space=pltpu.VMEM)
    return pl.pallas_call(
        functools.partial(early_kernel, count, head_cols),
        out_shape=[
            jax.ShapeDtypeStruct((rows, channels), jnp.float32),
            jax.ShapeDtypeStruct((rows, 128), jnp.float32),
            jax.ShapeDtypeStruct((rows, 128), jnp.float32),
            jax.ShapeDtypeStruct((rows, count * late), jnp.bfloat16),
            jax.ShapeDtypeStruct((3, count * late), jnp.float32),
            jax.ShapeDtypeStruct((count * late, channels), jnp.bfloat16),
        ],
        in_specs=[hbm] * (count + 3),
        out_specs=[vmem] * 6,
        scratch_shapes=[
            pltpu.VMEM((rows, count * width), jnp.bfloat16),
            pltpu.VMEM((rows, count * width), jnp.bfloat16),
            pltpu.VMEM((count * width, channels), jnp.bfloat16),
            pltpu.VMEM((3, count * width), jnp.float32),
            pltpu.SemaphoreType.DMA((count,)),
            pltpu.SemaphoreType.DMA((count,)),
            pltpu.SemaphoreType.DMA((count,)),
            pltpu.SemaphoreType.DMA((count,)),
            pltpu.SemaphoreType.DMA((3, count)),
        ],
        cost_estimate=pl.CostEstimate(
            flops=2 * rows * count * width * channels,
            bytes_accessed=4 * rows * model + 2 * model * channels,
            transcendentals=0,
        ),
        name="project_early",
    )(hidden_state, mod_rows, down_weight, *pieces)


def late_kernel(
    count, early, frames_ref, acc_ref, centre_ref, square_ref, h_ref, mod_ref, weight_ref, const_ref, *rest
):
    pieces, (out_ref, attended, in_sem) = rest[:count], rest[count:]
    rows, width = pieces[0].shape
    late = count * width
    model = early + late

    def load(step):
        return pltpu.make_async_copy(
            pieces[step], attended.at[:, pl.ds(step * width, width)], in_sem.at[step]
        )

    for step in range(count):
        load(step).start()
    for step in range(count):
        load(step).wait()
    wide = (
        (h_ref[...].astype(jnp.float32) + mod_ref[2:3, :] * attended[...].astype(jnp.float32))
        .astype(jnp.bfloat16)
        .astype(jnp.float32)
    )
    first = centre_ref[:, :1]
    own = jnp.mean(wide, axis=-1, keepdims=True)
    square = jnp.sum(jnp.square(wide - own), axis=-1, keepdims=True)
    gap = own - first
    centre = first + gap * (late / model)
    spread = (square_ref[:, :1] + square + gap * gap * (early * late / model)) / model
    scaled = ((wide - first) * (1.0 + mod_ref[1:2, :])).astype(jnp.bfloat16)
    total = acc_ref[...] + jnp.dot(scaled, weight_ref[...], preferred_element_type=jnp.float32)
    total = total + (first - centre) * const_ref[0, :1, :]
    total = total * lax.rsqrt(spread + 1e-06) + const_ref[1, :1, :]
    token = lax.axis_index("ctx") * rows + lax.broadcasted_iota(jnp.int32, (rows, 1), 0)
    out_ref[...] = jnp.where(token < frames_ref[0] * (HH * WW), total, 0.0).astype(out_ref.dtype)


def project_late(frames, early, consts, pieces, count, model):
    rows, width = pieces[0].shape
    channels = consts.shape[-1]
    hbm = pl.BlockSpec(memory_space=pltpu.HBM)
    vmem = pl.BlockSpec(memory_space=pltpu.VMEM)
    return pl.pallas_call(
        functools.partial(late_kernel, count, model - count * width),
        out_shape=jax.ShapeDtypeStruct((rows, channels), jnp.bfloat16),
        in_specs=[pl.BlockSpec(memory_space=pltpu.SMEM)] + [vmem] * 7 + [hbm] * count,
        out_specs=vmem,
        scratch_shapes=[
            pltpu.VMEM((rows, count * width), jnp.bfloat16),
            pltpu.SemaphoreType.DMA((count,)),
        ],
        cost_estimate=pl.CostEstimate(
            flops=2 * rows * count * width * channels,
            bytes_accessed=4 * rows * count * width,
            transcendentals=0,
        ),
        name="project_late",
    )(frames, *early, consts, *pieces)


def shifted_frames(frames, channels):
    cells = HH * WW
    column = lax.broadcasted_iota(jnp.int32, (cells, 1), 0) % WW
    blank = jnp.zeros((WW, channels), jnp.float32)
    shifted = []
    for offset in (-1, 0, 1):
        moved = []
        for frame in frames:
            cell = frame.astype(jnp.float32)
            if offset:
                cell = pltpu.roll(cell, (-offset) % cells, 0)
                inside = (column + offset >= 0) & (column + offset < WW)
                cell = jnp.where(inside, cell, 0.0)
            moved.append(jnp.concatenate([blank, cell, blank], axis=0))
        shifted.append(moved)
    return shifted


def window(shifted, across, down):
    cells = HH * WW
    return [f[down * WW : down * WW + cells].astype(jnp.bfloat16) for f in shifted[across]]


def inner_kernel(mid_ref, weight_ref, out_ref, weight, sem):
    cells = HH * WW
    rows, channels = mid_ref.shape
    copy = pltpu.make_async_copy(weight_ref, weight, sem)
    copy.start()
    frames = [mid_ref[pl.ds(start, cells), :] for start in range(0, rows, cells)]
    shifted = shifted_frames(frames, channels)
    copy.wait()
    totals = [frame.astype(jnp.float32) for frame in frames]
    centre = jnp.zeros((rows, channels), jnp.float32)
    for down in range(3):
        for across in range(3):
            picked = window(shifted, across, down)
            centre += jnp.dot(
                jnp.concatenate(picked, axis=0),
                weight[(3 + down) * 3 + across],
                preferred_element_type=jnp.float32,
            )
            for target in range(len(frames)):
                for ahead in (0, 2):
                    if 0 <= target + ahead - 1 < len(frames):
                        totals[target] += jnp.dot(
                            picked[target + ahead - 1],
                            weight[(ahead * 3 + down) * 3 + across],
                            preferred_element_type=jnp.float32,
                        )
    for target in range(len(frames)):
        here = pl.ds(target * cells, cells)
        out_ref[here, :] = totals[target] + centre[target * cells : (target + 1) * cells]


def edge_kernel(frames_ref, inner_ref, even_ref, odd_ref, weight_ref, out_ref, weight, sem):
    cells = HH * WW
    rows, channels = inner_ref.shape
    me = lax.axis_index("ctx")

    def fetch(ahead):
        return pltpu.make_async_copy(
            weight_ref.at[pl.ds(ahead * 9, 9)], weight.at[ahead // 2], sem.at[ahead // 2]
        )

    fetch(0).start()
    fetch(2).start()
    odd = lax.rem(me, 2) == 1
    low = jnp.where(odd, even_ref[...], odd_ref[...])
    high = jnp.where(odd, odd_ref[...], even_ref[...])
    shifted = shifted_frames([low, high], channels)
    first = inner_ref[pl.ds(0, cells), :]
    last = jnp.zeros((cells, channels), jnp.float32)
    fetch(0).wait()
    fetch(2).wait()
    for down in range(3):
        for across in range(3):
            below, above = window(shifted, across, down)
            first += jnp.dot(
                below, weight[0, down * 3 + across], preferred_element_type=jnp.float32
            )
            last += jnp.dot(
                above, weight[1, down * 3 + across], preferred_element_type=jnp.float32
            )
    blank = jnp.zeros((rows - cells, channels), jnp.float32)
    total = jnp.concatenate([first, inner_ref[pl.ds(cells, rows - cells), :]], axis=0)
    total = total + jnp.concatenate([blank, last], axis=0)
    token = me * rows + lax.broadcasted_iota(jnp.int32, (rows, 1), 0)
    out_ref[0] = jnp.where(token < frames_ref[0] * cells, total, 0.0).astype(out_ref.dtype)


def refine(frames, mid, even, odd, conv_weight):
    rows, channels = mid.shape
    taps = conv_weight.reshape(-1, channels, channels)
    hbm = pl.BlockSpec(memory_space=pltpu.HBM)
    vmem = pl.BlockSpec(memory_space=pltpu.VMEM)
    inner = pl.pallas_call(
        inner_kernel,
        out_shape=jax.ShapeDtypeStruct((rows, channels), jnp.float32),
        in_specs=[vmem, hbm],
        out_specs=vmem,
        scratch_shapes=[pltpu.VMEM(taps.shape, taps.dtype), pltpu.SemaphoreType.DMA],
        cost_estimate=pl.CostEstimate(
            flops=36 * rows * channels * channels,
            bytes_accessed=2 * taps.size + 6 * rows * channels,
            transcendentals=0,
        ),
        name="refine_inner",
    )(mid, taps)
    return pl.pallas_call(
        edge_kernel,
        out_shape=jax.ShapeDtypeStruct((1, rows, channels), jnp.bfloat16),
        in_specs=[pl.BlockSpec(memory_space=pltpu.SMEM)] + [vmem] * 3 + [hbm],
        out_specs=vmem,
        scratch_shapes=[
            pltpu.VMEM((2, 9) + taps.shape[1:], taps.dtype),
            pltpu.SemaphoreType.DMA((2,)),
        ],
        cost_estimate=pl.CostEstimate(
            flops=18 * rows * channels * channels,
            bytes_accessed=2 * taps.size + 6 * rows * channels,
            transcendentals=0,
        ),
        name="refine_edge",
    )(frames, inner, even, odd, taps)


def handoff(projected, destination, source, sec_count):
    if sec_count <= 4:
        orders = [
            order
            for order in itertools.permutations(range(sec_count))
            if any(order[(d + sec_count // 2) % sec_count] == d for d in range(sec_count))
        ]

        def take(order):
            return lambda value: lax.ppermute(value, "sec", list(enumerate(order)))

        codes = jnp.asarray(
            [sum(d * sec_count**i for i, d in enumerate(order)) for order in orders], jnp.int32
        )
        code = jnp.sum(destination * jnp.asarray([sec_count**i for i in range(sec_count)], jnp.int32))
        which = jnp.sum(jnp.where(codes == code, jnp.arange(len(orders), dtype=jnp.int32), 0))
        return lax.switch(which, [take(order) for order in orders], projected)
    my_section = lax.axis_index("sec")
    everyone = exchange([projected] * sec_count, "sec", sec_count)
    chosen = everyone[0]
    for step in range(1, sec_count):
        chosen = jnp.where(
            source == partner(my_section, step, sec_count)[1], everyone[step], chosen
        )
    return chosen


def halos(mid, count):
    cells = HH * WW
    rows, channels = mid.shape
    odd = lax.rem(lax.axis_index("ctx"), 2)
    start = jnp.where(odd == 1, 0, rows - cells)
    inner = [(i, i ^ 1) for i in range(count) if i ^ 1 < count]
    outer = [(i, i + 1) for i in range(1, count - 1, 2)] + [(i + 1, i) for i in range(1, count - 1, 2)]
    crossing = lax.dynamic_slice(mid, (rows - cells - start, 0), (cells, channels))
    beside = lax.dynamic_slice(mid, (start, 0), (cells, channels))
    return lax.ppermute(beside, "ctx", inner), lax.ppermute(crossing, "ctx", outer)


def body(
    hidden_state,
    queries,
    key_vectors,
    value_vectors,
    modulation,
    down_weight,
    conv_weight,
    clip_frames,
    destination,
    timestep,
):
    my_section = lax.axis_index("sec")
    sec_count = lax.axis_size("sec")
    count = lax.axis_size("ctx")
    model_width = hidden_state.shape[2]
    local_heads = HEADS // count
    head_size = model_width // HEADS
    head_cols = local_heads * head_size
    chunks = head_chunks(count)
    section_ids = jnp.arange(destination.shape[0], dtype=jnp.int32)
    source = jnp.sum(jnp.where(destination == my_section, section_ids, 0))
    own_frames = lax.dynamic_slice(clip_frames, (my_section,), (1,))
    clip_length = lax.dynamic_slice(clip_frames, (source,), (1,))
    my_step = timestep[my_section]
    mod_rows = lax.dynamic_index_in_dim(modulation, my_step, 0, keepdims=False)

    received = []
    first_head = 0
    for heads in chunks:
        sent = pack(
            (queries, key_vectors, value_vectors),
            count,
            head_cols,
            first_head * head_size,
            heads * head_size,
        )
        received.append(exchange(sent, "ctx", count))
        first_head += heads
    returned = []
    for chunk, heads in enumerate(chunks):
        outs = attend(own_frames, received[chunk], count, heads)
        returned.append(exchange(outs, "ctx", count))
    if len(chunks) == 1:
        projected = project(
            own_frames, hidden_state, mod_rows, down_weight, returned[0], count
        )
    else:
        early = project_early(hidden_state, mod_rows, down_weight, returned[0], count)
        consts = constants(mod_rows, down_weight)
        projected = project_late(own_frames, early, consts, returned[1], count, model_width)
    mid = handoff(projected, destination, source, sec_count)
    even, odd = halos(mid, count)
    return refine(clip_length, mid, even, odd, conv_weight)


def solution(mesh):
    split = P("sec", "ctx", None)
    return jax.shard_map(
        body,
        mesh=mesh,
        in_specs=(split,) * 4 + (P(),) * 6,
        out_specs=split,
        check_vma=False,
    )
```

```python
import functools
import itertools
import math

import jax
import jax.numpy as jnp
from jax import lax
from jax.experimental import pallas as pl
from jax.experimental.pallas import tpu as pltpu
from jax.sharding import PartitionSpec as P


HEADS = 32
VMEM_BYTES = 67043328
HH = 8
WW = 8


def head_chunks(count):
    local_heads = HEADS // count
    return (local_heads - 1, 1) if local_heads > 1 else (1,)


def partner(me, step, count):
    if count & (count - 1) == 0:
        return me ^ step, me ^ step
    return lax.rem(me + step, count), lax.rem(me - step + count, count)


def ring(step, count):
    if count & (count - 1) == 0:
        return [(i, i ^ step) for i in range(count)]
    return [(i, (i + step) % count) for i in range(count)]


def exchange(pieces, axis, count):
    out = [pieces[0]] + [None] * (count - 1)
    for step in range(1, count):
        out[step] = lax.ppermute(pieces[step], axis, ring(step, count))
    return out


def pack_kernel(count, kinds, head_cols, first_col, width, *rest):
    sources, outs, (buf, in_sem, out_sem) = rest[:kinds], rest[kinds : kinds + count], rest[kinds + count :]
    me = lax.axis_index("ctx")
    order = list(range(count - 1, -1, -1))

    def load(step, kind):
        col = pl.multiple_of(partner(me, step, count)[0] * head_cols + first_col, 128)
        return pltpu.make_async_copy(
            sources[kind].at[0, :, pl.ds(col, width)], buf.at[step, kind], in_sem.at[step, kind]
        )

    def save(step):
        return pltpu.make_async_copy(buf.at[step], outs[step], out_sem.at[step])

    for step in order:
        for kind in range(kinds):
            load(step, kind).start()
    for step in order:
        for kind in range(kinds):
            load(step, kind).wait()
        save(step).start()
    for step in order:
        save(step).wait()


def pack(sources, count, head_cols, first_col, width):
    rows = sources[0].shape[1]
    kinds = len(sources)
    piece = jax.ShapeDtypeStruct((kinds, rows, width), sources[0].dtype)
    return pl.pallas_call(
        functools.partial(pack_kernel, count, kinds, head_cols, first_col, width),
        out_shape=[piece] * count,
        in_specs=[pl.BlockSpec(memory_space=pltpu.HBM)] * kinds,
        out_specs=[pl.BlockSpec(memory_space=pltpu.HBM)] * count,
        scratch_shapes=[
            pltpu.VMEM((count, kinds, rows, width), sources[0].dtype),
            pltpu.SemaphoreType.DMA((count, kinds)),
            pltpu.SemaphoreType.DMA((count,)),
        ],
        cost_estimate=pl.CostEstimate(
            flops=0, bytes_accessed=4 * kinds * count * rows * width, transcendentals=0
        ),
        compiler_params=pltpu.CompilerParams(vmem_limit_bytes=VMEM_BYTES),
        name="pack",
    )(*sources)


def attend_kernel(count, heads, block_rows, frames_ref, *rest):
    pieces, outs = rest[:count], rest[count : 2 * count]
    data, values, result, in_sem, value_sem, out_sem = rest[2 * count :]
    me = lax.axis_index("ctx")
    rows = pieces[0].shape[1]
    seq = count * rows
    size = pieces[0].shape[2] // heads
    scale = math.log2(math.e) / math.sqrt(size)

    def place(step):
        return pl.ds(pl.multiple_of(partner(me, step, count)[1] * rows, rows), rows)

    def load(step):
        return pltpu.make_async_copy(
            pieces[step].at[pl.ds(0, 2)], data.at[:, place(step), :], in_sem.at[step]
        )

    def load_values(step, head):
        return pltpu.make_async_copy(
            pieces[step].at[2, :, pl.ds(head * size, size)],
            values.at[place(step), pl.ds(head * 2 * size, size)],
            value_sem.at[head, step],
        )

    def save(step):
        return pltpu.make_async_copy(result.at[place(step), :], outs[step], out_sem.at[step])

    for step in range(count):
        load(step).start()
    for head in range(heads):
        for step in range(count):
            load_values(step, head).start()
    for head in range(heads):
        values[:, pl.ds((head * 2 + 1) * size, size)] = jnp.ones((seq, size), jnp.bfloat16)
    for step in range(count):
        load(step).wait()
    for head in range(heads):
        for step in range(count):
            load_values(step, head).wait()
    valid = frames_ref[0] * (HH * WW)
    places = lax.broadcasted_iota(jnp.int32, (1, seq), 1)
    bias = jnp.where(places < valid, 0.0, -jnp.inf)

    def block(index, carry):
        start = pl.multiple_of(index * block_rows, block_rows)
        here = pl.ds(start, block_rows)
        for head in range(heads):
            lanes = pl.ds(head * size, size)
            scores = lax.dot_general(
                data[0, here, lanes],
                data[1, :, lanes],
                (((1,), (1,)), ((), ())),
                preferred_element_type=jnp.float32,
            )
            scores = scores * scale + bias
            weights = jnp.exp2(scores - jnp.max(scores, axis=1, keepdims=True))
            both = jnp.dot(
                weights.astype(jnp.bfloat16),
                values[:, pl.ds(head * 2 * size, 2 * size)],
                preferred_element_type=jnp.float32,
            )
            result[here, lanes] = (both[:, :size] / both[:, size:]).astype(result.dtype)
        return carry

    lax.fori_loop(0, seq // block_rows, block, 0, unroll=4)
    for step in range(count):
        save(step).start()
    for step in range(count):
        save(step).wait()


def attend(frames, pieces, count, heads):
    _, rows, width = pieces[0].shape
    seq = count * rows
    block_rows = min(256, seq)
    return pl.pallas_call(
        functools.partial(attend_kernel, count, heads, block_rows),
        out_shape=[jax.ShapeDtypeStruct((rows, width), jnp.bfloat16)] * count,
        in_specs=[pl.BlockSpec(memory_space=pltpu.SMEM)]
        + [pl.BlockSpec(memory_space=pltpu.HBM)] * count,
        out_specs=[pl.BlockSpec(memory_space=pltpu.HBM)] * count,
        scratch_shapes=[
            pltpu.VMEM((2, seq, width), jnp.bfloat16),
            pltpu.VMEM((seq, 2 * width), jnp.bfloat16),
            pltpu.VMEM((seq, width), jnp.bfloat16),
            pltpu.SemaphoreType.DMA((count,)),
            pltpu.SemaphoreType.DMA((heads, count)),
            pltpu.SemaphoreType.DMA((count,)),
        ],
        cost_estimate=pl.CostEstimate(
            flops=6 * seq * seq * width,
            bytes_accessed=8 * seq * width,
            transcendentals=seq * seq * heads,
        ),
        compiler_params=pltpu.CompilerParams(vmem_limit_bytes=VMEM_BYTES),
        name="attend",
    )(frames, *pieces)


def project_kernel(count, frames_ref, h_ref, mod_ref, weight_ref, *rest):
    pieces, rest = rest[:count], rest[count:]
    out_ref, attended, hidden, weight, mod_rows, in_sem, mod_sem, h_sem, weight_sem = rest
    me = lax.axis_index("ctx")
    rows, width = pieces[0].shape
    block_rows = 16

    def load(step):
        owner = partner(me, step, count)[1]
        col = pl.multiple_of(owner * width, 128)
        return pltpu.make_async_copy(
            pieces[step], attended.at[:, pl.ds(col, width)], in_sem.at[step]
        )

    mod_copy = pltpu.make_async_copy(mod_ref, mod_rows, mod_sem)
    h_copy = pltpu.make_async_copy(h_ref.at[0], hidden, h_sem)
    weight_copy = pltpu.make_async_copy(weight_ref, weight, weight_sem)
    mod_copy.start()
    h_copy.start()
    for step in range(count):
        load(step).start()
    weight_copy.start()
    mod_copy.wait()
    h_copy.wait()
    for step in range(count):
        load(step).wait()

    def rows_of(index, carry):
        here = pl.ds(pl.multiple_of(index * block_rows, block_rows), block_rows)
        block = (
            hidden[here, :].astype(jnp.float32)
            + mod_rows[2:3, :] * attended[here, :].astype(jnp.float32)
        ).astype(jnp.bfloat16)
        wide = block.astype(jnp.float32)
        centre = jnp.mean(wide, axis=-1, keepdims=True)
        spread = jnp.mean(jnp.square(wide - centre), axis=-1, keepdims=True)
        normed = (wide - centre) * lax.rsqrt(spread + 1e-06) * (
            1.0 + mod_rows[1:2, :]
        ) + mod_rows[0:1, :]
        attended[here, :] = normed.astype(jnp.bfloat16)
        return carry

    lax.fori_loop(0, rows // block_rows, rows_of, 0)
    weight_copy.wait()
    projected = jnp.dot(attended[...], weight[...], preferred_element_type=jnp.float32)
    token = me * rows + lax.broadcasted_iota(jnp.int32, (rows, 1), 0)
    out_ref[...] = jnp.where(token < frames_ref[0] * (HH * WW), projected, 0.0).astype(
        out_ref.dtype
    )


def project(frames, hidden_state, modulation, down_weight, pieces, count):
    _, rows, model = hidden_state.shape
    channels = down_weight.shape[1]
    return pl.pallas_call(
        functools.partial(project_kernel, count),
        out_shape=jax.ShapeDtypeStruct((rows, channels), jnp.bfloat16),
        in_specs=[pl.BlockSpec(memory_space=pltpu.SMEM)]
        + [pl.BlockSpec(memory_space=pltpu.HBM)] * (count + 3),
        out_specs=pl.BlockSpec(memory_space=pltpu.VMEM),
        scratch_shapes=[
            pltpu.VMEM((rows, model), jnp.bfloat16),
            pltpu.VMEM((rows, model), jnp.bfloat16),
            pltpu.VMEM((model, channels), jnp.bfloat16),
            pltpu.VMEM((3, model), jnp.float32),
            pltpu.SemaphoreType.DMA((count,)),
            pltpu.SemaphoreType.DMA,
            pltpu.SemaphoreType.DMA,
            pltpu.SemaphoreType.DMA,
        ],
        cost_estimate=pl.CostEstimate(
            flops=2 * rows * model * channels,
            bytes_accessed=4 * rows * model + 2 * model * channels,
            transcendentals=0,
        ),
        compiler_params=pltpu.CompilerParams(vmem_limit_bytes=VMEM_BYTES),
        name="project",
    )(frames, hidden_state, modulation, down_weight, *pieces)


def constants_kernel(mod_ref, weight_ref, out_ref):
    def product(row):
        high = row.astype(jnp.bfloat16)
        low = (row - high.astype(jnp.float32)).astype(jnp.bfloat16)
        split = jnp.concatenate(
            [jnp.broadcast_to(high, (8,) + high.shape[1:]), jnp.broadcast_to(low, (8,) + low.shape[1:])],
            axis=0,
        )
        both = jnp.dot(split, weight_ref[...], preferred_element_type=jnp.float32)
        return both[:8] + both[8:]

    out_ref[0] = product(1.0 + mod_ref[1:2, :])
    out_ref[1] = product(mod_ref[0:1, :])


def constants(mod_rows, down_weight):
    model, channels = down_weight.shape
    return pl.pallas_call(
        constants_kernel,
        out_shape=jax.ShapeDtypeStruct((2, 8, channels), jnp.float32),
        in_specs=[pl.BlockSpec(memory_space=pltpu.VMEM)] * 2,
        out_specs=pl.BlockSpec(memory_space=pltpu.VMEM),
        cost_estimate=pl.CostEstimate(
            flops=64 * model * channels, bytes_accessed=2 * model * channels, transcendentals=0
        ),
        compiler_params=pltpu.CompilerParams(vmem_limit_bytes=VMEM_BYTES),
        name="constants",
    )(mod_rows, down_weight)


def early_kernel(count, head_cols, h_ref, mod_ref, weight_ref, *rest):
    pieces, rest = rest[:count], rest[count:]
    acc_ref, centre_ref, square_ref, late_h, late_mod, late_weight = rest[:6]
    attended, hidden, weight, mod, in_sem, h_sem, mod_sem, weight_sem, late_sem = rest[6:]
    me = lax.axis_index("ctx")
    rows, width = pieces[0].shape
    late = head_cols - width
    block_rows = 16

    def copies(step):
        col = pl.multiple_of(partner(me, step, count)[1] * head_cols, 128)
        here = pl.ds(step * width, width)
        return (
            pltpu.make_async_copy(pieces[step], attended.at[:, here], in_sem.at[step]),
            pltpu.make_async_copy(
                h_ref.at[0, :, pl.ds(col, width)], hidden.at[:, here], h_sem.at[step]
            ),
            pltpu.make_async_copy(
                mod_ref.at[:, pl.ds(col, width)], mod.at[:, here], mod_sem.at[step]
            ),
            pltpu.make_async_copy(
                weight_ref.at[pl.ds(col, width), :], weight.at[here, :], weight_sem.at[step]
            ),
        )

    def late_copies(step):
        col = pl.multiple_of(partner(me, step, count)[1] * head_cols + width, 128)
        here = pl.ds(step * late, late)
        return (
            pltpu.make_async_copy(
                h_ref.at[0, :, pl.ds(col, late)], late_h.at[:, here], late_sem.at[0, step]
            ),
            pltpu.make_async_copy(
                mod_ref.at[:, pl.ds(col, late)], late_mod.at[:, here], late_sem.at[1, step]
            ),
            pltpu.make_async_copy(
                weight_ref.at[pl.ds(col, late), :], late_weight.at[here, :], late_sem.at[2, step]
            ),
        )

    for step in range(count):
        for copy in copies(step):
            copy.start()
    for step in range(count):
        for copy in late_copies(step):
            copy.start()
    for step in range(count):
        for copy in copies(step)[:3]:
            copy.wait()

    def rows_of(index, carry):
        here = pl.ds(pl.multiple_of(index * block_rows, block_rows), block_rows)
        wide = (
            (
                hidden[here, :].astype(jnp.float32)
                + mod[2:3, :] * attended[here, :].astype(jnp.float32)
            )
            .astype(jnp.bfloat16)
            .astype(jnp.float32)
        )
        centre = jnp.mean(wide, axis=-1, keepdims=True)
        away = wide - centre
        square = jnp.sum(jnp.square(away), axis=-1, keepdims=True)
        attended[here, :] = (away * (1.0 + mod[1:2, :])).astype(jnp.bfloat16)
        centre_ref[here, :] = jnp.broadcast_to(centre, (block_rows, 128))
        square_ref[here, :] = jnp.broadcast_to(square, (block_rows, 128))
        return carry

    lax.fori_loop(0, rows // block_rows, rows_of, 0)
    for step in range(count):
        copies(step)[3].wait()
    acc_ref[...] = jnp.dot(attended[...], weight[...], preferred_element_type=jnp.float32)
    for step in range(count):
        for copy in late_copies(step):
            copy.wait()


def project_early(hidden_state, mod_rows, down_weight, pieces, count):
    _, rows, model = hidden_state.shape
    channels = down_weight.shape[1]
    head_cols = model // count
    width = pieces[0].shape[1]
    late = head_cols - width
    hbm = pl.BlockSpec(memory_space=pltpu.HBM)
    vmem = pl.BlockSpec(memory_space=pltpu.VMEM)
    return pl.pallas_call(
        functools.partial(early_kernel, count, head_cols),
        out_shape=[
            jax.ShapeDtypeStruct((rows, channels), jnp.float32),
            jax.ShapeDtypeStruct((rows, 128), jnp.float32),
            jax.ShapeDtypeStruct((rows, 128), jnp.float32),
            jax.ShapeDtypeStruct((rows, count * late), jnp.bfloat16),
            jax.ShapeDtypeStruct((3, count * late), jnp.float32),
            jax.ShapeDtypeStruct((count * late, channels), jnp.bfloat16),
        ],
        in_specs=[hbm] * (count + 3),
        out_specs=[vmem] * 6,
        scratch_shapes=[
            pltpu.VMEM((rows, count * width), jnp.bfloat16),
            pltpu.VMEM((rows, count * width), jnp.bfloat16),
            pltpu.VMEM((count * width, channels), jnp.bfloat16),
            pltpu.VMEM((3, count * width), jnp.float32),
            pltpu.SemaphoreType.DMA((count,)),
            pltpu.SemaphoreType.DMA((count,)),
            pltpu.SemaphoreType.DMA((count,)),
            pltpu.SemaphoreType.DMA((count,)),
            pltpu.SemaphoreType.DMA((3, count)),
        ],
        cost_estimate=pl.CostEstimate(
            flops=2 * rows * count * width * channels,
            bytes_accessed=4 * rows * model + 2 * model * channels,
            transcendentals=0,
        ),
        compiler_params=pltpu.CompilerParams(vmem_limit_bytes=VMEM_BYTES),
        name="project_early",
    )(hidden_state, mod_rows, down_weight, *pieces)


def late_kernel(count, early, frames_ref, *rest):
    sources, pieces, rest = rest[:7], rest[7 : 7 + count], rest[7 + count :]
    out_ref, attended, held, in_sem, held_sem = rest[0], rest[1], rest[2:9], rest[9], rest[10]
    acc_ref, centre_ref, square_ref, h_ref, mod_ref, weight_ref, const_ref = held
    rows, width = pieces[0].shape
    late = count * width
    model = early + late

    def load(step):
        return pltpu.make_async_copy(
            pieces[step], attended.at[:, pl.ds(step * width, width)], in_sem.at[step]
        )

    def hold(which):
        return pltpu.make_async_copy(sources[which], held[which], held_sem.at[which])

    for step in range(count):
        load(step).start()
    for which in (3, 4, 1, 2, 5, 0, 6):
        hold(which).start()
    for which in (3, 4, 1, 2):
        hold(which).wait()
    for step in range(count):
        load(step).wait()
    wide = (
        (h_ref[...].astype(jnp.float32) + mod_ref[2:3, :] * attended[...].astype(jnp.float32))
        .astype(jnp.bfloat16)
        .astype(jnp.float32)
    )
    first = centre_ref[:, :1]
    scaled = ((wide - first) * (1.0 + mod_ref[1:2, :])).astype(jnp.bfloat16)
    for which in (5, 0, 6):
        hold(which).wait()
    total = acc_ref[...] + jnp.dot(scaled, weight_ref[...], preferred_element_type=jnp.float32)
    own = jnp.mean(wide, axis=-1, keepdims=True)
    square = jnp.sum(jnp.square(wide - own), axis=-1, keepdims=True)
    gap = own - first
    centre = first + gap * (late / model)
    spread = (square_ref[:, :1] + square + gap * gap * (early * late / model)) / model
    total = total + (first - centre) * const_ref[0, :1, :]
    total = total * lax.rsqrt(spread + 1e-06) + const_ref[1, :1, :]
    token = lax.axis_index("ctx") * rows + lax.broadcasted_iota(jnp.int32, (rows, 1), 0)
    out_ref[...] = jnp.where(token < frames_ref[0] * (HH * WW), total, 0.0).astype(out_ref.dtype)


def project_late(frames, early, consts, pieces, count, model):
    rows, width = pieces[0].shape
    channels = consts.shape[-1]
    hbm = pl.BlockSpec(memory_space=pltpu.HBM)
    sources = (*early, consts)
    return pl.pallas_call(
        functools.partial(late_kernel, count, model - count * width),
        out_shape=jax.ShapeDtypeStruct((rows, channels), jnp.bfloat16),
        in_specs=[pl.BlockSpec(memory_space=pltpu.SMEM)] + [hbm] * (7 + count),
        out_specs=pl.BlockSpec(memory_space=pltpu.VMEM),
        scratch_shapes=[pltpu.VMEM((rows, count * width), jnp.bfloat16)]
        + [pltpu.VMEM(source.shape, source.dtype) for source in sources]
        + [pltpu.SemaphoreType.DMA((count,)), pltpu.SemaphoreType.DMA((7,))],
        cost_estimate=pl.CostEstimate(
            flops=2 * rows * count * width * channels,
            bytes_accessed=4 * rows * count * width,
            transcendentals=0,
        ),
        compiler_params=pltpu.CompilerParams(vmem_limit_bytes=VMEM_BYTES),
        name="project_late",
    )(frames, *sources, *pieces)


def gather_taps(frames, taps):
    cells = HH * WW
    channels = frames[0].shape[1]
    column = lax.broadcasted_iota(jnp.int32, (cells, 1), 0) % WW
    blank = jnp.zeros((WW, channels), jnp.float32)
    for number, frame in enumerate(frames):
        wide = frame.astype(jnp.float32)
        for across, offset in enumerate((-1, 0, 1)):
            cell = wide
            if offset:
                inside = (column + offset >= 0) & (column + offset < WW)
                cell = jnp.where(inside, pltpu.roll(wide, (-offset) % cells, 0), 0.0)
            cell = jnp.concatenate([blank, cell, blank], axis=0)
            for down in range(3):
                taps[
                    pl.ds(number * cells, cells), pl.ds((down * 3 + across) * channels, channels)
                ] = cell[down * WW : down * WW + cells].astype(jnp.bfloat16)


def inner_kernel(mid_ref, weight_ref, out_ref, taps, weight, sem):
    cells = HH * WW
    rows, _ = mid_ref.shape

    def fetch(ahead):
        return pltpu.make_async_copy(weight_ref.at[ahead], weight.at[ahead], sem.at[ahead])

    for ahead in (1, 0, 2):
        fetch(ahead).start()
    gather_taps([mid_ref[pl.ds(start, cells), :] for start in range(0, rows, cells)], taps)
    fetch(1).wait()
    out_ref[...] = mid_ref[...].astype(jnp.float32) + jnp.dot(
        taps[...], weight[1], preferred_element_type=jnp.float32
    )
    fetch(0).wait()
    fetch(2).wait()
    if rows > cells:
        rest = rows - cells
        out_ref[pl.ds(cells, rest), :] += jnp.dot(
            taps[pl.ds(0, rest), :], weight[0], preferred_element_type=jnp.float32
        )
        out_ref[pl.ds(0, rest), :] += jnp.dot(
            taps[pl.ds(cells, rest), :], weight[2], preferred_element_type=jnp.float32
        )


def edge_kernel(frames_ref, inner_ref, even_ref, odd_ref, weight_ref, out_ref, taps, weight, sem):
    cells = HH * WW
    rows, channels = inner_ref.shape
    me = lax.axis_index("ctx")

    def fetch(side):
        return pltpu.make_async_copy(weight_ref.at[2 * side], weight.at[side], sem.at[side])

    fetch(0).start()
    fetch(1).start()
    odd = lax.rem(me, 2) == 1
    low = jnp.where(odd, even_ref[...], odd_ref[...])
    high = jnp.where(odd, odd_ref[...], even_ref[...])
    gather_taps([low, high], taps)
    token = me * rows + lax.broadcasted_iota(jnp.int32, (rows, 1), 0)
    keep = token < frames_ref[0] * cells
    sides = []
    for side in range(2):
        fetch(side).wait()
        sides.append(
            jnp.dot(
                taps[pl.ds(side * cells, cells), :],
                weight[side],
                preferred_element_type=jnp.float32,
            )
        )
    if rows > cells:
        blank = jnp.zeros((rows - cells, channels), jnp.float32)
        total = (
            inner_ref[...]
            + jnp.concatenate([sides[0], blank], axis=0)
            + jnp.concatenate([blank, sides[1]], axis=0)
        )
    else:
        total = inner_ref[...] + sides[0] + sides[1]
    out_ref[0] = jnp.where(keep, total, 0.0).astype(out_ref.dtype)


def refine(frames, mid, even, odd, conv_weight):
    rows, channels = mid.shape
    taps = conv_weight.reshape(3, 9 * channels, channels)
    hbm = pl.BlockSpec(memory_space=pltpu.HBM)
    vmem = pl.BlockSpec(memory_space=pltpu.VMEM)
    inner = pl.pallas_call(
        inner_kernel,
        out_shape=jax.ShapeDtypeStruct((rows, channels), jnp.float32),
        in_specs=[vmem, hbm],
        out_specs=vmem,
        scratch_shapes=[
            pltpu.VMEM((rows, 9 * channels), jnp.bfloat16),
            pltpu.VMEM(taps.shape, taps.dtype),
            pltpu.SemaphoreType.DMA((3,)),
        ],
        cost_estimate=pl.CostEstimate(
            flops=36 * rows * channels * channels,
            bytes_accessed=2 * taps.size + 6 * rows * channels,
            transcendentals=0,
        ),
        compiler_params=pltpu.CompilerParams(vmem_limit_bytes=VMEM_BYTES),
        name="refine_inner",
    )(mid, taps)
    return pl.pallas_call(
        edge_kernel,
        out_shape=jax.ShapeDtypeStruct((1, rows, channels), jnp.bfloat16),
        in_specs=[pl.BlockSpec(memory_space=pltpu.SMEM)] + [vmem] * 3 + [hbm],
        out_specs=vmem,
        scratch_shapes=[
            pltpu.VMEM((2 * HH * WW, 9 * channels), jnp.bfloat16),
            pltpu.VMEM((2,) + taps.shape[1:], taps.dtype),
            pltpu.SemaphoreType.DMA((2,)),
        ],
        cost_estimate=pl.CostEstimate(
            flops=18 * rows * channels * channels,
            bytes_accessed=2 * taps.size + 6 * rows * channels,
            transcendentals=0,
        ),
        compiler_params=pltpu.CompilerParams(vmem_limit_bytes=VMEM_BYTES),
        name="refine_edge",
    )(frames, inner, even, odd, taps)


def handoff(projected, destination, source, sec_count):
    if sec_count <= 4:
        orders = [
            order
            for order in itertools.permutations(range(sec_count))
            if any(order[(d + sec_count // 2) % sec_count] == d for d in range(sec_count))
        ]

        def take(order):
            return lambda value: lax.ppermute(value, "sec", list(enumerate(order)))

        codes = jnp.asarray(
            [sum(d * sec_count**i for i, d in enumerate(order)) for order in orders], jnp.int32
        )
        code = jnp.sum(destination * jnp.asarray([sec_count**i for i in range(sec_count)], jnp.int32))
        which = jnp.sum(jnp.where(codes == code, jnp.arange(len(orders), dtype=jnp.int32), 0))
        return lax.switch(which, [take(order) for order in orders], projected)
    my_section = lax.axis_index("sec")
    everyone = exchange([projected] * sec_count, "sec", sec_count)
    chosen = everyone[0]
    for step in range(1, sec_count):
        chosen = jnp.where(
            source == partner(my_section, step, sec_count)[1], everyone[step], chosen
        )
    return chosen


def halos(mid, count):
    cells = HH * WW
    rows, channels = mid.shape
    odd = lax.rem(lax.axis_index("ctx"), 2)
    start = jnp.where(odd == 1, 0, rows - cells)
    inner = [(i, i ^ 1) for i in range(count) if i ^ 1 < count]
    outer = [(i, i + 1) for i in range(1, count - 1, 2)] + [(i + 1, i) for i in range(1, count - 1, 2)]
    crossing = lax.dynamic_slice(mid, (rows - cells - start, 0), (cells, channels))
    beside = lax.dynamic_slice(mid, (start, 0), (cells, channels))
    return lax.ppermute(beside, "ctx", inner), lax.ppermute(crossing, "ctx", outer)


def body(
    hidden_state,
    queries,
    key_vectors,
    value_vectors,
    modulation,
    down_weight,
    conv_weight,
    clip_frames,
    destination,
    timestep,
):
    my_section = lax.axis_index("sec")
    sec_count = lax.axis_size("sec")
    count = lax.axis_size("ctx")
    model_width = hidden_state.shape[2]
    local_heads = HEADS // count
    head_size = model_width // HEADS
    head_cols = local_heads * head_size
    chunks = head_chunks(count)
    section_ids = jnp.arange(destination.shape[0], dtype=jnp.int32)
    source = jnp.sum(jnp.where(destination == my_section, section_ids, 0))
    own_frames = lax.dynamic_slice(clip_frames, (my_section,), (1,))
    clip_length = lax.dynamic_slice(clip_frames, (source,), (1,))
    my_step = timestep[my_section]
    mod_rows = lax.dynamic_index_in_dim(modulation, my_step, 0, keepdims=False)

    received = []
    first_head = 0
    for heads in chunks:
        sent = pack(
            (queries, key_vectors, value_vectors),
            count,
            head_cols,
            first_head * head_size,
            heads * head_size,
        )
        received.append(exchange(sent, "ctx", count))
        first_head += heads
    returned = []
    for chunk, heads in enumerate(chunks):
        outs = attend(own_frames, received[chunk], count, heads)
        returned.append(exchange(outs, "ctx", count))
    if len(chunks) == 1:
        projected = project(
            own_frames, hidden_state, mod_rows, down_weight, returned[0], count
        )
    else:
        early = project_early(hidden_state, mod_rows, down_weight, returned[0], count)
        consts = constants(mod_rows, down_weight)
        projected = project_late(own_frames, early, consts, returned[1], count, model_width)
    mid = handoff(projected, destination, source, sec_count)
    even, odd = halos(mid, count)
    return refine(clip_length, mid, even, odd, conv_weight)


def solution(mesh):
    split = P("sec", "ctx", None)
    return jax.shard_map(
        body,
        mesh=mesh,
        in_specs=(split,) * 4 + (P(),) * 6,
        out_specs=split,
        check_vma=False,
    )
```

```python
import functools
import itertools
import math

import jax
import jax.numpy as jnp
from jax import lax
from jax.experimental import pallas as pl
from jax.experimental.pallas import tpu as pltpu
from jax.sharding import PartitionSpec as P


HEADS = 32
VMEM_BYTES = 67043328
HH = 8
WW = 8


def head_chunks(group):
    late = max(1, group // 4)
    return group - late, late


def partner(me, step, count):
    if count & (count - 1) == 0:
        return me ^ step, me ^ step
    return lax.rem(me + step, count), lax.rem(me - step + count, count)


def ring(step, count):
    if count & (count - 1) == 0:
        return [(i, i ^ step) for i in range(count)]
    return [(i, (i + step) % count) for i in range(count)]


def send(value, step, chips):
    pairs = [
        (2 * one + core, 2 * two + core) for one, two in ring(step, chips) for core in range(2)
    ]
    return lax.ppermute(value, "ctx", pairs)


def across(value, chips):
    return lax.ppermute(value, "ctx", [(i, i ^ 1) for i in range(2 * chips)])


def my_chip(step, chips):
    return partner(lax.axis_index("ctx") // 2, step, chips)


def pack_kernel(chips, kinds, head_cols, first_col, width, *rest):
    sources, outs, (buf, in_sem, out_sem) = rest[:kinds], rest[kinds : kinds + chips], rest[kinds + chips :]
    order = list(range(chips - 1, -1, -1))

    def load(step, kind):
        col = pl.multiple_of(my_chip(step, chips)[0] * head_cols + first_col, 128)
        return pltpu.make_async_copy(
            sources[kind].at[0, :, pl.ds(col, width)], buf.at[step, kind], in_sem.at[step, kind]
        )

    def save(step):
        return pltpu.make_async_copy(buf.at[step], outs[step], out_sem.at[step])

    for step in order:
        for kind in range(kinds):
            load(step, kind).start()
    for step in order:
        for kind in range(kinds):
            load(step, kind).wait()
        save(step).start()
    for step in order:
        save(step).wait()


def pack(sources, chips, head_cols, first_col, width):
    rows = sources[0].shape[1]
    kinds = len(sources)
    piece = jax.ShapeDtypeStruct((kinds, rows, width), sources[0].dtype)
    return pl.pallas_call(
        functools.partial(pack_kernel, chips, kinds, head_cols, first_col, width),
        out_shape=[piece] * chips,
        in_specs=[pl.BlockSpec(memory_space=pltpu.HBM)] * kinds,
        out_specs=[pl.BlockSpec(memory_space=pltpu.HBM)] * chips,
        scratch_shapes=[
            pltpu.VMEM((chips, kinds, rows, width), sources[0].dtype),
            pltpu.SemaphoreType.DMA((chips, kinds)),
            pltpu.SemaphoreType.DMA((chips,)),
        ],
        cost_estimate=pl.CostEstimate(
            flops=0, bytes_accessed=4 * kinds * chips * rows * width, transcendentals=0
        ),
        compiler_params=pltpu.CompilerParams(vmem_limit_bytes=VMEM_BYTES),
        name="pack",
    )(*sources)


def attend_kernel(chips, heads, block_rows, frames_ref, *rest):
    own, beside, outs = rest[:chips], rest[chips : 2 * chips], rest[2 * chips : 3 * chips]
    queries, keys, values, result, in_sem, value_sem, out_sem = rest[3 * chips :]
    core = lax.rem(lax.axis_index("ctx"), 2)
    rows = own[0].shape[1]
    asked = chips * rows
    seq = 2 * asked
    size = own[0].shape[2] // heads
    scale = math.log2(math.e) / math.sqrt(size)
    blocks = asked // block_rows

    def place(step, side):
        device = my_chip(step, chips)[1] * 2 + (core if side == 0 else 1 - core)
        return pl.ds(pl.multiple_of(device * rows, rows), rows)

    def load(step, which):
        if which == 2:
            source, target = own[step].at[0], queries.at[pl.ds(step * rows, rows), :]
        else:
            source, target = (own, beside)[which][step].at[1], keys.at[place(step, which), :]
        return pltpu.make_async_copy(source, target, in_sem.at[which, step])

    def load_values(step, side, head):
        return pltpu.make_async_copy(
            (own, beside)[side][step].at[2, :, pl.ds(head * size, size)],
            values.at[place(step, side), pl.ds(head * 2 * size, size)],
            value_sem.at[side, head, step],
        )

    def save(step):
        return pltpu.make_async_copy(
            result.at[pl.ds(step * rows, rows), :], outs[step], out_sem.at[step]
        )

    for step in range(chips):
        for which in range(3):
            load(step, which).start()
    for head in range(heads):
        for step in range(chips):
            for side in range(2):
                load_values(step, side, head).start()
    for head in range(heads):
        values[:, pl.ds((head * 2 + 1) * size, size)] = jnp.ones((seq, size), jnp.bfloat16)
    valid = frames_ref[0] * (HH * WW)
    places = lax.broadcasted_iota(jnp.int32, (1, seq), 1)
    bias = jnp.where(places < valid, 0.0, -jnp.inf)
    for step in range(chips):
        for which in range(3):
            load(step, which).wait()
    for head in range(heads):
        for step in range(chips):
            for side in range(2):
                load_values(step, side, head).wait()

    def task(index, carry):
        head = index // blocks
        start = pl.multiple_of(lax.rem(index, blocks) * block_rows, block_rows)
        here = pl.ds(start, block_rows)
        lanes = pl.ds(pl.multiple_of(head * size, size), size)
        scores = lax.dot_general(
            queries[here, lanes],
            keys[:, lanes],
            (((1,), (1,)), ((), ())),
            preferred_element_type=jnp.float32,
        )
        scores = scores * scale + bias
        weights = jnp.exp2(scores - jnp.max(scores, axis=1, keepdims=True))
        both = jnp.dot(
            weights.astype(jnp.bfloat16),
            values[:, pl.ds(pl.multiple_of(head * (2 * size), 2 * size), 2 * size)],
            preferred_element_type=jnp.float32,
        )
        result[here, lanes] = (both[:, :size] / both[:, size:]).astype(result.dtype)
        return carry

    lax.fori_loop(0, heads * blocks, task, 0, unroll=4)
    for step in range(chips):
        save(step).start()
    for step in range(chips):
        save(step).wait()


def attend(frames, own, beside, heads):
    chips = len(own)
    _, rows, width = own[0].shape
    asked = chips * rows
    seq = 2 * asked
    block_rows = min(256, asked)
    return pl.pallas_call(
        functools.partial(attend_kernel, chips, heads, block_rows),
        out_shape=[jax.ShapeDtypeStruct((rows, width), jnp.bfloat16)] * chips,
        in_specs=[pl.BlockSpec(memory_space=pltpu.SMEM)]
        + [pl.BlockSpec(memory_space=pltpu.HBM)] * (2 * chips),
        out_specs=[pl.BlockSpec(memory_space=pltpu.HBM)] * chips,
        scratch_shapes=[
            pltpu.VMEM((asked, width), jnp.bfloat16),
            pltpu.VMEM((seq, width), jnp.bfloat16),
            pltpu.VMEM((seq, 2 * width), jnp.bfloat16),
            pltpu.VMEM((asked, width), jnp.bfloat16),
            pltpu.SemaphoreType.DMA((3, chips)),
            pltpu.SemaphoreType.DMA((2, heads, chips)),
            pltpu.SemaphoreType.DMA((chips,)),
        ],
        cost_estimate=pl.CostEstimate(
            flops=6 * asked * seq * width,
            bytes_accessed=8 * seq * width,
            transcendentals=asked * seq * heads,
        ),
        compiler_params=pltpu.CompilerParams(vmem_limit_bytes=VMEM_BYTES),
        name="attend",
    )(frames, *own, *beside)


def prepare_kernel(chips, head_cols, width, h_ref, mod_ref, weight_ref, *rest):
    h_out, mod_out, weight_out, const_ref, _, mod, weight, late_h, late_mod, late_weight, in_sem, out_sem = rest
    late = head_cols - width

    def pull(step, which):
        col = pl.multiple_of(my_chip(step, chips)[1] * head_cols + width, 128)
        here = pl.ds(step * late, late)
        source, target = (
            (h_ref.at[0, :, pl.ds(col, late)], late_h.at[:, here]),
            (mod_ref.at[:, pl.ds(col, late)], late_mod.at[:, here]),
            (weight_ref.at[pl.ds(col, late), :], late_weight.at[here, :]),
        )[which]
        return pltpu.make_async_copy(source, target, in_sem.at[which, step])

    def whole(which):
        source, target = ((mod_ref, mod), (weight_ref, weight))[which]
        return pltpu.make_async_copy(source, target, in_sem.at[3, which])

    def push(which):
        source, target = ((late_h, h_out), (late_mod, mod_out), (late_weight, weight_out))[which]
        return pltpu.make_async_copy(source, target, out_sem.at[which])

    for which in range(3):
        for step in range(chips):
            pull(step, which).start()
    whole(0).start()
    whole(1).start()
    for which in range(3):
        for step in range(chips):
            pull(step, which).wait()
        push(which).start()

    def product(row):
        high = row.astype(jnp.bfloat16)
        low = (row - high.astype(jnp.float32)).astype(jnp.bfloat16)
        split = jnp.concatenate(
            [jnp.broadcast_to(high, (8,) + high.shape[1:]), jnp.broadcast_to(low, (8,) + low.shape[1:])],
            axis=0,
        )
        both = jnp.dot(split, weight[...], preferred_element_type=jnp.float32)
        return both[:8] + both[8:]

    whole(0).wait()
    whole(1).wait()
    const_ref[0] = product(1.0 + mod[1:2, :])
    const_ref[1] = product(mod[0:1, :])
    for which in range(3):
        push(which).wait()


def prepare(hidden_state, mod_rows, down_weight, chips, width):
    _, rows, model = hidden_state.shape
    channels = down_weight.shape[1]
    head_cols = model // chips
    late = chips * (head_cols - width)
    hbm = pl.BlockSpec(memory_space=pltpu.HBM)
    shapes = [
        ((rows, late), jnp.bfloat16),
        ((3, late), jnp.float32),
        ((late, channels), jnp.bfloat16),
    ]
    return pl.pallas_call(
        functools.partial(prepare_kernel, chips, head_cols, width),
        out_shape=[jax.ShapeDtypeStruct(*shape) for shape in shapes]
        + [jax.ShapeDtypeStruct((2, 8, channels), jnp.float32)],
        in_specs=[hbm] * 3,
        out_specs=[hbm] * 3 + [pl.BlockSpec(memory_space=pltpu.VMEM)],
        scratch_shapes=[
            pltpu.VMEM((8, 128), jnp.float32),
            pltpu.VMEM((3, model), jnp.float32),
            pltpu.VMEM((model, channels), jnp.bfloat16),
        ]
        + [pltpu.VMEM(*shape) for shape in shapes]
        + [pltpu.SemaphoreType.DMA((4, max(chips, 2))), pltpu.SemaphoreType.DMA((3,))],
        cost_estimate=pl.CostEstimate(
            flops=64 * model * channels, bytes_accessed=4 * model * channels, transcendentals=0
        ),
        compiler_params=pltpu.CompilerParams(vmem_limit_bytes=VMEM_BYTES),
        name="prepare",
    )(hidden_state, mod_rows, down_weight)


def early_kernel(chips, head_cols, h_ref, mod_ref, weight_ref, *rest):
    pieces, rest = rest[:chips], rest[chips:]
    acc_ref, centre_ref, square_ref = rest[:3]
    attended, hidden, weight, mod, sem = rest[3:]
    rows, width = pieces[0].shape
    block_rows = 16

    def pull(step, which):
        col = pl.multiple_of(my_chip(step, chips)[1] * head_cols, 128)
        here = pl.ds(step * width, width)
        source, target = (
            (pieces[step], attended.at[:, here]),
            (h_ref.at[0, :, pl.ds(col, width)], hidden.at[:, here]),
            (mod_ref.at[:, pl.ds(col, width)], mod.at[:, here]),
            (weight_ref.at[pl.ds(col, width), :], weight.at[here, :]),
        )[which]
        return pltpu.make_async_copy(source, target, sem.at[which, step])

    for which in range(4):
        for step in range(chips):
            pull(step, which).start()
    for which in range(3):
        for step in range(chips):
            pull(step, which).wait()

    def rows_of(index, carry):
        here = pl.ds(pl.multiple_of(index * block_rows, block_rows), block_rows)
        wide = (
            (
                hidden[here, :].astype(jnp.float32)
                + mod[2:3, :] * attended[here, :].astype(jnp.float32)
            )
            .astype(jnp.bfloat16)
            .astype(jnp.float32)
        )
        centre = jnp.mean(wide, axis=-1, keepdims=True)
        away = wide - centre
        square = jnp.sum(jnp.square(away), axis=-1, keepdims=True)
        attended[here, :] = (away * (1.0 + mod[1:2, :])).astype(jnp.bfloat16)
        centre_ref[here, :] = jnp.broadcast_to(centre, (block_rows, 128))
        square_ref[here, :] = jnp.broadcast_to(square, (block_rows, 128))
        return carry

    lax.fori_loop(0, rows // block_rows, rows_of, 0, unroll=2)
    for step in range(chips):
        pull(step, 3).wait()
    acc_ref[...] = jnp.dot(attended[...], weight[...], preferred_element_type=jnp.float32)


def project_early(hidden_state, mod_rows, down_weight, pieces):
    chips = len(pieces)
    _, rows, model = hidden_state.shape
    channels = down_weight.shape[1]
    width = pieces[0].shape[1]
    return pl.pallas_call(
        functools.partial(early_kernel, chips, model // chips),
        out_shape=[
            jax.ShapeDtypeStruct((rows, channels), jnp.float32),
            jax.ShapeDtypeStruct((rows, 128), jnp.float32),
            jax.ShapeDtypeStruct((rows, 128), jnp.float32),
        ],
        in_specs=[pl.BlockSpec(memory_space=pltpu.HBM)] * (chips + 3),
        out_specs=[pl.BlockSpec(memory_space=pltpu.VMEM)] * 3,
        scratch_shapes=[
            pltpu.VMEM((rows, chips * width), jnp.bfloat16),
            pltpu.VMEM((rows, chips * width), jnp.bfloat16),
            pltpu.VMEM((chips * width, channels), jnp.bfloat16),
            pltpu.VMEM((3, chips * width), jnp.float32),
            pltpu.SemaphoreType.DMA((4, chips)),
        ],
        cost_estimate=pl.CostEstimate(
            flops=2 * rows * chips * width * channels,
            bytes_accessed=4 * rows * model + 2 * model * channels,
            transcendentals=0,
        ),
        compiler_params=pltpu.CompilerParams(vmem_limit_bytes=VMEM_BYTES),
        name="project_early",
    )(hidden_state, mod_rows, down_weight, *pieces)


def late_kernel(count, early, frames_ref, *rest):
    sources, pieces, rest = rest[:7], rest[7 : 7 + count], rest[7 + count :]
    out_ref, attended, held, in_sem, held_sem = rest[0], rest[1], rest[2:9], rest[9], rest[10]
    acc_ref, centre_ref, square_ref, h_ref, mod_ref, weight_ref, const_ref = held
    rows, width = pieces[0].shape
    late = count * width
    model = early + late

    def load(step):
        return pltpu.make_async_copy(
            pieces[step], attended.at[:, pl.ds(step * width, width)], in_sem.at[step]
        )

    def hold(which):
        return pltpu.make_async_copy(sources[which], held[which], held_sem.at[which])

    for step in range(count):
        load(step).start()
    for which in (3, 4, 1, 2, 5, 0, 6):
        hold(which).start()
    for which in (3, 4, 1, 2):
        hold(which).wait()
    for step in range(count):
        load(step).wait()
    wide = (
        (h_ref[...].astype(jnp.float32) + mod_ref[2:3, :] * attended[...].astype(jnp.float32))
        .astype(jnp.bfloat16)
        .astype(jnp.float32)
    )
    first = centre_ref[:, :1]
    scaled = ((wide - first) * (1.0 + mod_ref[1:2, :])).astype(jnp.bfloat16)
    for which in (5, 0, 6):
        hold(which).wait()
    total = acc_ref[...] + jnp.dot(scaled, weight_ref[...], preferred_element_type=jnp.float32)
    own = jnp.mean(wide, axis=-1, keepdims=True)
    square = jnp.sum(jnp.square(wide - own), axis=-1, keepdims=True)
    gap = own - first
    centre = first + gap * (late / model)
    spread = (square_ref[:, :1] + square + gap * gap * (early * late / model)) / model
    total = total + (first - centre) * const_ref[0, :1, :]
    total = total * lax.rsqrt(spread + 1e-06) + const_ref[1, :1, :]
    token = lax.axis_index("ctx") * rows + lax.broadcasted_iota(jnp.int32, (rows, 1), 0)
    out_ref[...] = jnp.where(token < frames_ref[0] * (HH * WW), total, 0.0).astype(out_ref.dtype)


def project_late(frames, early, consts, pieces, count, model):
    rows, width = pieces[0].shape
    channels = consts.shape[-1]
    hbm = pl.BlockSpec(memory_space=pltpu.HBM)
    sources = (*early, consts)
    return pl.pallas_call(
        functools.partial(late_kernel, count, model - count * width),
        out_shape=jax.ShapeDtypeStruct((rows, channels), jnp.bfloat16),
        in_specs=[pl.BlockSpec(memory_space=pltpu.SMEM)] + [hbm] * (7 + count),
        out_specs=pl.BlockSpec(memory_space=pltpu.VMEM),
        scratch_shapes=[pltpu.VMEM((rows, count * width), jnp.bfloat16)]
        + [pltpu.VMEM(source.shape, source.dtype) for source in sources]
        + [pltpu.SemaphoreType.DMA((count,)), pltpu.SemaphoreType.DMA((7,))],
        cost_estimate=pl.CostEstimate(
            flops=2 * rows * count * width * channels,
            bytes_accessed=4 * rows * count * width,
            transcendentals=0,
        ),
        compiler_params=pltpu.CompilerParams(vmem_limit_bytes=VMEM_BYTES),
        name="project_late",
    )(frames, *sources, *pieces)


def gather_taps(frames, taps):
    cells = HH * WW
    channels = frames[0].shape[1]
    column = lax.broadcasted_iota(jnp.int32, (cells, 1), 0) % WW
    blank = jnp.zeros((WW, channels), jnp.float32)
    for number, frame in enumerate(frames):
        wide = frame.astype(jnp.float32)
        for across, offset in enumerate((-1, 0, 1)):
            cell = wide
            if offset:
                inside = (column + offset >= 0) & (column + offset < WW)
                cell = jnp.where(inside, pltpu.roll(wide, (-offset) % cells, 0), 0.0)
            cell = jnp.concatenate([blank, cell, blank], axis=0)
            for down in range(3):
                taps[
                    pl.ds(number * cells, cells), pl.ds((down * 3 + across) * channels, channels)
                ] = cell[down * WW : down * WW + cells].astype(jnp.bfloat16)


def refine_kernel(frames_ref, mid_ref, even_ref, odd_ref, weight_ref, out_ref, held, taps, weight, sem, weight_sem):
    cells = HH * WW
    rows, _ = mid_ref.shape
    me = lax.axis_index("ctx")
    odd = lax.rem(me, 2)
    before, after = rows - cells, rows + cells

    def at(start):
        return pl.ds(pl.multiple_of(start, cells), cells)

    copies = (
        pltpu.make_async_copy(mid_ref, held.at[pl.ds(cells, rows), :], sem.at[0]),
        pltpu.make_async_copy(
            even_ref.at[at(odd * before), :], held.at[at((1 - odd) * after), :], sem.at[1]
        ),
        pltpu.make_async_copy(
            odd_ref.at[at((1 - odd) * before), :], held.at[at(odd * after), :], sem.at[2]
        ),
    )

    def fetch(ahead):
        return pltpu.make_async_copy(weight_ref.at[ahead], weight.at[ahead], weight_sem.at[ahead])

    for copy in copies:
        copy.start()
    for ahead in range(3):
        fetch(ahead).start()
    for copy in copies:
        copy.wait()
    gather_taps(
        [held[pl.ds(start, cells), :] for start in range(0, rows + 2 * cells, cells)], taps
    )
    total = held[pl.ds(cells, rows), :].astype(jnp.float32)
    for ahead in range(3):
        fetch(ahead).wait()
        total = total + jnp.dot(
            taps[pl.ds(ahead * cells, rows), :], weight[ahead], preferred_element_type=jnp.float32
        )
    token = me * rows + lax.broadcasted_iota(jnp.int32, (rows, 1), 0)
    out_ref[0] = jnp.where(token < frames_ref[0] * cells, total, 0.0).astype(out_ref.dtype)


def refine(frames, mid, even, odd, conv_weight):
    rows, channels = mid.shape
    taps = conv_weight.reshape(3, 9 * channels, channels)
    return pl.pallas_call(
        refine_kernel,
        out_shape=jax.ShapeDtypeStruct((1, rows, channels), jnp.bfloat16),
        in_specs=[pl.BlockSpec(memory_space=pltpu.SMEM)]
        + [pl.BlockSpec(memory_space=pltpu.HBM)] * 4,
        out_specs=pl.BlockSpec(memory_space=pltpu.VMEM),
        scratch_shapes=[
            pltpu.VMEM((rows + 2 * HH * WW, channels), jnp.bfloat16),
            pltpu.VMEM((rows + 2 * HH * WW, 9 * channels), jnp.bfloat16),
            pltpu.VMEM(taps.shape, taps.dtype),
            pltpu.SemaphoreType.DMA((3,)),
            pltpu.SemaphoreType.DMA((3,)),
        ],
        cost_estimate=pl.CostEstimate(
            flops=54 * rows * channels * channels,
            bytes_accessed=2 * taps.size + 6 * rows * channels,
            transcendentals=0,
        ),
        compiler_params=pltpu.CompilerParams(vmem_limit_bytes=VMEM_BYTES),
        name="refine",
    )(frames, mid, even, odd, taps)


def clip_orders(sec_count):
    return [
        order
        for order in itertools.permutations(range(sec_count))
        if any(order[(d + sec_count // 2) % sec_count] == d for d in range(sec_count))
    ]


def order_index(destination, sec_count):
    if sec_count > 4:
        return jnp.int32(0)
    orders = clip_orders(sec_count)
    codes = jnp.asarray(
        [sum(d * sec_count**i for i, d in enumerate(order)) for order in orders], jnp.int32
    )
    powers = jnp.asarray([sec_count**i for i in range(sec_count)], jnp.int32)
    code = jnp.sum(destination * powers)
    return jnp.sum(jnp.where(codes == code, jnp.arange(len(orders), dtype=jnp.int32), 0))


def handoff(projected, which, source, sec_count):
    if sec_count <= 4:
        def take(order):
            return lambda value: lax.ppermute(value, "sec", list(enumerate(order)))

        return lax.switch(which, [take(order) for order in clip_orders(sec_count)], projected)
    my_section = lax.axis_index("sec")
    chosen = projected
    for step in range(1, sec_count):
        arrived = lax.ppermute(projected, "sec", ring(step, sec_count))
        chosen = jnp.where(source == partner(my_section, step, sec_count)[1], arrived, chosen)
    return chosen


def body(
    hidden_state,
    queries,
    key_vectors,
    value_vectors,
    modulation,
    down_weight,
    conv_weight,
    clip_frames,
    destination,
    timestep,
):
    my_section = lax.axis_index("sec")
    sec_count = lax.axis_size("sec")
    count = lax.axis_size("ctx")
    chips = count // 2
    model_width = hidden_state.shape[2]
    group = HEADS // chips
    head_size = model_width // HEADS
    head_cols = group * head_size
    chunks = head_chunks(group)
    widths = [heads * head_size for heads in chunks]
    tensors = (queries, key_vectors, value_vectors)
    steps = range(1, chips)

    own, beside = [], []
    for chunk, width in enumerate(widths):
        packed = pack(tensors, chips, head_cols, sum(widths[:chunk]), width)
        beside.append([across(packed[0], chips)])
        own.append([packed[0]] + [send(packed[step], step, chips) for step in steps])
        beside[chunk] += [across(own[chunk][step], chips) for step in steps]

    section_ids = jnp.arange(destination.shape[0], dtype=jnp.int32)
    source = jnp.sum(jnp.where(destination == my_section, section_ids, 0))
    own_frames = lax.dynamic_slice(clip_frames, (my_section,), (1,))
    clip_length = lax.dynamic_slice(clip_frames, (source,), (1,))
    which = order_index(destination, sec_count)
    mod_rows = lax.dynamic_index_in_dim(modulation, timestep[my_section], 0, keepdims=False)
    ready = prepare(hidden_state, mod_rows, down_weight, chips, widths[0])
    own_frames, clip_length, which, mod_rows, ready = lax.optimization_barrier(
        (own_frames, clip_length, which, mod_rows, ready)
    )

    returned = []
    for chunk, heads in enumerate(chunks):
        outs = attend(own_frames, own[chunk], beside[chunk], heads)
        returned.append([outs[0]] + [send(outs[step], step, chips) for step in steps])
    early = project_early(hidden_state, mod_rows, down_weight, returned[0])
    projected = project_late(
        own_frames, (*early, *tuple(ready[:3])), ready[3], returned[1], chips, model_width
    )
    mid = handoff(projected, which, source, sec_count)
    even = lax.ppermute(mid, "ctx", [(i, i ^ 1) for i in range(count)])
    joints = [(i, i + 1) for i in range(1, count - 1, 2)]
    odd = lax.ppermute(mid, "ctx", joints + [(two, one) for one, two in joints])
    return refine(clip_length, mid, even, odd, conv_weight)


def solution(mesh):
    split = P("sec", "ctx", None)
    return jax.shard_map(
        body,
        mesh=mesh,
        in_specs=(split,) * 4 + (P(),) * 6,
        out_specs=split,
        check_vma=False,
    )
```

```python
import functools
import itertools
import math

import jax
import jax.numpy as jnp
from jax import lax
from jax.experimental import pallas as pl
from jax.experimental.pallas import tpu as pltpu
from jax.sharding import PartitionSpec as P


HEADS = 32
VMEM_BYTES = 67043328
HH = 8
WW = 8


def head_chunks(group):
    late = max(1, group // 4)
    return group - late, late


def partner(me, step, count):
    if count & (count - 1) == 0:
        return me ^ step, me ^ step
    return lax.rem(me + step, count), lax.rem(me - step + count, count)


def ring(step, count):
    if count & (count - 1) == 0:
        return [(i, i ^ step) for i in range(count)]
    return [(i, (i + step) % count) for i in range(count)]


def far_first(chips):
    far = list(range(chips - 1, max(chips // 2, 1) - 1, -1))
    return far + list(range(chips // 2 - 1, 0, -1)), far[-1]


def send(value, step, chips):
    pairs = [
        (2 * one + core, 2 * two + core) for one, two in ring(step, chips) for core in range(2)
    ]
    return lax.ppermute(value, "ctx", pairs)


def across(value, chips):
    return lax.ppermute(value, "ctx", [(i, i ^ 1) for i in range(2 * chips)])


def my_chip(step, chips):
    return partner(lax.axis_index("ctx") // 2, step, chips)


def pack_kernel(steps, chips, kinds, head_cols, first_col, width, *rest):
    sources, outs = rest[:kinds], rest[kinds : kinds + len(steps)]
    buf, in_sem, out_sem = rest[kinds + len(steps) :]
    order = range(len(steps))

    def load(step, kind):
        col = pl.multiple_of(my_chip(steps[step], chips)[0] * head_cols + first_col, 128)
        return pltpu.make_async_copy(
            sources[kind].at[0, :, pl.ds(col, width)], buf.at[step, kind], in_sem.at[step, kind]
        )

    def save(step):
        return pltpu.make_async_copy(buf.at[step], outs[step], out_sem.at[step])

    for step in order:
        for kind in range(kinds):
            load(step, kind).start()
    for step in order:
        for kind in range(kinds):
            load(step, kind).wait()
        save(step).start()
    for step in order:
        save(step).wait()


def pack(sources, steps, chips, head_cols, first_col, width):
    rows = sources[0].shape[1]
    kinds = len(sources)
    piece = jax.ShapeDtypeStruct((kinds, rows, width), sources[0].dtype)
    return pl.pallas_call(
        functools.partial(pack_kernel, steps, chips, kinds, head_cols, first_col, width),
        out_shape=[piece] * len(steps),
        in_specs=[pl.BlockSpec(memory_space=pltpu.HBM)] * kinds,
        out_specs=[pl.BlockSpec(memory_space=pltpu.HBM)] * len(steps),
        scratch_shapes=[
            pltpu.VMEM((len(steps), kinds, rows, width), sources[0].dtype),
            pltpu.SemaphoreType.DMA((len(steps), kinds)),
            pltpu.SemaphoreType.DMA((len(steps),)),
        ],
        cost_estimate=pl.CostEstimate(
            flops=0, bytes_accessed=4 * kinds * len(steps) * rows * width, transcendentals=0
        ),
        compiler_params=pltpu.CompilerParams(vmem_limit_bytes=VMEM_BYTES),
        name="pack",
    )(*sources)


def attend_kernel(chips, heads, block_rows, frames_ref, *rest):
    own, beside, outs = rest[:chips], rest[chips : 2 * chips], rest[2 * chips : 3 * chips]
    queries, keys, values, result, in_sem, value_sem, out_sem = rest[3 * chips :]
    core = lax.rem(lax.axis_index("ctx"), 2)
    rows = own[0].shape[1]
    asked = chips * rows
    seq = 2 * asked
    size = own[0].shape[2] // heads
    scale = math.log2(math.e) / math.sqrt(size)
    blocks = asked // block_rows

    def place(step, side):
        device = my_chip(step, chips)[1] * 2 + (core if side == 0 else 1 - core)
        return pl.ds(pl.multiple_of(device * rows, rows), rows)

    def load(step, which):
        if which == 2:
            source, target = own[step].at[0], queries.at[pl.ds(step * rows, rows), :]
        else:
            source, target = (own, beside)[which][step].at[1], keys.at[place(step, which), :]
        return pltpu.make_async_copy(source, target, in_sem.at[which, step])

    def load_values(step, side, head):
        return pltpu.make_async_copy(
            (own, beside)[side][step].at[2, :, pl.ds(head * size, size)],
            values.at[place(step, side), pl.ds(head * 2 * size, size)],
            value_sem.at[side, head, step],
        )

    def save(step):
        return pltpu.make_async_copy(
            result.at[pl.ds(step * rows, rows), :], outs[step], out_sem.at[step]
        )

    for step in range(chips):
        for which in range(3):
            load(step, which).start()
    for head in range(heads):
        for step in range(chips):
            for side in range(2):
                load_values(step, side, head).start()
    for head in range(heads):
        values[:, pl.ds((head * 2 + 1) * size, size)] = jnp.ones((seq, size), jnp.bfloat16)
    valid = frames_ref[0] * (HH * WW)
    places = lax.broadcasted_iota(jnp.int32, (1, seq), 1)
    bias = jnp.where(places < valid, 0.0, -jnp.inf)
    for step in range(chips):
        for which in range(3):
            load(step, which).wait()
    for head in range(heads):
        for step in range(chips):
            for side in range(2):
                load_values(step, side, head).wait()

    def task(index, carry):
        head = index // blocks
        start = pl.multiple_of(lax.rem(index, blocks) * block_rows, block_rows)
        here = pl.ds(start, block_rows)
        lanes = pl.ds(pl.multiple_of(head * size, size), size)
        scores = lax.dot_general(
            queries[here, lanes],
            keys[:, lanes],
            (((1,), (1,)), ((), ())),
            preferred_element_type=jnp.float32,
        )
        scores = scores * scale + bias
        weights = jnp.exp2(scores - jnp.max(scores, axis=1, keepdims=True))
        both = jnp.dot(
            weights.astype(jnp.bfloat16),
            values[:, pl.ds(pl.multiple_of(head * (2 * size), 2 * size), 2 * size)],
            preferred_element_type=jnp.float32,
        )
        result[here, lanes] = (both[:, :size] / both[:, size:]).astype(result.dtype)
        return carry

    lax.fori_loop(0, heads * blocks, task, 0, unroll=4)
    for step in range(chips):
        save(step).start()
    for step in range(chips):
        save(step).wait()


def attend(frames, own, beside, heads):
    chips = len(own)
    _, rows, width = own[0].shape
    asked = chips * rows
    seq = 2 * asked
    block_rows = min(256, asked)
    return pl.pallas_call(
        functools.partial(attend_kernel, chips, heads, block_rows),
        out_shape=[jax.ShapeDtypeStruct((rows, width), jnp.bfloat16)] * chips,
        in_specs=[pl.BlockSpec(memory_space=pltpu.SMEM)]
        + [pl.BlockSpec(memory_space=pltpu.HBM)] * (2 * chips),
        out_specs=[pl.BlockSpec(memory_space=pltpu.HBM)] * chips,
        scratch_shapes=[
            pltpu.VMEM((asked, width), jnp.bfloat16),
            pltpu.VMEM((seq, width), jnp.bfloat16),
            pltpu.VMEM((seq, 2 * width), jnp.bfloat16),
            pltpu.VMEM((asked, width), jnp.bfloat16),
            pltpu.SemaphoreType.DMA((3, chips)),
            pltpu.SemaphoreType.DMA((2, heads, chips)),
            pltpu.SemaphoreType.DMA((chips,)),
        ],
        cost_estimate=pl.CostEstimate(
            flops=6 * asked * seq * width,
            bytes_accessed=8 * seq * width,
            transcendentals=asked * seq * heads,
        ),
        compiler_params=pltpu.CompilerParams(vmem_limit_bytes=VMEM_BYTES),
        name="attend",
    )(frames, *own, *beside)


def prepare_kernel(chips, head_cols, width, h_ref, mod_ref, weight_ref, *rest):
    h_out, mod_out, weight_out, const_ref, _, mod, weight, late_h, late_mod, late_weight, in_sem, out_sem = rest
    late = head_cols - width

    def pull(step, which):
        col = pl.multiple_of(my_chip(step, chips)[1] * head_cols + width, 128)
        here = pl.ds(step * late, late)
        source, target = (
            (h_ref.at[0, :, pl.ds(col, late)], late_h.at[:, here]),
            (mod_ref.at[:, pl.ds(col, late)], late_mod.at[:, here]),
            (weight_ref.at[pl.ds(col, late), :], late_weight.at[here, :]),
        )[which]
        return pltpu.make_async_copy(source, target, in_sem.at[which, step])

    def whole(which):
        source, target = ((mod_ref, mod), (weight_ref, weight))[which]
        return pltpu.make_async_copy(source, target, in_sem.at[3, which])

    def push(which):
        source, target = ((late_h, h_out), (late_mod, mod_out), (late_weight, weight_out))[which]
        return pltpu.make_async_copy(source, target, out_sem.at[which])

    for which in range(3):
        for step in range(chips):
            pull(step, which).start()
    whole(0).start()
    whole(1).start()
    for which in range(3):
        for step in range(chips):
            pull(step, which).wait()
        push(which).start()

    def product(row):
        high = row.astype(jnp.bfloat16)
        low = (row - high.astype(jnp.float32)).astype(jnp.bfloat16)
        split = jnp.concatenate(
            [jnp.broadcast_to(high, (8,) + high.shape[1:]), jnp.broadcast_to(low, (8,) + low.shape[1:])],
            axis=0,
        )
        both = jnp.dot(split, weight[...], preferred_element_type=jnp.float32)
        return both[:8] + both[8:]

    whole(0).wait()
    whole(1).wait()
    const_ref[0] = product(1.0 + mod[1:2, :])
    const_ref[1] = product(mod[0:1, :])
    for which in range(3):
        push(which).wait()


def prepare(hidden_state, mod_rows, down_weight, chips, width):
    _, rows, model = hidden_state.shape
    channels = down_weight.shape[1]
    head_cols = model // chips
    late = chips * (head_cols - width)
    hbm = pl.BlockSpec(memory_space=pltpu.HBM)
    shapes = [
        ((rows, late), jnp.bfloat16),
        ((3, late), jnp.float32),
        ((late, channels), jnp.bfloat16),
    ]
    return pl.pallas_call(
        functools.partial(prepare_kernel, chips, head_cols, width),
        out_shape=[jax.ShapeDtypeStruct(*shape) for shape in shapes]
        + [jax.ShapeDtypeStruct((2, 8, channels), jnp.float32)],
        in_specs=[hbm] * 3,
        out_specs=[hbm] * 3 + [pl.BlockSpec(memory_space=pltpu.VMEM)],
        scratch_shapes=[
            pltpu.VMEM((8, 128), jnp.float32),
            pltpu.VMEM((3, model), jnp.float32),
            pltpu.VMEM((model, channels), jnp.bfloat16),
        ]
        + [pltpu.VMEM(*shape) for shape in shapes]
        + [pltpu.SemaphoreType.DMA((4, max(chips, 2))), pltpu.SemaphoreType.DMA((3,))],
        cost_estimate=pl.CostEstimate(
            flops=64 * model * channels, bytes_accessed=4 * model * channels, transcendentals=0
        ),
        compiler_params=pltpu.CompilerParams(vmem_limit_bytes=VMEM_BYTES),
        name="prepare",
    )(hidden_state, mod_rows, down_weight)


def early_kernel(chips, head_cols, h_ref, mod_ref, weight_ref, *rest):
    pieces, rest = rest[:chips], rest[chips:]
    acc_ref, centre_ref, square_ref = rest[:3]
    attended, hidden, weight, mod, sem = rest[3:]
    rows, width = pieces[0].shape
    block_rows = 16

    def pull(step, which):
        col = pl.multiple_of(my_chip(step, chips)[1] * head_cols, 128)
        here = pl.ds(step * width, width)
        source, target = (
            (pieces[step], attended.at[:, here]),
            (h_ref.at[0, :, pl.ds(col, width)], hidden.at[:, here]),
            (mod_ref.at[:, pl.ds(col, width)], mod.at[:, here]),
            (weight_ref.at[pl.ds(col, width), :], weight.at[here, :]),
        )[which]
        return pltpu.make_async_copy(source, target, sem.at[which, step])

    for which in range(4):
        for step in range(chips):
            pull(step, which).start()
    for which in range(3):
        for step in range(chips):
            pull(step, which).wait()

    def rows_of(index, carry):
        here = pl.ds(pl.multiple_of(index * block_rows, block_rows), block_rows)
        wide = (
            (
                hidden[here, :].astype(jnp.float32)
                + mod[2:3, :] * attended[here, :].astype(jnp.float32)
            )
            .astype(jnp.bfloat16)
            .astype(jnp.float32)
        )
        centre = jnp.mean(wide, axis=-1, keepdims=True)
        away = wide - centre
        square = jnp.sum(jnp.square(away), axis=-1, keepdims=True)
        attended[here, :] = (away * (1.0 + mod[1:2, :])).astype(jnp.bfloat16)
        centre_ref[here, :] = jnp.broadcast_to(centre, (block_rows, 128))
        square_ref[here, :] = jnp.broadcast_to(square, (block_rows, 128))
        return carry

    lax.fori_loop(0, rows // block_rows, rows_of, 0, unroll=2)
    for step in range(chips):
        pull(step, 3).wait()
    acc_ref[...] = jnp.dot(attended[...], weight[...], preferred_element_type=jnp.float32)


def project_early(hidden_state, mod_rows, down_weight, pieces):
    chips = len(pieces)
    _, rows, model = hidden_state.shape
    channels = down_weight.shape[1]
    width = pieces[0].shape[1]
    return pl.pallas_call(
        functools.partial(early_kernel, chips, model // chips),
        out_shape=[
            jax.ShapeDtypeStruct((rows, channels), jnp.float32),
            jax.ShapeDtypeStruct((rows, 128), jnp.float32),
            jax.ShapeDtypeStruct((rows, 128), jnp.float32),
        ],
        in_specs=[pl.BlockSpec(memory_space=pltpu.HBM)] * (chips + 3),
        out_specs=[pl.BlockSpec(memory_space=pltpu.VMEM)] * 3,
        scratch_shapes=[
            pltpu.VMEM((rows, chips * width), jnp.bfloat16),
            pltpu.VMEM((rows, chips * width), jnp.bfloat16),
            pltpu.VMEM((chips * width, channels), jnp.bfloat16),
            pltpu.VMEM((3, chips * width), jnp.float32),
            pltpu.SemaphoreType.DMA((4, chips)),
        ],
        cost_estimate=pl.CostEstimate(
            flops=2 * rows * chips * width * channels,
            bytes_accessed=4 * rows * model + 2 * model * channels,
            transcendentals=0,
        ),
        compiler_params=pltpu.CompilerParams(vmem_limit_bytes=VMEM_BYTES),
        name="project_early",
    )(hidden_state, mod_rows, down_weight, *pieces)


def late_kernel(count, early, frames_ref, *rest):
    sources, pieces, rest = rest[:7], rest[7 : 7 + count], rest[7 + count :]
    out_ref, attended, held, in_sem, held_sem = rest[0], rest[1], rest[2:9], rest[9], rest[10]
    acc_ref, centre_ref, square_ref, h_ref, mod_ref, weight_ref, const_ref = held
    rows, width = pieces[0].shape
    late = count * width
    model = early + late

    def load(step):
        return pltpu.make_async_copy(
            pieces[step], attended.at[:, pl.ds(step * width, width)], in_sem.at[step]
        )

    def hold(which):
        return pltpu.make_async_copy(sources[which], held[which], held_sem.at[which])

    for step in range(count):
        load(step).start()
    for which in (3, 4, 1, 2, 5, 0, 6):
        hold(which).start()
    for which in (3, 4, 1, 2):
        hold(which).wait()
    for step in range(count):
        load(step).wait()
    wide = (
        (h_ref[...].astype(jnp.float32) + mod_ref[2:3, :] * attended[...].astype(jnp.float32))
        .astype(jnp.bfloat16)
        .astype(jnp.float32)
    )
    first = centre_ref[:, :1]
    scaled = ((wide - first) * (1.0 + mod_ref[1:2, :])).astype(jnp.bfloat16)
    for which in (5, 0, 6):
        hold(which).wait()
    total = acc_ref[...] + jnp.dot(scaled, weight_ref[...], preferred_element_type=jnp.float32)
    own = jnp.mean(wide, axis=-1, keepdims=True)
    square = jnp.sum(jnp.square(wide - own), axis=-1, keepdims=True)
    gap = own - first
    centre = first + gap * (late / model)
    spread = (square_ref[:, :1] + square + gap * gap * (early * late / model)) / model
    total = total + (first - centre) * const_ref[0, :1, :]
    total = total * lax.rsqrt(spread + 1e-06) + const_ref[1, :1, :]
    token = lax.axis_index("ctx") * rows + lax.broadcasted_iota(jnp.int32, (rows, 1), 0)
    out_ref[...] = jnp.where(token < frames_ref[0] * (HH * WW), total, 0.0).astype(out_ref.dtype)


def project_late(frames, early, consts, pieces, count, model):
    rows, width = pieces[0].shape
    channels = consts.shape[-1]
    hbm = pl.BlockSpec(memory_space=pltpu.HBM)
    sources = (*early, consts)
    return pl.pallas_call(
        functools.partial(late_kernel, count, model - count * width),
        out_shape=jax.ShapeDtypeStruct((rows, channels), jnp.bfloat16),
        in_specs=[pl.BlockSpec(memory_space=pltpu.SMEM)] + [hbm] * (7 + count),
        out_specs=pl.BlockSpec(memory_space=pltpu.VMEM),
        scratch_shapes=[pltpu.VMEM((rows, count * width), jnp.bfloat16)]
        + [pltpu.VMEM(source.shape, source.dtype) for source in sources]
        + [pltpu.SemaphoreType.DMA((count,)), pltpu.SemaphoreType.DMA((7,))],
        cost_estimate=pl.CostEstimate(
            flops=2 * rows * count * width * channels,
            bytes_accessed=4 * rows * count * width,
            transcendentals=0,
        ),
        compiler_params=pltpu.CompilerParams(vmem_limit_bytes=VMEM_BYTES),
        name="project_late",
    )(frames, *sources, *pieces)


def gather_taps(frames, taps):
    cells = HH * WW
    channels = frames[0].shape[1]
    column = lax.broadcasted_iota(jnp.int32, (cells, 1), 0) % WW
    blank = jnp.zeros((WW, channels), jnp.float32)
    for number, frame in enumerate(frames):
        wide = frame.astype(jnp.float32)
        for across, offset in enumerate((-1, 0, 1)):
            cell = wide
            if offset:
                inside = (column + offset >= 0) & (column + offset < WW)
                cell = jnp.where(inside, pltpu.roll(wide, (-offset) % cells, 0), 0.0)
            cell = jnp.concatenate([blank, cell, blank], axis=0)
            for down in range(3):
                taps[
                    pl.ds(number * cells, cells), pl.ds((down * 3 + across) * channels, channels)
                ] = cell[down * WW : down * WW + cells].astype(jnp.bfloat16)


def refine_kernel(frames_ref, mid_ref, even_ref, odd_ref, weight_ref, out_ref, held, taps, weight, sem, weight_sem):
    cells = HH * WW
    rows, _ = mid_ref.shape
    me = lax.axis_index("ctx")
    odd = lax.rem(me, 2)
    before, after = rows - cells, rows + cells

    def at(start):
        return pl.ds(pl.multiple_of(start, cells), cells)

    copies = (
        pltpu.make_async_copy(mid_ref, held.at[pl.ds(cells, rows), :], sem.at[0]),
        pltpu.make_async_copy(
            even_ref.at[at(odd * before), :], held.at[at((1 - odd) * after), :], sem.at[1]
        ),
        pltpu.make_async_copy(
            odd_ref.at[at((1 - odd) * before), :], held.at[at(odd * after), :], sem.at[2]
        ),
    )

    def fetch(ahead):
        return pltpu.make_async_copy(weight_ref.at[ahead], weight.at[ahead], weight_sem.at[ahead])

    for copy in copies:
        copy.start()
    for ahead in range(3):
        fetch(ahead).start()
    for copy in copies:
        copy.wait()
    gather_taps(
        [held[pl.ds(start, cells), :] for start in range(0, rows + 2 * cells, cells)], taps
    )
    total = held[pl.ds(cells, rows), :].astype(jnp.float32)
    for ahead in range(3):
        fetch(ahead).wait()
        total = total + jnp.dot(
            taps[pl.ds(ahead * cells, rows), :], weight[ahead], preferred_element_type=jnp.float32
        )
    token = me * rows + lax.broadcasted_iota(jnp.int32, (rows, 1), 0)
    out_ref[0] = jnp.where(token < frames_ref[0] * cells, total, 0.0).astype(out_ref.dtype)


def refine(frames, mid, even, odd, conv_weight):
    rows, channels = mid.shape
    taps = conv_weight.reshape(3, 9 * channels, channels)
    return pl.pallas_call(
        refine_kernel,
        out_shape=jax.ShapeDtypeStruct((1, rows, channels), jnp.bfloat16),
        in_specs=[pl.BlockSpec(memory_space=pltpu.SMEM)]
        + [pl.BlockSpec(memory_space=pltpu.HBM)] * 4,
        out_specs=pl.BlockSpec(memory_space=pltpu.VMEM),
        scratch_shapes=[
            pltpu.VMEM((rows + 2 * HH * WW, channels), jnp.bfloat16),
            pltpu.VMEM((rows + 2 * HH * WW, 9 * channels), jnp.bfloat16),
            pltpu.VMEM(taps.shape, taps.dtype),
            pltpu.SemaphoreType.DMA((3,)),
            pltpu.SemaphoreType.DMA((3,)),
        ],
        cost_estimate=pl.CostEstimate(
            flops=54 * rows * channels * channels,
            bytes_accessed=2 * taps.size + 6 * rows * channels,
            transcendentals=0,
        ),
        compiler_params=pltpu.CompilerParams(vmem_limit_bytes=VMEM_BYTES),
        name="refine",
    )(frames, mid, even, odd, taps)


def clip_orders(sec_count):
    return [
        order
        for order in itertools.permutations(range(sec_count))
        if any(order[(d + sec_count // 2) % sec_count] == d for d in range(sec_count))
    ]


def order_index(destination, sec_count):
    if sec_count > 4:
        return jnp.int32(0)
    orders = clip_orders(sec_count)
    codes = jnp.asarray(
        [sum(d * sec_count**i for i, d in enumerate(order)) for order in orders], jnp.int32
    )
    powers = jnp.asarray([sec_count**i for i in range(sec_count)], jnp.int32)
    code = jnp.sum(destination * powers)
    return jnp.sum(jnp.where(codes == code, jnp.arange(len(orders), dtype=jnp.int32), 0))


def handoff(projected, which, source, sec_count):
    if sec_count <= 4:
        def take(order):
            return lambda value: lax.ppermute(value, "sec", list(enumerate(order)))

        return lax.switch(which, [take(order) for order in clip_orders(sec_count)], projected)
    my_section = lax.axis_index("sec")
    chosen = projected
    for step in range(1, sec_count):
        arrived = lax.ppermute(projected, "sec", ring(step, sec_count))
        chosen = jnp.where(source == partner(my_section, step, sec_count)[1], arrived, chosen)
    return chosen


def body(
    hidden_state,
    queries,
    key_vectors,
    value_vectors,
    modulation,
    down_weight,
    conv_weight,
    clip_frames,
    destination,
    timestep,
):
    my_section = lax.axis_index("sec")
    sec_count = lax.axis_size("sec")
    count = lax.axis_size("ctx")
    chips = count // 2
    model_width = hidden_state.shape[2]
    group = HEADS // chips
    head_size = model_width // HEADS
    head_cols = group * head_size
    chunks = head_chunks(group)
    widths = [heads * head_size for heads in chunks]
    tensors = (queries, key_vectors, value_vectors)
    steps = range(1, chips)

    own, beside = [], []
    for chunk, width in enumerate(widths):
        packed = [None] * chips
        order = far_first(chips)[0]
        for batch in (order[:1], order[1:] + [0]) if chunk == 0 else (order + [0],):
            pieces = pack(tensors, batch, chips, head_cols, sum(widths[:chunk]), width)
            for step, piece in zip(batch, pieces):
                packed[step] = piece
        beside.append([across(packed[0], chips)])
        own.append([packed[0]] + [send(packed[step], step, chips) for step in steps])
        beside[chunk] += [across(own[chunk][step], chips) for step in steps]

    section_ids = jnp.arange(destination.shape[0], dtype=jnp.int32)
    source = jnp.sum(jnp.where(destination == my_section, section_ids, 0))
    own_frames = lax.dynamic_slice(clip_frames, (my_section,), (1,))
    clip_length = lax.dynamic_slice(clip_frames, (source,), (1,))
    which = order_index(destination, sec_count)
    mod_rows = lax.dynamic_index_in_dim(modulation, timestep[my_section], 0, keepdims=False)
    ready = prepare(hidden_state, mod_rows, down_weight, chips, widths[0])
    own_frames, clip_length, which, mod_rows, ready = lax.optimization_barrier(
        (own_frames, clip_length, which, mod_rows, ready)
    )

    returned = []
    for chunk, heads in enumerate(chunks):
        outs = attend(own_frames, own[chunk], beside[chunk], heads)
        returned.append([outs[0]] + [send(outs[step], step, chips) for step in steps])
    early = project_early(hidden_state, mod_rows, down_weight, returned[0])
    projected = project_late(
        own_frames, (*early, *tuple(ready[:3])), ready[3], returned[1], chips, model_width
    )
    mid = handoff(projected, which, source, sec_count)
    even = lax.ppermute(mid, "ctx", [(i, i ^ 1) for i in range(count)])
    joints = [(i, i + 1) for i in range(1, count - 1, 2)]
    odd = lax.ppermute(mid, "ctx", joints + [(two, one) for one, two in joints])
    return refine(clip_length, mid, even, odd, conv_weight)


def solution(mesh):
    split = P("sec", "ctx", None)
    return jax.shard_map(
        body,
        mesh=mesh,
        in_specs=(split,) * 4 + (P(),) * 6,
        out_specs=split,
        check_vma=False,
    )
```

```python
import functools
import itertools
import math

import jax
import jax.numpy as jnp
from jax import lax
from jax.experimental import pallas as pl
from jax.experimental.pallas import tpu as pltpu
from jax.sharding import PartitionSpec as P


HEADS = 32
VMEM_BYTES = 67043328
SPARE_BYTES = 128 * 1024
HH = 8
WW = 8


def head_chunks(group):
    late = max(1, group // 4)
    return group - late, late


def partner(me, step, count):
    if count & (count - 1) == 0:
        return me ^ step, me ^ step
    return lax.rem(me + step, count), lax.rem(me - step + count, count)


def ring(step, count):
    if count & (count - 1) == 0:
        return [(i, i ^ step) for i in range(count)]
    return [(i, (i + step) % count) for i in range(count)]


def far_first(chips):
    far = list(range(chips - 1, max(chips // 2, 1) - 1, -1))
    return far + list(range(chips // 2 - 1, 0, -1)), far[-1]


def send(value, step, chips):
    pairs = [
        (2 * one + core, 2 * two + core) for one, two in ring(step, chips) for core in range(2)
    ]
    return lax.ppermute(value, "ctx", pairs)


def across(value, chips):
    return lax.ppermute(value, "ctx", [(i, i ^ 1) for i in range(2 * chips)])


def my_chip(step, chips):
    return partner(lax.axis_index("ctx") // 2, step, chips)


def pack_kernel(steps, chips, kinds, head_cols, first_col, width, *rest):
    sources, outs = rest[:kinds], rest[kinds : kinds + len(steps)]
    buf, in_sem, out_sem = rest[kinds + len(steps) :]
    order = range(len(steps))

    def load(step, kind):
        col = pl.multiple_of(my_chip(steps[step], chips)[0] * head_cols + first_col, 128)
        return pltpu.make_async_copy(
            sources[kind].at[0, :, pl.ds(col, width)], buf.at[step, kind], in_sem.at[step, kind]
        )

    def save(step):
        return pltpu.make_async_copy(buf.at[step], outs[step], out_sem.at[step])

    for step in order:
        for kind in range(kinds):
            load(step, kind).start()
    for step in order:
        for kind in range(kinds):
            load(step, kind).wait()
        save(step).start()
    for step in order:
        save(step).wait()


def pack(sources, steps, chips, head_cols, first_col, width):
    rows = sources[0].shape[1]
    kinds = len(sources)
    piece = jax.ShapeDtypeStruct((kinds, rows, width), sources[0].dtype)
    return pl.pallas_call(
        functools.partial(pack_kernel, steps, chips, kinds, head_cols, first_col, width),
        out_shape=[piece] * len(steps),
        in_specs=[pl.BlockSpec(memory_space=pltpu.HBM)] * kinds,
        out_specs=[pl.BlockSpec(memory_space=pltpu.HBM)] * len(steps),
        scratch_shapes=[
            pltpu.VMEM((len(steps), kinds, rows, width), sources[0].dtype),
            pltpu.SemaphoreType.DMA((len(steps), kinds)),
            pltpu.SemaphoreType.DMA((len(steps),)),
        ],
        cost_estimate=pl.CostEstimate(
            flops=0, bytes_accessed=4 * kinds * len(steps) * rows * width, transcendentals=0
        ),
        compiler_params=pltpu.CompilerParams(vmem_limit_bytes=VMEM_BYTES),
        name="pack",
    )(*sources)


def attend_kernel(chips, heads, block_rows, frames_ref, *rest):
    own, beside, outs = rest[:chips], rest[chips : 2 * chips], rest[2 * chips : 3 * chips]
    queries, keys, values, result, in_sem, value_sem, out_sem = rest[3 * chips :]
    core = lax.rem(lax.axis_index("ctx"), 2)
    rows = own[0].shape[1]
    asked = chips * rows
    seq = 2 * asked
    size = own[0].shape[2] // heads
    scale = math.log2(math.e) / math.sqrt(size)
    blocks = asked // block_rows

    def place(step, side):
        device = my_chip(step, chips)[1] * 2 + (core if side == 0 else 1 - core)
        return pl.ds(pl.multiple_of(device * rows, rows), rows)

    def load(step, which):
        if which == 2:
            source, target = own[step].at[0], queries.at[pl.ds(step * rows, rows), :]
        else:
            source, target = (own, beside)[which][step].at[1], keys.at[place(step, which), :]
        return pltpu.make_async_copy(source, target, in_sem.at[which, step])

    def load_values(step, side, head):
        return pltpu.make_async_copy(
            (own, beside)[side][step].at[2, :, pl.ds(head * size, size)],
            values.at[place(step, side), pl.ds(head * 2 * size, size)],
            value_sem.at[side, head, step],
        )

    def save(step):
        return pltpu.make_async_copy(
            result.at[pl.ds(step * rows, rows), :], outs[step], out_sem.at[step]
        )

    for step in range(chips):
        for which in range(3):
            load(step, which).start()
    for head in range(heads):
        for step in range(chips):
            for side in range(2):
                load_values(step, side, head).start()
    for head in range(heads):
        values[:, pl.ds((head * 2 + 1) * size, size)] = jnp.ones((seq, size), jnp.bfloat16)
    valid = frames_ref[0] * (HH * WW)
    places = lax.broadcasted_iota(jnp.int32, (1, seq), 1)
    bias = jnp.where(places < valid, 0.0, -jnp.inf)
    for step in range(chips):
        for which in range(3):
            load(step, which).wait()
    for head in range(heads):
        for step in range(chips):
            for side in range(2):
                load_values(step, side, head).wait()

    def task(index, carry):
        head = index // blocks
        start = pl.multiple_of(lax.rem(index, blocks) * block_rows, block_rows)
        here = pl.ds(start, block_rows)
        lanes = pl.ds(pl.multiple_of(head * size, size), size)
        scores = lax.dot_general(
            queries[here, lanes],
            keys[:, lanes],
            (((1,), (1,)), ((), ())),
            preferred_element_type=jnp.float32,
        )
        scores = scores * scale + bias
        weights = jnp.exp2(scores - jnp.max(scores, axis=1, keepdims=True))
        both = jnp.dot(
            weights.astype(jnp.bfloat16),
            values[:, pl.ds(pl.multiple_of(head * (2 * size), 2 * size), 2 * size)],
            preferred_element_type=jnp.float32,
        )
        result[here, lanes] = (both[:, :size] / both[:, size:]).astype(result.dtype)
        return carry

    lax.fori_loop(0, heads * blocks, task, 0, unroll=4)
    for step in range(chips):
        save(step).start()
    for step in range(chips):
        save(step).wait()


def attend(frames, own, beside, heads):
    chips = len(own)
    _, rows, width = own[0].shape
    asked = chips * rows
    seq = 2 * asked
    block_rows = min(256, asked)
    return pl.pallas_call(
        functools.partial(attend_kernel, chips, heads, block_rows),
        out_shape=[jax.ShapeDtypeStruct((rows, width), jnp.bfloat16)] * chips,
        in_specs=[pl.BlockSpec(memory_space=pltpu.SMEM)]
        + [pl.BlockSpec(memory_space=pltpu.HBM)] * (2 * chips),
        out_specs=[pl.BlockSpec(memory_space=pltpu.HBM)] * chips,
        scratch_shapes=[
            pltpu.VMEM((asked, width), jnp.bfloat16),
            pltpu.VMEM((seq, width), jnp.bfloat16),
            pltpu.VMEM((seq, 2 * width), jnp.bfloat16),
            pltpu.VMEM((asked, width), jnp.bfloat16),
            pltpu.SemaphoreType.DMA((3, chips)),
            pltpu.SemaphoreType.DMA((2, heads, chips)),
            pltpu.SemaphoreType.DMA((chips,)),
        ],
        cost_estimate=pl.CostEstimate(
            flops=6 * asked * seq * width,
            bytes_accessed=8 * seq * width,
            transcendentals=asked * seq * heads,
        ),
        compiler_params=pltpu.CompilerParams(vmem_limit_bytes=VMEM_BYTES),
        name="attend",
    )(frames, *own, *beside)


def prepare_kernel(chips, head_cols, width, h_ref, mod_ref, weight_ref, *rest):
    h_out, mod_out, weight_out, const_ref, _, mod, weight, late_h, late_mod, late_weight, in_sem, out_sem = rest
    late = head_cols - width

    def pull(step, which):
        col = pl.multiple_of(my_chip(step, chips)[1] * head_cols + width, 128)
        here = pl.ds(step * late, late)
        source, target = (
            (h_ref.at[0, :, pl.ds(col, late)], late_h.at[:, here]),
            (mod_ref.at[:, pl.ds(col, late)], late_mod.at[:, here]),
            (weight_ref.at[pl.ds(col, late), :], late_weight.at[here, :]),
        )[which]
        return pltpu.make_async_copy(source, target, in_sem.at[which, step])

    def whole(which):
        source, target = ((mod_ref, mod), (weight_ref, weight))[which]
        return pltpu.make_async_copy(source, target, in_sem.at[3, which])

    def push(which):
        source, target = ((late_h, h_out), (late_mod, mod_out), (late_weight, weight_out))[which]
        return pltpu.make_async_copy(source, target, out_sem.at[which])

    for which in range(3):
        for step in range(chips):
            pull(step, which).start()
    whole(0).start()
    whole(1).start()
    for which in range(3):
        for step in range(chips):
            pull(step, which).wait()
        push(which).start()

    def product(row):
        high = row.astype(jnp.bfloat16)
        low = (row - high.astype(jnp.float32)).astype(jnp.bfloat16)
        split = jnp.concatenate(
            [jnp.broadcast_to(high, (8,) + high.shape[1:]), jnp.broadcast_to(low, (8,) + low.shape[1:])],
            axis=0,
        )
        both = jnp.dot(split, weight[...], preferred_element_type=jnp.float32)
        return both[:8] + both[8:]

    whole(0).wait()
    whole(1).wait()
    const_ref[0] = product(1.0 + mod[1:2, :])
    const_ref[1] = product(mod[0:1, :])
    for which in range(3):
        push(which).wait()


def prepare(hidden_state, mod_rows, down_weight, chips, width):
    _, rows, model = hidden_state.shape
    channels = down_weight.shape[1]
    head_cols = model // chips
    late = chips * (head_cols - width)
    hbm = pl.BlockSpec(memory_space=pltpu.HBM)
    shapes = [
        ((rows, late), jnp.bfloat16),
        ((3, late), jnp.float32),
        ((late, channels), jnp.bfloat16),
    ]
    return pl.pallas_call(
        functools.partial(prepare_kernel, chips, head_cols, width),
        out_shape=[jax.ShapeDtypeStruct(*shape) for shape in shapes]
        + [jax.ShapeDtypeStruct((2, 8, channels), jnp.float32)],
        in_specs=[hbm] * 3,
        out_specs=[hbm] * 3 + [pl.BlockSpec(memory_space=pltpu.VMEM)],
        scratch_shapes=[
            pltpu.VMEM((8, 128), jnp.float32),
            pltpu.VMEM((3, model), jnp.float32),
            pltpu.VMEM((model, channels), jnp.bfloat16),
        ]
        + [pltpu.VMEM(*shape) for shape in shapes]
        + [pltpu.SemaphoreType.DMA((4, max(chips, 2))), pltpu.SemaphoreType.DMA((3,))],
        cost_estimate=pl.CostEstimate(
            flops=64 * model * channels, bytes_accessed=4 * model * channels, transcendentals=0
        ),
        compiler_params=pltpu.CompilerParams(vmem_limit_bytes=VMEM_BYTES),
        name="prepare",
    )(hidden_state, mod_rows, down_weight)


def share(rows, channels, later):
    kept = sum(array.size * array.dtype.itemsize for array in later)
    return VMEM_BYTES - kept - 4 * rows * (channels + 256) - SPARE_BYTES


def early_kernel(chips, head_cols, h_ref, mod_ref, weight_ref, *rest):
    pieces, later, rest = rest[:chips], rest[chips : chips + 5], rest[chips + 5 :]
    acc_ref, centre_ref, square_ref = rest[:3]
    kept, (attended, hidden, weight, mod, sem, keep_sem) = rest[3:8], rest[8:]
    rows, width = pieces[0].shape
    block_rows = 16

    def pull(step, which):
        col = pl.multiple_of(my_chip(step, chips)[1] * head_cols, 128)
        here = pl.ds(step * width, width)
        source, target = (
            (pieces[step], attended.at[:, here]),
            (h_ref.at[0, :, pl.ds(col, width)], hidden.at[:, here]),
            (mod_ref.at[:, pl.ds(col, width)], mod.at[:, here]),
            (weight_ref.at[pl.ds(col, width), :], weight.at[here, :]),
        )[which]
        return pltpu.make_async_copy(source, target, sem.at[which, step])

    def keep(which):
        return pltpu.make_async_copy(later[which], kept[which], keep_sem.at[which])

    for which in range(4):
        for step in range(chips):
            pull(step, which).start()
    for which in range(5):
        keep(which).start()
    for which in range(3):
        for step in range(chips):
            pull(step, which).wait()

    def rows_of(index, carry):
        here = pl.ds(pl.multiple_of(index * block_rows, block_rows), block_rows)
        wide = (
            (
                hidden[here, :].astype(jnp.float32)
                + mod[2:3, :] * attended[here, :].astype(jnp.float32)
            )
            .astype(jnp.bfloat16)
            .astype(jnp.float32)
        )
        centre = jnp.mean(wide, axis=-1, keepdims=True)
        away = wide - centre
        square = jnp.sum(jnp.square(away), axis=-1, keepdims=True)
        attended[here, :] = (away * (1.0 + mod[1:2, :])).astype(jnp.bfloat16)
        centre_ref[here, :] = jnp.broadcast_to(centre, (block_rows, 128))
        square_ref[here, :] = jnp.broadcast_to(square, (block_rows, 128))
        return carry

    lax.fori_loop(0, rows // block_rows, rows_of, 0, unroll=4)
    for step in range(chips):
        pull(step, 3).wait()
    acc_ref[...] = jnp.dot(attended[...], weight[...], preferred_element_type=jnp.float32)
    for which in range(5):
        keep(which).wait()


def project_early(hidden_state, mod_rows, down_weight, pieces, later):
    chips = len(pieces)
    _, rows, model = hidden_state.shape
    channels = down_weight.shape[1]
    width = pieces[0].shape[1]
    return pl.pallas_call(
        functools.partial(early_kernel, chips, model // chips),
        out_shape=[
            pltpu.VMEM((rows, channels), jnp.float32),
            pltpu.VMEM((rows, 128), jnp.float32),
            pltpu.VMEM((rows, 128), jnp.float32),
        ]
        + [pltpu.VMEM(array.shape, array.dtype) for array in later],
        in_specs=[pl.BlockSpec(memory_space=pltpu.HBM)] * (chips + 8),
        out_specs=[pl.BlockSpec(memory_space=pltpu.VMEM)] * 8,
        scratch_shapes=[
            pltpu.VMEM((rows, chips * width), jnp.bfloat16),
            pltpu.VMEM((rows, chips * width), jnp.bfloat16),
            pltpu.VMEM((chips * width, channels), jnp.bfloat16),
            pltpu.VMEM((3, chips * width), jnp.float32),
            pltpu.SemaphoreType.DMA((4, chips)),
            pltpu.SemaphoreType.DMA((5,)),
        ],
        cost_estimate=pl.CostEstimate(
            flops=2 * rows * chips * width * channels,
            bytes_accessed=4 * rows * model + 2 * model * channels,
            transcendentals=0,
        ),
        compiler_params=pltpu.CompilerParams(vmem_limit_bytes=share(rows, channels, later)),
        name="project_early",
    )(hidden_state, mod_rows, down_weight, *pieces, *later)


def late_kernel(count, early, frames_ref, *rest):
    held, pieces, (out_ref, attended, in_sem) = rest[:7], rest[7 : 7 + count], rest[7 + count :]
    acc_ref, centre_ref, square_ref, h_ref, mod_ref, weight_ref, const_ref = held
    rows, width = pieces[0].shape
    late = count * width
    model = early + late

    def load(step):
        return pltpu.make_async_copy(
            pieces[step], attended.at[:, pl.ds(step * width, width)], in_sem.at[step]
        )

    for step in range(count):
        load(step).start()
    for step in range(count):
        load(step).wait()
    wide = (
        (h_ref[...].astype(jnp.float32) + mod_ref[2:3, :] * attended[...].astype(jnp.float32))
        .astype(jnp.bfloat16)
        .astype(jnp.float32)
    )
    first = centre_ref[:, :1]
    scaled = ((wide - first) * (1.0 + mod_ref[1:2, :])).astype(jnp.bfloat16)
    total = acc_ref[...] + jnp.dot(scaled, weight_ref[...], preferred_element_type=jnp.float32)
    own = jnp.mean(wide, axis=-1, keepdims=True)
    square = jnp.sum(jnp.square(wide - own), axis=-1, keepdims=True)
    gap = own - first
    centre = first + gap * (late / model)
    spread = (square_ref[:, :1] + square + gap * gap * (early * late / model)) / model
    total = total + (first - centre) * const_ref[0, :1, :]
    total = total * lax.rsqrt(spread + 1e-06) + const_ref[1, :1, :]
    token = lax.axis_index("ctx") * rows + lax.broadcasted_iota(jnp.int32, (rows, 1), 0)
    out_ref[...] = jnp.where(token < frames_ref[0] * (HH * WW), total, 0.0).astype(out_ref.dtype)


def project_late(frames, held, pieces, model, limit):
    count = len(pieces)
    rows, width = pieces[0].shape
    channels = held[0].shape[1]
    return pl.pallas_call(
        functools.partial(late_kernel, count, model - count * width),
        out_shape=jax.ShapeDtypeStruct((rows, channels), jnp.bfloat16),
        in_specs=[pl.BlockSpec(memory_space=pltpu.SMEM)]
        + [pl.BlockSpec(memory_space=pltpu.VMEM)] * 7
        + [pl.BlockSpec(memory_space=pltpu.HBM)] * count,
        out_specs=pl.BlockSpec(memory_space=pltpu.VMEM),
        scratch_shapes=[
            pltpu.VMEM((rows, count * width), jnp.bfloat16),
            pltpu.SemaphoreType.DMA((count,)),
        ],
        cost_estimate=pl.CostEstimate(
            flops=2 * rows * count * width * channels,
            bytes_accessed=4 * rows * count * width,
            transcendentals=0,
        ),
        compiler_params=pltpu.CompilerParams(vmem_limit_bytes=limit),
        name="project_late",
    )(frames, *[pltpu.with_memory_space_constraint(one, pltpu.VMEM) for one in held], *pieces)


def gather_taps(frames, taps):
    cells = HH * WW
    channels = frames[0].shape[1]
    column = lax.broadcasted_iota(jnp.int32, (cells, 1), 0) % WW
    blank = jnp.zeros((WW, channels), jnp.float32)
    for number, frame in enumerate(frames):
        wide = frame.astype(jnp.float32)
        for across, offset in enumerate((-1, 0, 1)):
            cell = wide
            if offset:
                inside = (column + offset >= 0) & (column + offset < WW)
                cell = jnp.where(inside, pltpu.roll(wide, (-offset) % cells, 0), 0.0)
            cell = jnp.concatenate([blank, cell, blank], axis=0)
            for down in range(3):
                taps[
                    pl.ds(number * cells, cells), pl.ds((down * 3 + across) * channels, channels)
                ] = cell[down * WW : down * WW + cells].astype(jnp.bfloat16)


def refine_kernel(frames_ref, mid_ref, even_ref, odd_ref, weight, out_ref, held, taps, sem):
    cells = HH * WW
    rows, _ = mid_ref.shape
    me = lax.axis_index("ctx")
    odd = lax.rem(me, 2)
    before, after = rows - cells, rows + cells

    def at(start):
        return pl.ds(pl.multiple_of(start, cells), cells)

    copies = (
        pltpu.make_async_copy(mid_ref, held.at[pl.ds(cells, rows), :], sem.at[0]),
        pltpu.make_async_copy(
            even_ref.at[at(odd * before), :], held.at[at((1 - odd) * after), :], sem.at[1]
        ),
        pltpu.make_async_copy(
            odd_ref.at[at((1 - odd) * before), :], held.at[at(odd * after), :], sem.at[2]
        ),
    )

    for copy in copies:
        copy.start()
    for copy in copies:
        copy.wait()
    gather_taps(
        [held[pl.ds(start, cells), :] for start in range(0, rows + 2 * cells, cells)], taps
    )
    total = held[pl.ds(cells, rows), :].astype(jnp.float32)
    for ahead in range(3):
        total = total + jnp.dot(
            taps[pl.ds(ahead * cells, rows), :], weight[ahead], preferred_element_type=jnp.float32
        )
    token = me * rows + lax.broadcasted_iota(jnp.int32, (rows, 1), 0)
    out_ref[0] = jnp.where(token < frames_ref[0] * cells, total, 0.0).astype(out_ref.dtype)


def refine(frames, mid, even, odd, taps, limit):
    rows, channels = mid.shape
    return pl.pallas_call(
        refine_kernel,
        out_shape=jax.ShapeDtypeStruct((1, rows, channels), jnp.bfloat16),
        in_specs=[pl.BlockSpec(memory_space=pltpu.SMEM)]
        + [pl.BlockSpec(memory_space=pl.ANY)] * 3
        + [pl.BlockSpec(memory_space=pltpu.VMEM)],
        out_specs=pl.BlockSpec(memory_space=pltpu.VMEM),
        scratch_shapes=[
            pltpu.VMEM((rows + 2 * HH * WW, channels), jnp.bfloat16),
            pltpu.VMEM((rows + 2 * HH * WW, 9 * channels), jnp.bfloat16),
            pltpu.SemaphoreType.DMA((3,)),
        ],
        cost_estimate=pl.CostEstimate(
            flops=54 * rows * channels * channels,
            bytes_accessed=2 * taps.size + 6 * rows * channels,
            transcendentals=0,
        ),
        compiler_params=pltpu.CompilerParams(vmem_limit_bytes=limit),
        name="refine",
    )(frames, mid, even, odd, pltpu.with_memory_space_constraint(taps, pltpu.VMEM))


def clip_orders(sec_count):
    return [
        order
        for order in itertools.permutations(range(sec_count))
        if any(order[(d + sec_count // 2) % sec_count] == d for d in range(sec_count))
    ]


def order_index(destination, sec_count):
    if sec_count > 4:
        return jnp.int32(0)
    orders = clip_orders(sec_count)
    codes = jnp.asarray(
        [sum(d * sec_count**i for i, d in enumerate(order)) for order in orders], jnp.int32
    )
    powers = jnp.asarray([sec_count**i for i in range(sec_count)], jnp.int32)
    code = jnp.sum(destination * powers)
    return jnp.sum(jnp.where(codes == code, jnp.arange(len(orders), dtype=jnp.int32), 0))


def handoff(projected, which, source, sec_count):
    if sec_count <= 4:
        def take(order):
            return lambda value: lax.ppermute(value, "sec", list(enumerate(order)))

        return lax.switch(which, [take(order) for order in clip_orders(sec_count)], projected)
    my_section = lax.axis_index("sec")
    chosen = projected
    for step in range(1, sec_count):
        arrived = lax.ppermute(projected, "sec", ring(step, sec_count))
        chosen = jnp.where(source == partner(my_section, step, sec_count)[1], arrived, chosen)
    return chosen


def body(
    hidden_state,
    queries,
    key_vectors,
    value_vectors,
    modulation,
    down_weight,
    conv_weight,
    clip_frames,
    destination,
    timestep,
):
    my_section = lax.axis_index("sec")
    sec_count = lax.axis_size("sec")
    count = lax.axis_size("ctx")
    chips = count // 2
    model_width = hidden_state.shape[2]
    group = HEADS // chips
    head_size = model_width // HEADS
    head_cols = group * head_size
    chunks = head_chunks(group)
    widths = [heads * head_size for heads in chunks]
    tensors = (queries, key_vectors, value_vectors)
    steps = range(1, chips)

    own, beside = [], []
    for chunk, width in enumerate(widths):
        packed = [None] * chips
        order = far_first(chips)[0]
        for batch in (order[:1], order[1:] + [0]) if chunk == 0 else (order + [0],):
            pieces = pack(tensors, batch, chips, head_cols, sum(widths[:chunk]), width)
            for step, piece in zip(batch, pieces):
                packed[step] = piece
        beside.append([across(packed[0], chips)])
        own.append([packed[0]] + [send(packed[step], step, chips) for step in steps])
        beside[chunk] += [across(own[chunk][step], chips) for step in steps]

    section_ids = jnp.arange(destination.shape[0], dtype=jnp.int32)
    source = jnp.sum(jnp.where(destination == my_section, section_ids, 0))
    own_frames = lax.dynamic_slice(clip_frames, (my_section,), (1,))
    clip_length = lax.dynamic_slice(clip_frames, (source,), (1,))
    which = order_index(destination, sec_count)
    mod_rows = lax.dynamic_index_in_dim(modulation, timestep[my_section], 0, keepdims=False)
    ready = prepare(hidden_state, mod_rows, down_weight, chips, widths[0])
    own_frames, clip_length, which, mod_rows, ready = lax.optimization_barrier(
        (own_frames, clip_length, which, mod_rows, ready)
    )

    returned = []
    for chunk, heads in enumerate(chunks):
        outs = attend(own_frames, own[chunk], beside[chunk], heads)
        returned.append([outs[0]] + [send(outs[step], step, chips) for step in steps])
    channels = down_weight.shape[1]
    later = (*ready, conv_weight.reshape(3, 9 * channels, channels))
    kept = project_early(hidden_state, mod_rows, down_weight, returned[0], later)
    limit = share(hidden_state.shape[1], channels, later)
    projected = project_late(own_frames, kept[:7], returned[1], model_width, limit)
    mid = handoff(projected, which, source, sec_count)
    even = lax.ppermute(mid, "ctx", [(i, i ^ 1) for i in range(count)])
    joints = [(i, i + 1) for i in range(1, count - 1, 2)]
    odd = lax.ppermute(mid, "ctx", joints + [(two, one) for one, two in joints])
    return refine(clip_length, mid, even, odd, kept[7], limit)


def solution(mesh):
    split = P("sec", "ctx", None)
    return jax.shard_map(
        body,
        mesh=mesh,
        in_specs=(split,) * 4 + (P(),) * 6,
        out_specs=split,
        check_vma=False,
    )
```

```python
import functools
import itertools
import math

import jax
import jax.numpy as jnp
from jax import lax
from jax.experimental import pallas as pl
from jax.experimental.pallas import tpu as pltpu
from jax.sharding import PartitionSpec as P


HEADS = 32
VMEM_BYTES = 67043328
SPARE_BYTES = 128 * 1024
HH = 8
WW = 8


def head_chunks(group):
    late = max(1, group // 4)
    return group - late, late


def partner(me, step, count):
    if count & (count - 1) == 0:
        return me ^ step, me ^ step
    return lax.rem(me + step, count), lax.rem(me - step + count, count)


def ring(step, count):
    if count & (count - 1) == 0:
        return [(i, i ^ step) for i in range(count)]
    return [(i, (i + step) % count) for i in range(count)]


def far_first(chips):
    far = list(range(chips - 1, max(chips // 2, 1) - 1, -1))
    return far + list(range(chips // 2 - 1, 0, -1))


def send(value, step, chips):
    pairs = [
        (2 * one + core, 2 * two + core) for one, two in ring(step, chips) for core in range(2)
    ]
    return lax.ppermute(value, "ctx", pairs)


def across(value, chips):
    return lax.ppermute(value, "ctx", [(i, i ^ 1) for i in range(2 * chips)])


def my_chip(step, chips):
    return partner(lax.axis_index("ctx") // 2, step, chips)


def pack_kernel(steps, chips, kinds, head_cols, first_col, width, *rest):
    sources, outs = rest[:kinds], rest[kinds : kinds + len(steps)]
    buf, in_sem, out_sem = rest[kinds + len(steps) :]
    order = range(len(steps))

    def load(step, kind):
        col = pl.multiple_of(my_chip(steps[step], chips)[0] * head_cols + first_col, 128)
        return pltpu.make_async_copy(
            sources[kind].at[0, :, pl.ds(col, width)], buf.at[step, kind], in_sem.at[step, kind]
        )

    def save(step):
        return pltpu.make_async_copy(buf.at[step], outs[step], out_sem.at[step])

    for step in order:
        for kind in range(kinds):
            load(step, kind).start()
    for step in order:
        for kind in range(kinds):
            load(step, kind).wait()
        save(step).start()
    for step in order:
        save(step).wait()


def pack(sources, steps, chips, head_cols, first_col, width):
    rows = sources[0].shape[1]
    kinds = len(sources)
    piece = jax.ShapeDtypeStruct((kinds, rows, width), sources[0].dtype)
    return pl.pallas_call(
        functools.partial(pack_kernel, steps, chips, kinds, head_cols, first_col, width),
        out_shape=[piece] * len(steps),
        in_specs=[pl.BlockSpec(memory_space=pltpu.HBM)] * kinds,
        out_specs=[pl.BlockSpec(memory_space=pltpu.HBM)] * len(steps),
        scratch_shapes=[
            pltpu.VMEM((len(steps), kinds, rows, width), sources[0].dtype),
            pltpu.SemaphoreType.DMA((len(steps), kinds)),
            pltpu.SemaphoreType.DMA((len(steps),)),
        ],
        cost_estimate=pl.CostEstimate(
            flops=0, bytes_accessed=4 * kinds * len(steps) * rows * width, transcendentals=0
        ),
        compiler_params=pltpu.CompilerParams(vmem_limit_bytes=VMEM_BYTES),
        name="pack",
    )(*sources)


def attend_kernel(chips, heads, block_rows, frames_ref, *rest):
    own, beside, outs = rest[:chips], rest[chips : 2 * chips], rest[2 * chips : 3 * chips]
    queries, keys, values, result, in_sem, value_sem, out_sem = rest[3 * chips :]
    core = lax.rem(lax.axis_index("ctx"), 2)
    rows = own[0].shape[1]
    asked = chips * rows
    seq = 2 * asked
    size = own[0].shape[2] // heads
    scale = math.log2(math.e) / math.sqrt(size)
    blocks = asked // block_rows

    def place(step, side):
        device = my_chip(step, chips)[1] * 2 + (core if side == 0 else 1 - core)
        return pl.ds(pl.multiple_of(device * rows, rows), rows)

    def load(step, which):
        if which == 2:
            source, target = own[step].at[0], queries.at[pl.ds(step * rows, rows), :]
        else:
            source, target = (own, beside)[which][step].at[1], keys.at[place(step, which), :]
        return pltpu.make_async_copy(source, target, in_sem.at[which, step])

    def load_values(step, side, head):
        return pltpu.make_async_copy(
            (own, beside)[side][step].at[2, :, pl.ds(head * size, size)],
            values.at[place(step, side), pl.ds(head * 2 * size, size)],
            value_sem.at[side, head, step],
        )

    def save(step):
        return pltpu.make_async_copy(
            result.at[pl.ds(step * rows, rows), :], outs[step], out_sem.at[step]
        )

    for step in range(chips):
        for which in range(3):
            load(step, which).start()
    for head in range(heads):
        for step in range(chips):
            for side in range(2):
                load_values(step, side, head).start()
    for head in range(heads):
        values[:, pl.ds((head * 2 + 1) * size, size)] = jnp.ones((seq, size), jnp.bfloat16)
    valid = frames_ref[0] * (HH * WW)
    places = lax.broadcasted_iota(jnp.int32, (1, seq), 1)
    bias = jnp.where(places < valid, 0.0, -jnp.inf)
    for step in range(chips):
        for which in range(3):
            load(step, which).wait()
    for head in range(heads):
        for step in range(chips):
            for side in range(2):
                load_values(step, side, head).wait()

    def task(index, carry):
        head = index // blocks
        start = pl.multiple_of(lax.rem(index, blocks) * block_rows, block_rows)
        here = pl.ds(start, block_rows)
        lanes = pl.ds(pl.multiple_of(head * size, size), size)
        scores = lax.dot_general(
            queries[here, lanes],
            keys[:, lanes],
            (((1,), (1,)), ((), ())),
            preferred_element_type=jnp.float32,
        )
        scores = scores * scale + bias
        weights = jnp.exp2(scores - jnp.max(scores, axis=1, keepdims=True))
        both = jnp.dot(
            weights.astype(jnp.bfloat16),
            values[:, pl.ds(pl.multiple_of(head * (2 * size), 2 * size), 2 * size)],
            preferred_element_type=jnp.float32,
        )
        result[here, lanes] = (both[:, :size] / both[:, size:]).astype(result.dtype)
        return carry

    lax.fori_loop(0, heads * blocks, task, 0, unroll=4)
    for step in range(chips):
        save(step).start()
    for step in range(chips):
        save(step).wait()


def attend(frames, own, beside, heads):
    chips = len(own)
    _, rows, width = own[0].shape
    asked = chips * rows
    seq = 2 * asked
    block_rows = min(256, asked)
    return pl.pallas_call(
        functools.partial(attend_kernel, chips, heads, block_rows),
        out_shape=[jax.ShapeDtypeStruct((rows, width), jnp.bfloat16)] * chips,
        in_specs=[pl.BlockSpec(memory_space=pltpu.SMEM)]
        + [pl.BlockSpec(memory_space=pltpu.HBM)] * (2 * chips),
        out_specs=[pl.BlockSpec(memory_space=pltpu.HBM)] * chips,
        scratch_shapes=[
            pltpu.VMEM((asked, width), jnp.bfloat16),
            pltpu.VMEM((seq, width), jnp.bfloat16),
            pltpu.VMEM((seq, 2 * width), jnp.bfloat16),
            pltpu.VMEM((asked, width), jnp.bfloat16),
            pltpu.SemaphoreType.DMA((3, chips)),
            pltpu.SemaphoreType.DMA((2, heads, chips)),
            pltpu.SemaphoreType.DMA((chips,)),
        ],
        cost_estimate=pl.CostEstimate(
            flops=6 * asked * seq * width,
            bytes_accessed=8 * seq * width,
            transcendentals=asked * seq * heads,
        ),
        compiler_params=pltpu.CompilerParams(vmem_limit_bytes=VMEM_BYTES),
        name="attend",
    )(frames, *own, *beside)


def prepare_kernel(chips, head_cols, width, h_ref, mod_ref, weight_ref, *rest):
    h_out, mod_out, weight_out, const_ref, _, mod, weight, late_h, late_mod, late_weight, in_sem, out_sem = rest
    late = head_cols - width

    def pull(step, which):
        col = pl.multiple_of(my_chip(step, chips)[1] * head_cols + width, 128)
        here = pl.ds(step * late, late)
        source, target = (
            (h_ref.at[0, :, pl.ds(col, late)], late_h.at[:, here]),
            (mod_ref.at[:, pl.ds(col, late)], late_mod.at[:, here]),
            (weight_ref.at[pl.ds(col, late), :], late_weight.at[here, :]),
        )[which]
        return pltpu.make_async_copy(source, target, in_sem.at[which, step])

    def whole(which):
        source, target = ((mod_ref, mod), (weight_ref, weight))[which]
        return pltpu.make_async_copy(source, target, in_sem.at[3, which])

    def push(which):
        source, target = ((late_h, h_out), (late_mod, mod_out), (late_weight, weight_out))[which]
        return pltpu.make_async_copy(source, target, out_sem.at[which])

    for which in range(3):
        for step in range(chips):
            pull(step, which).start()
    whole(0).start()
    whole(1).start()
    for which in range(3):
        for step in range(chips):
            pull(step, which).wait()
        push(which).start()

    def product(row):
        high = row.astype(jnp.bfloat16)
        low = (row - high.astype(jnp.float32)).astype(jnp.bfloat16)
        split = jnp.concatenate(
            [jnp.broadcast_to(high, (8,) + high.shape[1:]), jnp.broadcast_to(low, (8,) + low.shape[1:])],
            axis=0,
        )
        both = jnp.dot(split, weight[...], preferred_element_type=jnp.float32)
        return both[:8] + both[8:]

    whole(0).wait()
    whole(1).wait()
    const_ref[0] = product(1.0 + mod[1:2, :])
    const_ref[1] = product(mod[0:1, :])
    for which in range(3):
        push(which).wait()


def prepare(hidden_state, mod_rows, down_weight, chips, width):
    _, rows, model = hidden_state.shape
    channels = down_weight.shape[1]
    head_cols = model // chips
    late = chips * (head_cols - width)
    hbm = pl.BlockSpec(memory_space=pltpu.HBM)
    shapes = [
        ((rows, late), jnp.bfloat16),
        ((3, late), jnp.float32),
        ((late, channels), jnp.bfloat16),
    ]
    return pl.pallas_call(
        functools.partial(prepare_kernel, chips, head_cols, width),
        out_shape=[jax.ShapeDtypeStruct(*shape) for shape in shapes]
        + [jax.ShapeDtypeStruct((2, 8, channels), jnp.float32)],
        in_specs=[hbm] * 3,
        out_specs=[hbm] * 3 + [pl.BlockSpec(memory_space=pltpu.VMEM)],
        scratch_shapes=[
            pltpu.VMEM((8, 128), jnp.float32),
            pltpu.VMEM((3, model), jnp.float32),
            pltpu.VMEM((model, channels), jnp.bfloat16),
        ]
        + [pltpu.VMEM(*shape) for shape in shapes]
        + [pltpu.SemaphoreType.DMA((4, max(chips, 2))), pltpu.SemaphoreType.DMA((3,))],
        cost_estimate=pl.CostEstimate(
            flops=64 * model * channels, bytes_accessed=4 * model * channels, transcendentals=0
        ),
        compiler_params=pltpu.CompilerParams(vmem_limit_bytes=VMEM_BYTES),
        name="prepare",
    )(hidden_state, mod_rows, down_weight)


def share(rows, channels, later):
    kept = sum(array.size * array.dtype.itemsize for array in later)
    return VMEM_BYTES - kept - 4 * rows * (channels + 256) - SPARE_BYTES


def early_kernel(chips, head_cols, h_ref, mod_ref, weight_ref, *rest):
    pieces, later, rest = rest[:chips], rest[chips : chips + 5], rest[chips + 5 :]
    acc_ref, centre_ref, square_ref = rest[:3]
    kept, (attended, hidden, weight, mod, sem, keep_sem) = rest[3:8], rest[8:]
    rows, width = pieces[0].shape
    block_rows = 16

    def pull(step, which):
        col = pl.multiple_of(my_chip(step, chips)[1] * head_cols, 128)
        here = pl.ds(step * width, width)
        source, target = (
            (pieces[step], attended.at[:, here]),
            (h_ref.at[0, :, pl.ds(col, width)], hidden.at[:, here]),
            (mod_ref.at[:, pl.ds(col, width)], mod.at[:, here]),
            (weight_ref.at[pl.ds(col, width), :], weight.at[here, :]),
        )[which]
        return pltpu.make_async_copy(source, target, sem.at[which, step])

    def keep(which):
        return pltpu.make_async_copy(later[which], kept[which], keep_sem.at[which])

    for which in range(4):
        for step in range(chips):
            pull(step, which).start()
    for which in range(5):
        keep(which).start()
    for which in range(3):
        for step in range(chips):
            pull(step, which).wait()

    def rows_of(index, carry):
        here = pl.ds(pl.multiple_of(index * block_rows, block_rows), block_rows)
        wide = (
            (
                hidden[here, :].astype(jnp.float32)
                + mod[2:3, :] * attended[here, :].astype(jnp.float32)
            )
            .astype(jnp.bfloat16)
            .astype(jnp.float32)
        )
        centre = jnp.mean(wide, axis=-1, keepdims=True)
        away = wide - centre
        square = jnp.sum(jnp.square(away), axis=-1, keepdims=True)
        attended[here, :] = (away * (1.0 + mod[1:2, :])).astype(jnp.bfloat16)
        centre_ref[here, :] = jnp.broadcast_to(centre, (block_rows, 128))
        square_ref[here, :] = jnp.broadcast_to(square, (block_rows, 128))
        return carry

    lax.fori_loop(0, rows // block_rows, rows_of, 0, unroll=4)
    for step in range(chips):
        pull(step, 3).wait()
    acc_ref[...] = jnp.dot(attended[...], weight[...], preferred_element_type=jnp.float32)
    for which in range(5):
        keep(which).wait()


def project_early(hidden_state, mod_rows, down_weight, pieces, later):
    chips = len(pieces)
    _, rows, model = hidden_state.shape
    channels = down_weight.shape[1]
    width = pieces[0].shape[1]
    return pl.pallas_call(
        functools.partial(early_kernel, chips, model // chips),
        out_shape=[
            pltpu.VMEM((rows, channels), jnp.float32),
            pltpu.VMEM((rows, 128), jnp.float32),
            pltpu.VMEM((rows, 128), jnp.float32),
        ]
        + [pltpu.VMEM(array.shape, array.dtype) for array in later],
        in_specs=[pl.BlockSpec(memory_space=pltpu.HBM)] * (chips + 8),
        out_specs=[pl.BlockSpec(memory_space=pltpu.VMEM)] * 8,
        scratch_shapes=[
            pltpu.VMEM((rows, chips * width), jnp.bfloat16),
            pltpu.VMEM((rows, chips * width), jnp.bfloat16),
            pltpu.VMEM((chips * width, channels), jnp.bfloat16),
            pltpu.VMEM((3, chips * width), jnp.float32),
            pltpu.SemaphoreType.DMA((4, chips)),
            pltpu.SemaphoreType.DMA((5,)),
        ],
        cost_estimate=pl.CostEstimate(
            flops=2 * rows * chips * width * channels,
            bytes_accessed=4 * rows * model + 2 * model * channels,
            transcendentals=0,
        ),
        compiler_params=pltpu.CompilerParams(vmem_limit_bytes=share(rows, channels, later)),
        name="project_early",
    )(hidden_state, mod_rows, down_weight, *pieces, *later)


def late_kernel(count, early, frames_ref, *rest):
    held, pieces, (out_ref, attended, in_sem) = rest[:7], rest[7 : 7 + count], rest[7 + count :]
    acc_ref, centre_ref, square_ref, h_ref, mod_ref, weight_ref, const_ref = held
    rows, width = pieces[0].shape
    late = count * width
    model = early + late

    def load(step):
        return pltpu.make_async_copy(
            pieces[step], attended.at[:, pl.ds(step * width, width)], in_sem.at[step]
        )

    for step in range(count):
        load(step).start()
    for step in range(count):
        load(step).wait()
    wide = (
        (h_ref[...].astype(jnp.float32) + mod_ref[2:3, :] * attended[...].astype(jnp.float32))
        .astype(jnp.bfloat16)
        .astype(jnp.float32)
    )
    first = centre_ref[:, :1]
    scaled = ((wide - first) * (1.0 + mod_ref[1:2, :])).astype(jnp.bfloat16)
    total = acc_ref[...] + jnp.dot(scaled, weight_ref[...], preferred_element_type=jnp.float32)
    own = jnp.mean(wide, axis=-1, keepdims=True)
    square = jnp.sum(jnp.square(wide - own), axis=-1, keepdims=True)
    gap = own - first
    centre = first + gap * (late / model)
    spread = (square_ref[:, :1] + square + gap * gap * (early * late / model)) / model
    total = total + (first - centre) * const_ref[0, :1, :]
    total = total * lax.rsqrt(spread + 1e-06) + const_ref[1, :1, :]
    token = lax.axis_index("ctx") * rows + lax.broadcasted_iota(jnp.int32, (rows, 1), 0)
    out_ref[...] = jnp.where(token < frames_ref[0] * (HH * WW), total, 0.0).astype(out_ref.dtype)


def project_late(frames, held, pieces, model, limit):
    count = len(pieces)
    rows, width = pieces[0].shape
    channels = held[0].shape[1]
    return pl.pallas_call(
        functools.partial(late_kernel, count, model - count * width),
        out_shape=jax.ShapeDtypeStruct((rows, channels), jnp.bfloat16),
        in_specs=[pl.BlockSpec(memory_space=pltpu.SMEM)]
        + [pl.BlockSpec(memory_space=pltpu.VMEM)] * 7
        + [pl.BlockSpec(memory_space=pltpu.HBM)] * count,
        out_specs=pl.BlockSpec(memory_space=pltpu.VMEM),
        scratch_shapes=[
            pltpu.VMEM((rows, count * width), jnp.bfloat16),
            pltpu.SemaphoreType.DMA((count,)),
        ],
        cost_estimate=pl.CostEstimate(
            flops=2 * rows * count * width * channels,
            bytes_accessed=4 * rows * count * width,
            transcendentals=0,
        ),
        compiler_params=pltpu.CompilerParams(vmem_limit_bytes=limit),
        name="project_late",
    )(frames, *[pltpu.with_memory_space_constraint(one, pltpu.VMEM) for one in held], *pieces)


def gather_taps(frames, taps):
    cells = HH * WW
    channels = frames[0].shape[1]
    column = lax.broadcasted_iota(jnp.int32, (cells, 1), 0) % WW
    blank = jnp.zeros((WW, channels), jnp.float32)
    for number, frame in enumerate(frames):
        wide = frame.astype(jnp.float32)
        for across, offset in enumerate((-1, 0, 1)):
            cell = wide
            if offset:
                inside = (column + offset >= 0) & (column + offset < WW)
                cell = jnp.where(inside, pltpu.roll(wide, (-offset) % cells, 0), 0.0)
            cell = jnp.concatenate([blank, cell, blank], axis=0)
            for down in range(3):
                taps[
                    pl.ds(number * cells, cells), pl.ds((down * 3 + across) * channels, channels)
                ] = cell[down * WW : down * WW + cells].astype(jnp.bfloat16)


def refine_kernel(frames_ref, mid_ref, even_ref, odd_ref, weight, out_ref, held, taps, sem):
    cells = HH * WW
    rows, _ = mid_ref.shape
    me = lax.axis_index("ctx")
    odd = lax.rem(me, 2)
    before, after = rows - cells, rows + cells

    def at(start):
        return pl.ds(pl.multiple_of(start, cells), cells)

    copies = (
        pltpu.make_async_copy(mid_ref, held.at[pl.ds(cells, rows), :], sem.at[0]),
        pltpu.make_async_copy(
            even_ref.at[at(odd * before), :], held.at[at((1 - odd) * after), :], sem.at[1]
        ),
        pltpu.make_async_copy(
            odd_ref.at[at((1 - odd) * before), :], held.at[at(odd * after), :], sem.at[2]
        ),
    )

    for copy in copies:
        copy.start()
    for copy in copies:
        copy.wait()
    gather_taps(
        [held[pl.ds(start, cells), :] for start in range(0, rows + 2 * cells, cells)], taps
    )
    total = held[pl.ds(cells, rows), :].astype(jnp.float32)
    for ahead in range(3):
        total = total + jnp.dot(
            taps[pl.ds(ahead * cells, rows), :], weight[ahead], preferred_element_type=jnp.float32
        )
    token = me * rows + lax.broadcasted_iota(jnp.int32, (rows, 1), 0)
    out_ref[0] = jnp.where(token < frames_ref[0] * cells, total, 0.0).astype(out_ref.dtype)


def refine(frames, mid, even, odd, taps, limit):
    rows, channels = mid.shape
    return pl.pallas_call(
        refine_kernel,
        out_shape=jax.ShapeDtypeStruct((1, rows, channels), jnp.bfloat16),
        in_specs=[pl.BlockSpec(memory_space=pltpu.SMEM)]
        + [pl.BlockSpec(memory_space=pl.ANY)] * 3
        + [pl.BlockSpec(memory_space=pltpu.VMEM)],
        out_specs=pl.BlockSpec(memory_space=pltpu.VMEM),
        scratch_shapes=[
            pltpu.VMEM((rows + 2 * HH * WW, channels), jnp.bfloat16),
            pltpu.VMEM((rows + 2 * HH * WW, 9 * channels), jnp.bfloat16),
            pltpu.SemaphoreType.DMA((3,)),
        ],
        cost_estimate=pl.CostEstimate(
            flops=54 * rows * channels * channels,
            bytes_accessed=2 * taps.size + 6 * rows * channels,
            transcendentals=0,
        ),
        compiler_params=pltpu.CompilerParams(vmem_limit_bytes=limit),
        name="refine",
    )(frames, mid, even, odd, pltpu.with_memory_space_constraint(taps, pltpu.VMEM))


def clip_orders(sec_count):
    return [
        order
        for order in itertools.permutations(range(sec_count))
        if any(order[(d + sec_count // 2) % sec_count] == d for d in range(sec_count))
    ]


def order_index(destination, sec_count):
    if sec_count > 4:
        return jnp.int32(0)
    orders = clip_orders(sec_count)
    codes = jnp.asarray(
        [sum(d * sec_count**i for i, d in enumerate(order)) for order in orders], jnp.int32
    )
    powers = jnp.asarray([sec_count**i for i in range(sec_count)], jnp.int32)
    code = jnp.sum(destination * powers)
    return jnp.sum(jnp.where(codes == code, jnp.arange(len(orders), dtype=jnp.int32), 0))


def handoff(projected, which, source, sec_count):
    if sec_count <= 4:
        def take(order):
            return lambda value: lax.ppermute(value, "sec", list(enumerate(order)))

        return lax.switch(which, [take(order) for order in clip_orders(sec_count)], projected)
    my_section = lax.axis_index("sec")
    chosen = projected
    for step in range(1, sec_count):
        arrived = lax.ppermute(projected, "sec", ring(step, sec_count))
        chosen = jnp.where(source == partner(my_section, step, sec_count)[1], arrived, chosen)
    return chosen


def body(
    hidden_state,
    queries,
    key_vectors,
    value_vectors,
    modulation,
    down_weight,
    conv_weight,
    clip_frames,
    destination,
    timestep,
):
    my_section = lax.axis_index("sec")
    sec_count = lax.axis_size("sec")
    count = lax.axis_size("ctx")
    chips = count // 2
    model_width = hidden_state.shape[2]
    group = HEADS // chips
    head_size = model_width // HEADS
    head_cols = group * head_size
    chunks = head_chunks(group)
    widths = [heads * head_size for heads in chunks]
    tensors = (queries, key_vectors, value_vectors)
    steps = range(1, chips)

    own, beside = [], []
    for chunk, width in enumerate(widths):
        packed = [None] * chips
        order = far_first(chips)
        for batch in (order[:1], order[1:] + [0]) if chunk == 0 else (order + [0],):
            pieces = pack(tensors, batch, chips, head_cols, sum(widths[:chunk]), width)
            for step, piece in zip(batch, pieces):
                packed[step] = piece
        beside.append([across(packed[0], chips)])
        own.append([packed[0]] + [send(packed[step], step, chips) for step in steps])
        beside[chunk] += [across(own[chunk][step], chips) for step in steps]

    section_ids = jnp.arange(destination.shape[0], dtype=jnp.int32)
    source = jnp.sum(jnp.where(destination == my_section, section_ids, 0))
    own_frames = lax.dynamic_slice(clip_frames, (my_section,), (1,))
    clip_length = lax.dynamic_slice(clip_frames, (source,), (1,))
    which = order_index(destination, sec_count)
    mod_rows = lax.dynamic_index_in_dim(modulation, timestep[my_section], 0, keepdims=False)
    ready = prepare(hidden_state, mod_rows, down_weight, chips, widths[0])
    own_frames, clip_length, which, mod_rows, ready = lax.optimization_barrier(
        (own_frames, clip_length, which, mod_rows, ready)
    )

    returned = []
    for chunk, heads in enumerate(chunks):
        outs = attend(own_frames, own[chunk], beside[chunk], heads)
        returned.append([outs[0]] + [send(outs[step], step, chips) for step in steps])
    channels = down_weight.shape[1]
    later = (*ready, conv_weight.reshape(3, 9 * channels, channels))
    kept = project_early(hidden_state, mod_rows, down_weight, returned[0], later)
    limit = share(hidden_state.shape[1], channels, later)
    projected = project_late(own_frames, kept[:7], returned[1], model_width, limit)
    mid = handoff(projected, which, source, sec_count)
    even = lax.ppermute(mid, "ctx", [(i, i ^ 1) for i in range(count)])
    joints = [(i, i + 1) for i in range(1, count - 1, 2)]
    odd = lax.ppermute(mid, "ctx", joints + [(two, one) for one, two in joints])
    return refine(clip_length, mid, even, odd, kept[7], limit - 4 * SPARE_BYTES)


def solution(mesh):
    split = P("sec", "ctx", None)
    return jax.shard_map(
        body,
        mesh=mesh,
        in_specs=(split,) * 4 + (P(),) * 6,
        out_specs=split,
        check_vma=False,
    )
```

```python
import functools
import itertools
import math

import jax
import jax.numpy as jnp
from jax import lax
from jax.experimental import pallas as pl
from jax.experimental.pallas import tpu as pltpu
from jax.sharding import PartitionSpec as P


HEADS = 32
VMEM_BYTES = 67043328
SPARE_BYTES = 128 * 1024
HH = 8
WW = 8


def head_chunks(group):
    late = max(1, group // 4)
    return group - late, late


def partner(me, step, count):
    if count & (count - 1) == 0:
        return me ^ step, me ^ step
    return lax.rem(me + step, count), lax.rem(me - step + count, count)


def ring(step, count):
    if count & (count - 1) == 0:
        return [(i, i ^ step) for i in range(count)]
    return [(i, (i + step) % count) for i in range(count)]


def far_first(chips):
    far = list(range(chips - 1, max(chips // 2, 1) - 1, -1))
    return far + list(range(chips // 2 - 1, 0, -1))


def send(value, step, chips):
    pairs = [
        (2 * one + core, 2 * two + core) for one, two in ring(step, chips) for core in range(2)
    ]
    return lax.ppermute(value, "ctx", pairs)


def across(value, chips):
    return lax.ppermute(value, "ctx", [(i, i ^ 1) for i in range(2 * chips)])


def my_chip(step, chips):
    return partner(lax.axis_index("ctx") // 2, step, chips)


def pack_kernel(steps, chips, kinds, head_cols, first_col, width, *rest):
    sources, outs = rest[:kinds], rest[kinds : kinds + len(steps)]
    buf, in_sem, out_sem = rest[kinds + len(steps) :]
    order = range(len(steps))

    def load(step, kind):
        col = pl.multiple_of(my_chip(steps[step], chips)[0] * head_cols + first_col, 128)
        return pltpu.make_async_copy(
            sources[kind].at[0, :, pl.ds(col, width)], buf.at[step, kind], in_sem.at[step, kind]
        )

    def save(step):
        return pltpu.make_async_copy(buf.at[step], outs[step], out_sem.at[step])

    for step in order:
        for kind in range(kinds):
            load(step, kind).start()
    for step in order:
        for kind in range(kinds):
            load(step, kind).wait()
        save(step).start()
    for step in order:
        save(step).wait()


def pack(sources, steps, chips, head_cols, first_col, width):
    rows = sources[0].shape[1]
    kinds = len(sources)
    piece = jax.ShapeDtypeStruct((kinds, rows, width), sources[0].dtype)
    return pl.pallas_call(
        functools.partial(pack_kernel, steps, chips, kinds, head_cols, first_col, width),
        out_shape=[piece] * len(steps),
        in_specs=[pl.BlockSpec(memory_space=pltpu.HBM)] * kinds,
        out_specs=[pl.BlockSpec(memory_space=pltpu.HBM)] * len(steps),
        scratch_shapes=[
            pltpu.VMEM((len(steps), kinds, rows, width), sources[0].dtype),
            pltpu.SemaphoreType.DMA((len(steps), kinds)),
            pltpu.SemaphoreType.DMA((len(steps),)),
        ],
        cost_estimate=pl.CostEstimate(
            flops=0, bytes_accessed=4 * kinds * len(steps) * rows * width, transcendentals=0
        ),
        compiler_params=pltpu.CompilerParams(vmem_limit_bytes=VMEM_BYTES),
        name="pack",
    )(*sources)


def attend_kernel(chips, heads, block_rows, frames_ref, *rest):
    own, beside, outs = rest[:chips], rest[chips : 2 * chips], rest[2 * chips : 3 * chips]
    queries, keys, values, result, in_sem, value_sem, out_sem = rest[3 * chips :]
    core = lax.rem(lax.axis_index("ctx"), 2)
    rows = own[0].shape[1]
    asked = chips * rows
    seq = 2 * asked
    size = own[0].shape[2] // heads
    scale = math.log2(math.e) / math.sqrt(size)
    blocks = asked // block_rows

    def place(step, side):
        device = my_chip(step, chips)[1] * 2 + (core if side == 0 else 1 - core)
        return pl.ds(pl.multiple_of(device * rows, rows), rows)

    def load(step, which):
        if which == 2:
            source, target = own[step].at[0], queries.at[pl.ds(step * rows, rows), :]
        else:
            source, target = (own, beside)[which][step].at[1], keys.at[place(step, which), :]
        return pltpu.make_async_copy(source, target, in_sem.at[which, step])

    def load_values(step, side, head):
        return pltpu.make_async_copy(
            (own, beside)[side][step].at[2, :, pl.ds(head * size, size)],
            values.at[place(step, side), pl.ds(head * 2 * size, size)],
            value_sem.at[side, head, step],
        )

    def save(step):
        return pltpu.make_async_copy(
            result.at[pl.ds(step * rows, rows), :], outs[step], out_sem.at[step]
        )

    for step in range(chips):
        for which in range(3):
            load(step, which).start()
    for head in range(heads):
        for step in range(chips):
            for side in range(2):
                load_values(step, side, head).start()
    for head in range(heads):
        values[:, pl.ds((head * 2 + 1) * size, size)] = jnp.ones((seq, size), jnp.bfloat16)
    valid = frames_ref[0] * (HH * WW)
    places = lax.broadcasted_iota(jnp.int32, (1, seq), 1)
    bias = jnp.where(places < valid, 0.0, -jnp.inf)
    for step in range(chips):
        for which in range(3):
            load(step, which).wait()
    for head in range(heads):
        for step in range(chips):
            for side in range(2):
                load_values(step, side, head).wait()

    def task(index, carry):
        head = index // blocks
        start = pl.multiple_of(lax.rem(index, blocks) * block_rows, block_rows)
        here = pl.ds(start, block_rows)
        lanes = pl.ds(pl.multiple_of(head * size, size), size)
        scores = lax.dot_general(
            queries[here, lanes],
            keys[:, lanes],
            (((1,), (1,)), ((), ())),
            preferred_element_type=jnp.float32,
        )
        scores = scores * scale + bias
        weights = jnp.exp2(scores - jnp.max(scores, axis=1, keepdims=True))
        both = jnp.dot(
            weights.astype(jnp.bfloat16),
            values[:, pl.ds(pl.multiple_of(head * (2 * size), 2 * size), 2 * size)],
            preferred_element_type=jnp.float32,
        )
        result[here, lanes] = (both[:, :size] / both[:, size:]).astype(result.dtype)
        return carry

    lax.fori_loop(0, heads * blocks, task, 0, unroll=4)
    for step in range(chips):
        save(step).start()
    for step in range(chips):
        save(step).wait()


def attend(frames, own, beside, heads):
    chips = len(own)
    _, rows, width = own[0].shape
    asked = chips * rows
    seq = 2 * asked
    block_rows = min(256, asked)
    return pl.pallas_call(
        functools.partial(attend_kernel, chips, heads, block_rows),
        out_shape=[jax.ShapeDtypeStruct((rows, width), jnp.bfloat16)] * chips,
        in_specs=[pl.BlockSpec(memory_space=pltpu.SMEM)]
        + [pl.BlockSpec(memory_space=pltpu.HBM)] * (2 * chips),
        out_specs=[pl.BlockSpec(memory_space=pltpu.HBM)] * chips,
        scratch_shapes=[
            pltpu.VMEM((asked, width), jnp.bfloat16),
            pltpu.VMEM((seq, width), jnp.bfloat16),
            pltpu.VMEM((seq, 2 * width), jnp.bfloat16),
            pltpu.VMEM((asked, width), jnp.bfloat16),
            pltpu.SemaphoreType.DMA((3, chips)),
            pltpu.SemaphoreType.DMA((2, heads, chips)),
            pltpu.SemaphoreType.DMA((chips,)),
        ],
        cost_estimate=pl.CostEstimate(
            flops=6 * asked * seq * width,
            bytes_accessed=8 * seq * width,
            transcendentals=asked * seq * heads,
        ),
        compiler_params=pltpu.CompilerParams(vmem_limit_bytes=VMEM_BYTES),
        name="attend",
    )(frames, *own, *beside)


def prepare_kernel(chips, head_cols, width, h_ref, mod_ref, weight_ref, *rest):
    h_out, mod_out, weight_out, const_ref, _, mod, weight, late_h, late_mod, late_weight, in_sem, out_sem = rest
    late = head_cols - width

    def pull(step, which):
        col = pl.multiple_of(my_chip(step, chips)[1] * head_cols + width, 128)
        here = pl.ds(step * late, late)
        source, target = (
            (h_ref.at[0, :, pl.ds(col, late)], late_h.at[:, here]),
            (mod_ref.at[:, pl.ds(col, late)], late_mod.at[:, here]),
            (weight_ref.at[pl.ds(col, late), :], late_weight.at[here, :]),
        )[which]
        return pltpu.make_async_copy(source, target, in_sem.at[which, step])

    def whole(which):
        source, target = ((mod_ref, mod), (weight_ref, weight))[which]
        return pltpu.make_async_copy(source, target, in_sem.at[3, which])

    def push(which):
        source, target = ((late_h, h_out), (late_mod, mod_out), (late_weight, weight_out))[which]
        return pltpu.make_async_copy(source, target, out_sem.at[which])

    for which in range(3):
        for step in range(chips):
            pull(step, which).start()
    whole(0).start()
    whole(1).start()
    for which in range(3):
        for step in range(chips):
            pull(step, which).wait()
        push(which).start()

    def product(row):
        high = row.astype(jnp.bfloat16)
        low = (row - high.astype(jnp.float32)).astype(jnp.bfloat16)
        split = jnp.concatenate(
            [jnp.broadcast_to(high, (8,) + high.shape[1:]), jnp.broadcast_to(low, (8,) + low.shape[1:])],
            axis=0,
        )
        both = jnp.dot(split, weight[...], preferred_element_type=jnp.float32)
        return both[:8] + both[8:]

    whole(0).wait()
    whole(1).wait()
    const_ref[0] = product(1.0 + mod[1:2, :])
    const_ref[1] = product(mod[0:1, :])
    for which in range(3):
        push(which).wait()


def prepare(hidden_state, mod_rows, down_weight, chips, width):
    _, rows, model = hidden_state.shape
    channels = down_weight.shape[1]
    head_cols = model // chips
    late = chips * (head_cols - width)
    hbm = pl.BlockSpec(memory_space=pltpu.HBM)
    shapes = [
        ((rows, late), jnp.bfloat16),
        ((3, late), jnp.float32),
        ((late, channels), jnp.bfloat16),
    ]
    return pl.pallas_call(
        functools.partial(prepare_kernel, chips, head_cols, width),
        out_shape=[jax.ShapeDtypeStruct(*shape) for shape in shapes]
        + [jax.ShapeDtypeStruct((2, 8, channels), jnp.float32)],
        in_specs=[hbm] * 3,
        out_specs=[hbm] * 3 + [pl.BlockSpec(memory_space=pltpu.VMEM)],
        scratch_shapes=[
            pltpu.VMEM((8, 128), jnp.float32),
            pltpu.VMEM((3, model), jnp.float32),
            pltpu.VMEM((model, channels), jnp.bfloat16),
        ]
        + [pltpu.VMEM(*shape) for shape in shapes]
        + [pltpu.SemaphoreType.DMA((4, max(chips, 2))), pltpu.SemaphoreType.DMA((3,))],
        cost_estimate=pl.CostEstimate(
            flops=64 * model * channels, bytes_accessed=4 * model * channels, transcendentals=0
        ),
        compiler_params=pltpu.CompilerParams(vmem_limit_bytes=VMEM_BYTES),
        name="prepare",
    )(hidden_state, mod_rows, down_weight)


def share(rows, channels, later):
    kept = sum(array.size * array.dtype.itemsize for array in later)
    return VMEM_BYTES - kept - 4 * rows * (channels + 256) - SPARE_BYTES


def early_kernel(chips, head_cols, h_ref, mod_ref, weight_ref, *rest):
    pieces, later, rest = rest[:chips], rest[chips : chips + 5], rest[chips + 5 :]
    acc_ref, centre_ref, square_ref = rest[:3]
    kept, (attended, hidden, weight, mod, sem, keep_sem) = rest[3:8], rest[8:]
    rows, width = pieces[0].shape
    block_rows = 16

    def pull(step, which):
        col = pl.multiple_of(my_chip(step, chips)[1] * head_cols, 128)
        here = pl.ds(step * width, width)
        source, target = (
            (pieces[step], attended.at[:, here]),
            (h_ref.at[0, :, pl.ds(col, width)], hidden.at[:, here]),
            (mod_ref.at[:, pl.ds(col, width)], mod.at[:, here]),
            (weight_ref.at[pl.ds(col, width), :], weight.at[here, :]),
        )[which]
        return pltpu.make_async_copy(source, target, sem.at[which, step])

    def keep(which):
        return pltpu.make_async_copy(later[which], kept[which], keep_sem.at[which])

    for which in range(4):
        for step in range(chips):
            pull(step, which).start()
    for which in range(5):
        keep(which).start()
    for which in range(3):
        for step in range(chips):
            pull(step, which).wait()

    def rows_of(index, carry):
        here = pl.ds(pl.multiple_of(index * block_rows, block_rows), block_rows)
        wide = (
            (
                hidden[here, :].astype(jnp.float32)
                + mod[2:3, :] * attended[here, :].astype(jnp.float32)
            )
            .astype(jnp.bfloat16)
            .astype(jnp.float32)
        )
        centre = jnp.mean(wide, axis=-1, keepdims=True)
        away = wide - centre
        square = jnp.sum(jnp.square(away), axis=-1, keepdims=True)
        attended[here, :] = (away * (1.0 + mod[1:2, :])).astype(jnp.bfloat16)
        centre_ref[here, :] = jnp.broadcast_to(centre, (block_rows, 128))
        square_ref[here, :] = jnp.broadcast_to(square, (block_rows, 128))
        return carry

    lax.fori_loop(0, rows // block_rows, rows_of, 0, unroll=4)
    for step in range(chips):
        pull(step, 3).wait()
    acc_ref[...] = jnp.dot(attended[...], weight[...], preferred_element_type=jnp.float32)
    for which in range(5):
        keep(which).wait()


def project_early(hidden_state, mod_rows, down_weight, pieces, later):
    chips = len(pieces)
    _, rows, model = hidden_state.shape
    channels = down_weight.shape[1]
    width = pieces[0].shape[1]
    return pl.pallas_call(
        functools.partial(early_kernel, chips, model // chips),
        out_shape=[
            pltpu.VMEM((rows, channels), jnp.float32),
            pltpu.VMEM((rows, 128), jnp.float32),
            pltpu.VMEM((rows, 128), jnp.float32),
        ]
        + [pltpu.VMEM(array.shape, array.dtype) for array in later],
        in_specs=[pl.BlockSpec(memory_space=pltpu.HBM)] * (chips + 8),
        out_specs=[pl.BlockSpec(memory_space=pltpu.VMEM)] * 8,
        scratch_shapes=[
            pltpu.VMEM((rows, chips * width), jnp.bfloat16),
            pltpu.VMEM((rows, chips * width), jnp.bfloat16),
            pltpu.VMEM((chips * width, channels), jnp.bfloat16),
            pltpu.VMEM((3, chips * width), jnp.float32),
            pltpu.SemaphoreType.DMA((4, chips)),
            pltpu.SemaphoreType.DMA((5,)),
        ],
        cost_estimate=pl.CostEstimate(
            flops=2 * rows * chips * width * channels,
            bytes_accessed=4 * rows * model + 2 * model * channels,
            transcendentals=0,
        ),
        compiler_params=pltpu.CompilerParams(vmem_limit_bytes=share(rows, channels, later)),
        name="project_early",
    )(hidden_state, mod_rows, down_weight, *pieces, *later)


def late_kernel(count, early, frames_ref, *rest):
    held, pieces, (out_ref, attended, in_sem) = rest[:7], rest[7 : 7 + count], rest[7 + count :]
    acc_ref, centre_ref, square_ref, h_ref, mod_ref, weight_ref, const_ref = held
    rows, width = pieces[0].shape
    late = count * width
    model = early + late

    def load(step):
        return pltpu.make_async_copy(
            pieces[step], attended.at[:, pl.ds(step * width, width)], in_sem.at[step]
        )

    for step in range(count):
        load(step).start()
    for step in range(count):
        load(step).wait()
    wide = (
        (h_ref[...].astype(jnp.float32) + mod_ref[2:3, :] * attended[...].astype(jnp.float32))
        .astype(jnp.bfloat16)
        .astype(jnp.float32)
    )
    first = centre_ref[:, :1]
    scaled = ((wide - first) * (1.0 + mod_ref[1:2, :])).astype(jnp.bfloat16)
    total = acc_ref[...] + jnp.dot(scaled, weight_ref[...], preferred_element_type=jnp.float32)
    own = jnp.mean(wide, axis=-1, keepdims=True)
    square = jnp.sum(jnp.square(wide - own), axis=-1, keepdims=True)
    gap = own - first
    centre = first + gap * (late / model)
    spread = (square_ref[:, :1] + square + gap * gap * (early * late / model)) / model
    total = total + (first - centre) * const_ref[0, :1, :]
    total = total * lax.rsqrt(spread + 1e-06) + const_ref[1, :1, :]
    token = lax.axis_index("ctx") * rows + lax.broadcasted_iota(jnp.int32, (rows, 1), 0)
    out_ref[...] = jnp.where(token < frames_ref[0] * (HH * WW), total, 0.0).astype(out_ref.dtype)


def project_late(frames, held, pieces, model, limit):
    count = len(pieces)
    rows, width = pieces[0].shape
    channels = held[0].shape[1]
    return pl.pallas_call(
        functools.partial(late_kernel, count, model - count * width),
        out_shape=jax.ShapeDtypeStruct((rows, channels), jnp.bfloat16),
        in_specs=[pl.BlockSpec(memory_space=pltpu.SMEM)]
        + [pl.BlockSpec(memory_space=pltpu.VMEM)] * 7
        + [pl.BlockSpec(memory_space=pltpu.HBM)] * count,
        out_specs=pl.BlockSpec(memory_space=pltpu.VMEM),
        scratch_shapes=[
            pltpu.VMEM((rows, count * width), jnp.bfloat16),
            pltpu.SemaphoreType.DMA((count,)),
        ],
        cost_estimate=pl.CostEstimate(
            flops=2 * rows * count * width * channels,
            bytes_accessed=4 * rows * count * width,
            transcendentals=0,
        ),
        compiler_params=pltpu.CompilerParams(vmem_limit_bytes=limit),
        name="project_late",
    )(frames, *[pltpu.with_memory_space_constraint(one, pltpu.VMEM) for one in held], *pieces)


def gather_taps(frames, taps):
    cells = HH * WW
    channels = frames[0].shape[1]
    column = lax.broadcasted_iota(jnp.int32, (cells, 1), 0) % WW
    blank = jnp.zeros((WW, channels), jnp.float32)
    for number, frame in enumerate(frames):
        wide = frame.astype(jnp.float32)
        for across, offset in enumerate((-1, 0, 1)):
            cell = wide
            if offset:
                inside = (column + offset >= 0) & (column + offset < WW)
                cell = jnp.where(inside, pltpu.roll(wide, (-offset) % cells, 0), 0.0)
            cell = jnp.concatenate([blank, cell, blank], axis=0)
            for down in range(3):
                taps[
                    pl.ds(number * cells, cells), pl.ds((down * 3 + across) * channels, channels)
                ] = cell[down * WW : down * WW + cells].astype(jnp.bfloat16)


def refine_kernel(frames_ref, mid_ref, even_ref, odd_ref, weight, out_ref, held, taps, sem):
    cells = HH * WW
    rows, _ = mid_ref.shape
    me = lax.axis_index("ctx")
    odd = lax.rem(me, 2) == 1
    copy = pltpu.make_async_copy(mid_ref, held, sem)
    copy.start()
    last, first = pl.ds(rows - cells, cells), pl.ds(0, cells)
    low = jnp.where(odd, even_ref[last, :], odd_ref[last, :])
    high = jnp.where(odd, odd_ref[first, :], even_ref[first, :])
    copy.wait()
    frames = [held[pl.ds(start, cells), :] for start in range(0, rows, cells)]
    gather_taps([low, *frames, high], taps)
    total = held[...].astype(jnp.float32)
    for ahead in range(3):
        total = total + jnp.dot(
            taps[pl.ds(ahead * cells, rows), :], weight[ahead], preferred_element_type=jnp.float32
        )
    token = me * rows + lax.broadcasted_iota(jnp.int32, (rows, 1), 0)
    out_ref[0] = jnp.where(token < frames_ref[0] * cells, total, 0.0).astype(out_ref.dtype)


def refine(frames, mid, even, odd, taps, limit):
    rows, channels = mid.shape
    on_chip = [pltpu.with_memory_space_constraint(one, pltpu.VMEM) for one in (even, odd, taps)]
    return pl.pallas_call(
        refine_kernel,
        out_shape=jax.ShapeDtypeStruct((1, rows, channels), jnp.bfloat16),
        in_specs=[pl.BlockSpec(memory_space=pltpu.SMEM), pl.BlockSpec(memory_space=pl.ANY)]
        + [pl.BlockSpec(memory_space=pltpu.VMEM)] * 3,
        out_specs=pl.BlockSpec(memory_space=pltpu.VMEM),
        scratch_shapes=[
            pltpu.VMEM((rows, channels), jnp.bfloat16),
            pltpu.VMEM((rows + 2 * HH * WW, 9 * channels), jnp.bfloat16),
            pltpu.SemaphoreType.DMA,
        ],
        cost_estimate=pl.CostEstimate(
            flops=54 * rows * channels * channels,
            bytes_accessed=2 * taps.size + 6 * rows * channels,
            transcendentals=0,
        ),
        compiler_params=pltpu.CompilerParams(vmem_limit_bytes=limit),
        name="refine",
    )(frames, mid, *on_chip)


def clip_orders(sec_count):
    return [
        order
        for order in itertools.permutations(range(sec_count))
        if any(order[(d + sec_count // 2) % sec_count] == d for d in range(sec_count))
    ]


def order_index(destination, sec_count):
    if sec_count > 4:
        return jnp.int32(0)
    orders = clip_orders(sec_count)
    codes = jnp.asarray(
        [sum(d * sec_count**i for i, d in enumerate(order)) for order in orders], jnp.int32
    )
    powers = jnp.asarray([sec_count**i for i in range(sec_count)], jnp.int32)
    code = jnp.sum(destination * powers)
    return jnp.sum(jnp.where(codes == code, jnp.arange(len(orders), dtype=jnp.int32), 0))


def handoff(projected, which, source, sec_count):
    if sec_count <= 4:
        def take(order):
            return lambda value: lax.ppermute(value, "sec", list(enumerate(order)))

        return lax.switch(which, [take(order) for order in clip_orders(sec_count)], projected)
    my_section = lax.axis_index("sec")
    chosen = projected
    for step in range(1, sec_count):
        arrived = lax.ppermute(projected, "sec", ring(step, sec_count))
        chosen = jnp.where(source == partner(my_section, step, sec_count)[1], arrived, chosen)
    return chosen


def body(
    hidden_state,
    queries,
    key_vectors,
    value_vectors,
    modulation,
    down_weight,
    conv_weight,
    clip_frames,
    destination,
    timestep,
):
    my_section = lax.axis_index("sec")
    sec_count = lax.axis_size("sec")
    count = lax.axis_size("ctx")
    chips = count // 2
    model_width = hidden_state.shape[2]
    group = HEADS // chips
    head_size = model_width // HEADS
    head_cols = group * head_size
    chunks = head_chunks(group)
    widths = [heads * head_size for heads in chunks]
    tensors = (queries, key_vectors, value_vectors)
    steps = range(1, chips)

    own, beside = [], []
    for chunk, width in enumerate(widths):
        packed = [None] * chips
        order = far_first(chips)
        for batch in (order[:1], order[1:] + [0]) if chunk == 0 else (order + [0],):
            pieces = pack(tensors, batch, chips, head_cols, sum(widths[:chunk]), width)
            for step, piece in zip(batch, pieces):
                packed[step] = piece
        beside.append([across(packed[0], chips)])
        own.append([packed[0]] + [send(packed[step], step, chips) for step in steps])
        beside[chunk] += [across(own[chunk][step], chips) for step in steps]

    section_ids = jnp.arange(destination.shape[0], dtype=jnp.int32)
    source = jnp.sum(jnp.where(destination == my_section, section_ids, 0))
    own_frames = lax.dynamic_slice(clip_frames, (my_section,), (1,))
    clip_length = lax.dynamic_slice(clip_frames, (source,), (1,))
    which = order_index(destination, sec_count)
    mod_rows = lax.dynamic_index_in_dim(modulation, timestep[my_section], 0, keepdims=False)
    ready = prepare(hidden_state, mod_rows, down_weight, chips, widths[0])
    own_frames, clip_length, which, mod_rows, ready = lax.optimization_barrier(
        (own_frames, clip_length, which, mod_rows, ready)
    )

    returned = []
    for chunk, heads in enumerate(chunks):
        outs = attend(own_frames, own[chunk], beside[chunk], heads)
        returned.append([outs[0]] + [send(outs[step], step, chips) for step in steps])
    channels = down_weight.shape[1]
    later = (*ready, conv_weight.reshape(3, 9 * channels, channels))
    kept = project_early(hidden_state, mod_rows, down_weight, returned[0], later)
    limit = share(hidden_state.shape[1], channels, later)
    projected = project_late(own_frames, kept[:7], returned[1], model_width, limit)
    mid = handoff(projected, which, source, sec_count)
    joints = [(i, i + 1) for i in range(1, count - 1, 2)]
    odd = lax.ppermute(mid, "ctx", joints + [(two, one) for one, two in joints])
    even = across(mid, chips)
    return refine(clip_length, mid, even, odd, kept[7], limit // 2)


def solution(mesh):
    split = P("sec", "ctx", None)
    return jax.shard_map(
        body,
        mesh=mesh,
        in_specs=(split,) * 4 + (P(),) * 6,
        out_specs=split,
        check_vma=False,
    )
```
